32 devices in a mesh: section: 8 (over z, core), tensor: 2 (over x), replica: 2 (over y).
Axes of the slice: x: 2, y: 2, z: 4, core: 2. Of those that a mesh axis runs over, the one named last changes fastest.
Arguments:
- pool_inputs: bfloat16 [8, 256, 2, 1408], P('section', 'replica', None, 'tensor'), may hold values from -6 to 6
- pool_mixed: bfloat16 [8, 256, 1408], P('section', 'replica'), may hold values from -6 to 6
- crop_ids: int32 [8, 8, 128], P('section', 'replica'), may hold values from 0 to 127
- incoming: bfloat16 [8, 256, 1408], P('section', 'replica', 'tensor'), may hold values from -6 to 6
- loss_grads: bfloat16 [3, 256, 1408], P(None, 'replica', 'tensor'), may hold values from -6 to 6
- w_proj: bfloat16 [8, 2, 1408, 1408], P('section', None, ('tensor', 'replica')), may hold values from -0.109375 to 0.109375
- w_up: bfloat16 [8, 1408, 3072], P('section', None, ('tensor', 'replica')), may hold values from -0.15625 to 0.15625
- w_down: bfloat16 [8, 3072, 1408], P('section', ('tensor', 'replica')), may hold values from -0.109375 to 0.109375
Outputs:
- grad_proj: bfloat16 [8, 2, 1408, 1408], P('section', None, ('tensor', 'replica'))
- grad_up: bfloat16 [8, 1408, 3072], P('section', None, ('tensor', 'replica'))
- grad_down: bfloat16 [8, 3072, 1408], P('section', ('tensor', 'replica'))
- outgoing: bfloat16 [8, 256, 2, 1408], P('section', 'replica', None, 'tensor')
The draws below stay inside these ranges and needn't reach their ends.
All inputs are finite; a program needn't handle non-finite values.
Results may differ from the reference program's by a relative error of at most 0.02.
Values may be sent and summed in bfloat16 or wider, within the bound.
A program may use at most 128 MiB of HBM per device.

```python
import math
import jax
import jax.numpy as jnp
import numpy as np
from jax import lax

D = 1408
FF = 3072
M = 128
TICKS = 4
POOL = 128
SECTIONS = 8
REPLICAS = 2


def set_ends(drawn, stream_key, low, high):
    longest = drawn.shape.index(max(drawn.shape))
    spots = []
    for shift in (0, 1):
        where = [jax.random.randint(jax.random.fold_in(stream_key, axis), (), 0, length) for axis, length in enumerate(drawn.shape)]
        where[longest] = (where[longest] + shift) % drawn.shape[longest]
        spots.append(tuple(where))
    return drawn.at[spots[0]].set(low).at[spots[1]].set(high)


def shard_levels(stream_key, dims, cuts, smallest, top_value):
    factor_of, own = 1.0, jax.random.fold_in(stream_key, 6)
    for position, shards_of in cuts:
        draws = jnp.exp(jax.random.uniform(jax.random.fold_in(own, position), (shards_of,), jnp.float32, smallest / len(cuts), top_value / len(cuts)))
        factor_of = factor_of * jnp.repeat(draws, dims[position] // shards_of).reshape([-1 if axis == position else 1 for axis in range(len(dims))])
    return factor_of


def rank_bounds(count, lean):
    loads = [(1 << 20) // math.isqrt(rank ** lean) + 1 for rank in range(1, count + 1)]
    width = 1 + sum(loads) // (1 << 30)
    return np.cumsum(np.array([max(1, weight // width) for weight in loads]))


def ranked(key, shape, number_of, slope):
    listing = rank_bounds(number_of, slope)
    lot = jax.random.randint(jax.random.fold_in(key, 1), shape, 0, int(listing[number_of - 1]))
    rank = jnp.searchsorted(jnp.asarray(listing, jnp.int32), lot, side="right")
    return jax.random.permutation(jax.random.fold_in(key, 2), number_of)[rank].astype(jnp.int32)


def noise(rng, extent, width, limit, split=(), kind=jnp.bfloat16):
    factor_of = shard_levels(rng, extent, split, -0.22, 0.18) if split else 1.0
    array = jax.random.normal(rng, extent, jnp.float32) * width * factor_of
    return jnp.minimum(jnp.maximum(array, -limit), limit).astype(kind)


def setup_inputs(seed: int = 0) -> dict:
    key_of = jax.random.split(jax.random.key(seed), 9)
    return {
        "pool_inputs": noise(key_of[0], (SECTIONS, REPLICAS * POOL, 2, D), 1.0, 6.0, ((0, 8), (1, 2), (3, 2))),
        "pool_mixed": noise(key_of[1], (SECTIONS, REPLICAS * POOL, D), 1.0, 6.0, ((0, 8), (1, 2))),
        "crop_ids": set_ends(ranked(key_of[2], (SECTIONS, REPLICAS * TICKS, M), POOL, 2), jax.random.fold_in(key_of[2], 3), 0, POOL - 1).astype(jnp.int32),
        "incoming": noise(key_of[3], (SECTIONS, REPLICAS * M, D), 1.0, 6.0, ((0, 8), (1, 2), (2, 2))),
        "loss_grads": noise(key_of[4], (TICKS - 1, REPLICAS * M, D), 1.0, 6.0, ((1, 2), (2, 2))),
        "w_proj": noise(key_of[5], (SECTIONS, 2, D, D), (2 * D) ** -0.5, 0.109375, ((0, 8), (2, 4))),
        "w_up": noise(key_of[6], (SECTIONS, D, FF), D ** -0.5, 0.15625, ((0, 8), (2, 4))),
        "w_down": noise(key_of[7], (SECTIONS, FF, D), FF ** -0.5, 0.109375, ((0, 8), (1, 4))),
    }


gelu_scale = 0.7978845608
gelu_cubic = 0.044715


def gelu_pair(pre_gelu):
    inner = gelu_scale * (pre_gelu + gelu_cubic * pre_gelu * pre_gelu * pre_gelu)
    tanh_part = jnp.tanh(inner)
    gelu_value = 0.5 * pre_gelu * (1.0 + tanh_part)
    gelu_slope = 0.5 * (1.0 + tanh_part) + 0.5 * pre_gelu * (1.0 - tanh_part * tanh_part) * gelu_scale * (1.0 + 3.0 * gelu_cubic * pre_gelu * pre_gelu)
    return gelu_value, gelu_slope


def section_back(proj_weight, up_weight, down_weight, inputs, mixed_rows, upstream):
    pre_gelu = jnp.dot(mixed_rows, up_weight, preferred_element_type=jnp.float32)
    gelu_value, gelu_slope = gelu_pair(pre_gelu)
    activated = gelu_value.astype(jnp.bfloat16)
    back_act = jnp.dot(upstream, down_weight.T, preferred_element_type=jnp.float32)
    back_hidden = (back_act * gelu_slope).astype(jnp.bfloat16)
    back_mixed = upstream.astype(jnp.float32) + jnp.dot(back_hidden, up_weight.T, preferred_element_type=jnp.float32)
    mixed_grad = back_mixed.astype(jnp.bfloat16)
    input_grad = jnp.einsum('mj,kij->mki', mixed_grad.astype(jnp.float32), proj_weight.astype(jnp.float32)).astype(jnp.bfloat16)
    return activated, back_hidden, mixed_grad, input_grad


def finish(total):
    rounded = lax.optimization_barrier(total.astype(jnp.bfloat16))
    return jnp.sum(rounded.astype(jnp.float32), axis=0).astype(jnp.bfloat16)


def reference(pool_inputs, pool_mixed, crop_ids, incoming, loss_grads, w_proj, w_up, w_down):
    section_ids = jnp.arange(SECTIONS, dtype=jnp.int32)
    decoder_flag = (section_ids >= SECTIONS // 2).astype(jnp.float32)
    skip_mask = jnp.stack([jnp.ones((SECTIONS,), jnp.float32), decoder_flag], axis=1).astype(jnp.bfloat16)[:, None, :, None]
    encoder_weight = (section_ids < SECTIONS // 2).astype(jnp.float32)[:, None, None]
    offsets = (jnp.arange(REPLICAS, dtype=jnp.int32) * POOL)[None, :, None, None]
    row_ids = crop_ids.reshape(SECTIONS, REPLICAS, TICKS, M).astype(jnp.int32) + offsets
    upstream = incoming
    seen_inputs, seen_mixed, seen_upstream = [], [], []
    input_grad = None
    for tick_index in range(TICKS):
        picked_rows = row_ids[:, :, tick_index, :].reshape(SECTIONS, REPLICAS * M)
        inputs = jax.vmap(lambda source_rows, chosen: source_rows[chosen])(pool_inputs, picked_rows) * skip_mask
        mixed_rows = jax.vmap(lambda source_rows, chosen: source_rows[chosen])(pool_mixed, picked_rows)
        seen_inputs.append(inputs)
        seen_mixed.append(mixed_rows)
        seen_upstream.append(upstream)
        input_grad = lax.map(lambda packed: section_back(*packed)[3], (w_proj, w_up, w_down, inputs, mixed_rows, upstream))
        if tick_index + 1 < TICKS:
            below_grad = input_grad[:, :, 0]
            skip_grad = input_grad[:, :, 1]
            from_above = jnp.concatenate([below_grad[1:], jnp.zeros_like(below_grad[:1])], axis=0)
            mirrored = skip_grad[::-1]
            upstream = (from_above.astype(jnp.float32) + encoder_weight * mirrored.astype(jnp.float32)).astype(jnp.bfloat16)
            upstream = upstream.at[SECTIONS - 1].set(loss_grads[tick_index])
    all_inputs = jnp.stack(seen_inputs, axis=1)
    all_mixed = jnp.stack(seen_mixed, axis=1)
    all_upstream = jnp.stack(seen_upstream, axis=1)

    def section_grads(packed):
        proj_weight, up_weight, down_weight, inputs_ticks, mixed_ticks, upstream_ticks = packed
        proj_total = jnp.zeros((REPLICAS, 2, D, D), jnp.float32)
        up_total = jnp.zeros((REPLICAS, D, FF), jnp.float32)
        down_total = jnp.zeros((REPLICAS, FF, D), jnp.float32)
        for tick_index in range(TICKS):
            inputs = inputs_ticks[tick_index]
            mixed_rows = mixed_ticks[tick_index]
            upstream_now = upstream_ticks[tick_index]
            activated, back_hidden, mixed_grad, unused_grad = section_back(proj_weight, up_weight, down_weight, inputs, mixed_rows, upstream_now)
            down_total = down_total + jnp.einsum('rmf,rmd->rfd', activated.reshape(REPLICAS, M, FF).astype(jnp.float32), upstream_now.reshape(REPLICAS, M, D).astype(jnp.float32))
            up_total = up_total + jnp.einsum('rmd,rmf->rdf', mixed_rows.reshape(REPLICAS, M, D).astype(jnp.float32), back_hidden.reshape(REPLICAS, M, FF).astype(jnp.float32))
            proj_total = proj_total + jnp.einsum('rmki,rmj->rkij', inputs.reshape(REPLICAS, M, 2, D).astype(jnp.float32), mixed_grad.reshape(REPLICAS, M, D).astype(jnp.float32))
        return finish(proj_total), finish(up_total), finish(down_total)

    grad_proj, grad_up, grad_down = lax.map(section_grads, (w_proj, w_up, w_down, all_inputs, all_mixed, all_upstream))
    return grad_proj, grad_up, grad_down, input_grad
```

```python
import functools

import jax
import jax.numpy as jnp
from jax import lax
from jax.experimental import pallas as pl
from jax.experimental.pallas import tpu as pltpu
from jax.sharding import PartitionSpec as P

gelu_scale = 0.7978845608
gelu_cubic = 0.044715
bf16, f32 = jnp.bfloat16, jnp.float32
MESH = pl.DeviceIdType.MESH


def gelu_pair(pre_gelu):
    inner = gelu_scale * (pre_gelu + gelu_cubic * pre_gelu * pre_gelu * pre_gelu)
    tanh_part = jnp.tanh(inner)
    gelu_value = 0.5 * pre_gelu * (1.0 + tanh_part)
    gelu_slope = 0.5 * (1.0 + tanh_part) + 0.5 * pre_gelu * (
        1.0 - tanh_part * tanh_part
    ) * gelu_scale * (1.0 + 3.0 * gelu_cubic * pre_gelu * pre_gelu)
    return (gelu_value, gelu_slope)


def dot(a, b):
    return jnp.dot(a, b, preferred_element_type=f32)


def dot_nt(a, b):
    return lax.dot_general(a, b, (((1,), (1,)), ((), ())), preferred_element_type=f32)


def ticks_kernel(
    sections, tensors, replicas, own, ticks,
    inputs_hbm, pool_hbm, ids_hbm, seed_hbm, loss_hbm, proj_hbm, up_hbm, down_hbm,
    in_got, pool_out, act_out, hidden_out, grad_out, up_out, out,
    proj, up, down, loss_src, ids, loss_t, pool, pool_t, act_t,
    upstream, grads, hidden, part, relay, got, keep_part, own_part, slope_hi, slope_lo, slope,
    edge, edge_got, acc_hidden, acc_grad, acc_up, sum_hidden, sum_grad, sum_up,
    load_sem, out_sem, pool_sems, inputs_sems, ids_sems, loss_sems, seed_sems,
    part_sems, grad_sems, up_sems, edge_sems, outgoing_sems,
):
    members = tensors * replicas
    square = tensors == 2 and replicas == 2 and own % 32 == 0
    half = own // 2
    section = lax.axis_index("section")
    tensor = lax.axis_index("tensor")
    replica = lax.axis_index("replica")
    me = tensor * replicas + replica
    hidden_rows = down.shape[0]
    saved = pool.shape[1]
    last = ticks - 1
    along = (1 - tensor) * replicas + replica
    across = tensor * replicas + (1 - replica)
    far = (1 - tensor) * replicas + (1 - replica)

    def device(s, member):
        return {
            "section": s,
            "tensor": lax.div(member, replicas),
            "replica": lax.rem(member, replicas),
        }

    def member_at(by):
        return lax.rem(me + by, members)

    def replica_at(by):
        return lax.rem(replica + by, replicas)

    def slab_of(member):
        return pl.ds(pl.multiple_of(member * own, 16), own)

    def load(i, src, dst):
        copy = pltpu.make_async_copy(src, dst, load_sem.at[i])
        copy.start()
        return copy

    wide = pl.ds(pl.multiple_of(tensor * (replicas * own), 16), replicas * own)
    pairs = [
        (pool_hbm, pool.at[replica]), (seed_hbm, upstream.at[0, replica, wide]),
        (ids_hbm, ids.at[replica]), (up_hbm, up), (loss_hbm, loss_src),
        (loss_hbm.at[:, replica], loss_t.at[replica]), (down_hbm, down), (proj_hbm, proj),
    ]
    loads = [load(i, src, dst) for i, (src, dst) in enumerate(pairs)]
    ld_pool, ld_seed, ld_ids, ld_up, ld_loss, ld_loss_own, ld_down, ld_proj = loads

    barrier = pltpu.get_barrier_semaphore()
    above = lax.rem(section + 1, sections)
    below = lax.rem(section + sections - 1, sections)
    mirror = sections - 1 - section
    for by in range(1, members):
        pl.semaphore_signal(barrier, 1, device_id=device(section, member_at(by)), device_id_type=MESH)
    for other in (above, below, mirror):
        pl.semaphore_signal(barrier, 1, device_id=device(other, me), device_id_type=MESH)
    pl.semaphore_wait(barrier, members - 1 + 3)

    sent = []
    written = []

    def send(src, dst, sems, index, member):
        copy = pltpu.make_async_remote_copy(
            src_ref=src, dst_ref=dst, send_sem=sems.at[(0,) + index], recv_sem=sems.at[(1,) + index],
            device_id=device(section, member), device_id_type=MESH,
        )
        copy.start()
        sent.append(copy)
        return copy

    def over_replicas(src_of, dst, sems):
        return [
            send(src_of(replica_at(by)), dst, sems, (by - 1,), tensor * replicas + replica_at(by))
            for by in range(1, replicas)
        ]

    def write(src, dst):
        copy = pltpu.make_async_copy(src, dst, out_sem.at[len(written)])
        copy.start()
        written.append(copy)

    class Gather:
        def __init__(self, at, whole, sems, index):
            self.at, self.sems, self.index = at, sems, index
            if square:
                self.copies = [
                    self.put(me, h, i, to)
                    for i, (h, to) in enumerate(((0, along), (1, across), (1, along), (0, across)))
                ]
            else:
                self.copies = [
                    send(whole, whole, sems, index + (by - 1,), member_at(by))
                    for by in range(1, members)
                ]

        def put(self, member, h, i, to):
            ref = self.at(member, h)
            return send(ref, ref, self.sems, self.index + (i,), to)

        def forward(self):
            if square:
                self.copies[0].wait_recv()
                self.copies.append(self.put(along, 0, 4, across))
                self.copies[1].wait_recv()
                self.copies.append(self.put(across, 1, 5, along))

        def finish(self):
            for copy in self.copies[2 if square else 0:]:
                copy.wait_recv()

    def halves_of(ref):
        return lambda member, h: ref.at[pl.ds(pl.multiple_of(member * own + h * half, 16), half)]

    def seed_at(member, h):
        return upstream.at[0, lax.rem(member, replicas),
                           pl.ds(pl.multiple_of(lax.div(member, replicas) * (replicas * own) + h * own, 16), own)]

    slab = slab_of(me)
    ld_pool.wait()
    if square:
        mine = pl.ds(pl.multiple_of(tensor * (saved // 2), 16), saved // 2)
        own_pool = pool.at[replica, mine]
        pool_in = send(own_pool, own_pool, pool_sems, (0,), across)
    else:
        pool_in = over_replicas(lambda r: pool.at[replica], pool.at[replica], pool_sems)
    ld_ids.wait()
    ids_in = over_replicas(lambda r: ids.at[replica], ids.at[replica], ids_sems)
    ld_seed.wait()
    seed_in = Gather(seed_at, upstream.at[0, replica, wide], seed_sems, ())
    is_top = section == sections - 1

    step = 128

    def pre_slopes(r):
        def pre_at(start, size):
            cols = pl.ds(start, size)
            value, gelu_slope = gelu_pair(dot(pool[r], up[:, cols]).T)
            act_t[cols, pl.ds(pl.multiple_of(r * saved, 128), saved)] = value.astype(bf16)
            high = gelu_slope.astype(bf16)
            slope_hi[r, cols, :] = high
            slope_lo[r, cols, :] = (gelu_slope - high.astype(f32)).astype(bf16)

        @pl.loop(0, hidden_rows // step)
        def _(c):
            pre_at(pl.multiple_of(c * step, step), step)

        if hidden_rows % step:
            pre_at(hidden_rows - hidden_rows % step, hidden_rows % step)

    ld_up.wait()
    pre_slopes(replica)
    if square:
        pool_in.wait_recv()
        come = pool.at[1 - replica, mine]
        pool_over = send(come, come, pool_sems, (1,), along)
        seed_in.forward()
        pool_over.wait_recv()
        pre_slopes(1 - replica)
    else:
        for by in range(1, replicas):
            pool_in[by - 1].wait_recv()
            pre_slopes(lax.rem(replica + replicas - by, replicas))
    write(act_t, act_out)
    for copy in ids_in:
        copy.wait_recv()

    def picks(t, r):
        row = ids[r, pl.ds(t, 1), :]
        place_of = lax.broadcasted_iota(jnp.int32, (saved, row.shape[1]), 0)
        return jnp.where(place_of == row, 1.0, 0.0).astype(bf16)

    def pick_slope(t, r):
        chosen = picks(t, r)
        slope[r] = dot(slope_hi[r], chosen) + dot(slope_lo[r], chosen)

    for r in range(replicas):
        pick_slope(0, r)

    ld_down.wait()
    seed_in.finish()

    up_in, part_in, grad_in, edge_in = {}, {}, {}, {}

    def stage_hidden(t, r):
        if t > 0:
            up_in[t, r].finish()
        hidden[t, r] = (dot(down[...], upstream[t, r]) * slope[r]).astype(bf16)

        def partial(member):
            return dot(up[slab_of(member), :], hidden[t, r])

        if square:
            part[t, r, 0] = partial(far).astype(bf16)
            low, high = pl.ds(0, half), pl.ds(half, half)
            copies = [
                send(part.at[t, r, 0, low], relay.at[t, r, 0], part_sems, (t, r, 0), across),
                send(part.at[t, r, 0, high], relay.at[t, r, 1], part_sems, (t, r, 1), along),
            ]
            term = partial(along)
            part[t, r, 1, high] = term[half:].astype(bf16)
            copies.append(send(part.at[t, r, 1, high], got.at[t, r, 0, high], part_sems, (t, r, 2), along))
            keep_part[r, 0] = term[:half]
            term = partial(across)
            part[t, r, 2, low] = term[:half].astype(bf16)
            copies.append(send(part.at[t, r, 2, low], got.at[t, r, 1, low], part_sems, (t, r, 3), across))
            keep_part[r, 1] = term[half:]
        else:
            copies = []
            for by in range(1, members):
                to = member_at(by)
                part[t, r, by - 1] = partial(to).astype(bf16)
                copies.append(send(part.at[t, r, by - 1], got.at[t, r, by - 1], part_sems,
                                   (t, r, by - 1), to))
        own_part[r] = partial(me) + upstream[t, r, slab, :].astype(f32)
        part_in[t, r] = copies

    def stage_relay(t, r):
        if square:
            copies = part_in[t, r]
            for k, (to, start) in enumerate(((along, 0), (across, half))):
                rows = pl.ds(start, half)
                copies[k].wait_recv()
                part[t, r, k + 1, rows] = (keep_part[r, k] + relay[t, r, k].astype(f32)).astype(bf16)
                copies.append(send(part.at[t, r, k + 1, rows], got.at[t, r, k, rows], part_sems,
                                   (t, r, 4 + k), to))

    def stage_sum(t, r):
        for copy in part_in[t, r][2 if square else 0:]:
            copy.wait_recv()
        total = own_part[r]
        for k in range(got.shape[2]):
            total = total + got[t, r, k].astype(f32)
        grads[t, r, slab, :] = total.astype(bf16)
        grad_in[t, r] = Gather(halves_of(grads.at[t, r]), grads.at[t, r, slab], grad_sems, (t, r))

    def stage_project(t, r):
        grad_in[t, r].finish()
        edge[t, r, 0] = dot(proj[0], grads[t, r]).astype(bf16)
        if t == last:
            return
        down_copy = pltpu.make_async_remote_copy(
            src_ref=edge.at[t, r, 0], dst_ref=edge_got.at[t, r, 0],
            send_sem=edge_sems.at[0, t, r, 0], recv_sem=edge_sems.at[1, t, r, 0],
            device_id=device(below, me), device_id_type=MESH,
        )
        pl.when(section > 0)(down_copy.start)
        skip = pltpu.make_async_remote_copy(
            src_ref=edge.at[t, r, 1], dst_ref=edge_got.at[t, r, 1],
            send_sem=edge_sems.at[0, t, r, 1], recv_sem=edge_sems.at[1, t, r, 1],
            device_id=device(mirror, me), device_id_type=MESH,
        )

        @pl.when(section >= sections // 2)
        def _():
            edge[t, r, 1] = dot(proj[1], grads[t, r]).astype(bf16)
            skip.start()

        edge_in[t, r] = (down_copy, skip)

    def stage_next(t, r):
        down_copy, skip = edge_in[t, r]

        @pl.when(section < sections // 2)
        def _():
            down_copy.wait_recv()
            skip.wait_recv()
            summed = edge_got[t, r, 0].astype(f32) + edge_got[t, r, 1].astype(f32)
            upstream[t + 1, r, slab, :] = summed.astype(bf16)

        @pl.when((section >= sections // 2) & (section < sections - 1))
        def _():
            down_copy.wait_recv()
            upstream[t + 1, r, slab, :] = edge_got[t, r, 0]

        @pl.when(section == sections - 1)
        def _():
            upstream[t + 1, r, slab, :] = loss_t[r, t]

        up_in[t + 1, r] = Gather(halves_of(upstream.at[t + 1, r]), upstream.at[t + 1, r, slab], up_sems, (t, r))

    def add(t, r, acc, total, term):
        rows = pl.ds(r * saved, saved)
        value = term if t == 0 else acc[r] + term
        if t == last:
            total[rows, :] = value.astype(bf16)
        else:
            acc[r] = value

    every = range(replicas)
    to_last = []
    for t in range(ticks):
        for r in every:
            stage_hidden(t, r)
        if t == 0:
            ld_loss.wait()
            ld_loss_own.wait()
            loss_in = []
            for by in range(1, replicas):
                to = replica_at(by)
                loss_in.append(pltpu.make_async_remote_copy(
                    src_ref=loss_src.at[:, to], dst_ref=loss_t.at[replica],
                    send_sem=loss_sems.at[0, by - 1], recv_sem=loss_sems.at[1, by - 1],
                    device_id=device(section, tensor * replicas + to), device_id_type=MESH,
                ))
            for copy in loss_in:
                pl.when(is_top)(copy.start)
        for r in every:
            stage_relay(t, r)
            chosen = picks(t, r)
            add(t, r, acc_hidden, sum_hidden, dot_nt(chosen, hidden[t, r]))
            add(t, r, acc_up, sum_up, dot_nt(chosen, upstream[t, r]))
        if t == last:
            write(sum_hidden, hidden_out)
            write(sum_up, up_out)
        for r in every:
            stage_sum(t, r)
        if t < last:
            for r in every:
                pick_slope(t + 1, r)
        if t == 0:
            ld_proj.wait()
            for r in every:
                pool_t[:, pl.ds(r * saved, saved)] = pool[r].T
            write(pool_t, pool_out)
            for copy in loss_in:
                pl.when(is_top)(copy.wait_recv)
        for r in every:
            grad_in[t, r].forward()
        if t < last:
            for r in every:
                stage_project(t, r)
            if t == min(1, ticks - 1):
                inputs_in = over_replicas(lambda r: inputs_hbm.at[:, r], in_got.at[replica], inputs_sems)
            for r in every:
                stage_next(t, r)
            for r in every:
                add(t, r, acc_grad, sum_grad, dot_nt(picks(t, r), grads[t, r]))
            for r in every:
                up_in[t + 1, r].forward()

    outs = []
    for by in range(1, replicas):
        to = replica_at(by)
        for k in range(2):
            outs.append(pltpu.make_async_remote_copy(
                src_ref=edge.at[last, to, k], dst_ref=out.at[k, replica],
                send_sem=outgoing_sems.at[0, by - 1, k], recv_sem=outgoing_sems.at[1, by - 1, k],
                device_id=device(section, tensor * replicas + to), device_id_type=MESH,
            ))
    for r in every:
        grad_in[last, r].finish()
        for k in range(2):
            edge[last, r, k] = dot(proj[k], grads[last, r]).astype(bf16)
            for by in range(1, replicas):
                pl.when(replica_at(by) == r)(outs[2 * (by - 1) + k].start)
        add(last, r, acc_grad, sum_grad, dot_nt(picks(last, r), grads[last, r]))
    write(sum_grad, grad_out)
    write(edge.at[last, replica], out.at[:, replica])
    for copy in outs:
        copy.wait()
    for copy in inputs_in:
        copy.wait_recv()
    for copy in written:
        copy.wait()
    for copy in loss_in:
        pl.when(is_top)(copy.wait_send)
    for copy in sent:
        copy.wait_send()
    for key in edge_in:
        down_copy, skip = edge_in[key]
        pl.when(section > 0)(down_copy.wait_send)
        pl.when(section >= sections // 2)(skip.wait_send)


def tail_kernel(
    replicas, keep_ref, act_hbm, sum_up_hbm, pool_hbm, sum_hidden_hbm, inputs_hbm, in_got_hbm,
    sum_grad_hbm, outgoing_hbm,
    down_out, up_out, proj_out, outgoing_out,
    act, sum_up, pool, sum_hidden, inputs, sum_grad, outgoing, down_v, up_v, proj_v, load_sems, sems,
):
    replica = lax.axis_index("replica")
    saved = sum_up.shape[0] // replicas
    copies = []

    def lanes(r):
        return inputs.at[:, :, pl.ds(pl.multiple_of(r * saved, 128), saved)]

    pairs = [
        (act_hbm, act), (sum_up_hbm, sum_up), (pool_hbm, pool), (sum_hidden_hbm, sum_hidden),
        (sum_grad_hbm, sum_grad), (outgoing_hbm, outgoing),
        (inputs_hbm.at[:, replica], lanes(replica)),
    ]
    for by in range(1, replicas):
        r = lax.rem(replica + by, replicas)
        pairs.append((in_got_hbm.at[r], lanes(r)))
    loads = [
        pltpu.make_async_copy(src, dst, load_sems.at[i]) for i, (src, dst) in enumerate(pairs)
    ]
    for copy in loads:
        copy.start()

    def put(src, dst):
        copy = pltpu.make_async_copy(src, dst, sems.at[len(copies)])
        copy.start()
        copies.append(copy)

    def finish(a, b, rows, kept, out, scale=None):
        total = dot(a[rows], b[...])
        if scale is not None:
            total = total * scale
        kept.at[rows][...] = total.astype(bf16)
        put(kept.at[rows], out.at[rows])

    loads[0].wait()
    loads[1].wait()
    for start in range(0, down_v.shape[0], 128):
        finish(act, sum_up, pl.ds(start, min(128, down_v.shape[0] - start)), down_v, down_out)
    loads[2].wait()
    loads[3].wait()
    for start in range(0, up_v.shape[0], 128):
        finish(pool, sum_hidden, pl.ds(start, min(128, up_v.shape[0] - start)), up_v, up_out)
    loads[5].wait()
    put(outgoing, outgoing_out)
    loads[4].wait()
    for copy in loads[6:]:
        copy.wait()
    half = proj_v.shape[1] // 2
    for k in range(2):
        for start in (0, half):
            finish(inputs, sum_grad, (k, pl.ds(start, half)), proj_v, proj_out, keep_ref[0] if k else None)
    for copy in copies:
        copy.wait()


def body(pool_inputs, pool_mixed, crop_ids, incoming, loss_grads, w_proj, w_up, w_down):
    sections = lax.axis_size("section")
    tensors, replicas = lax.axis_size("tensor"), lax.axis_size("replica")
    members = tensors * replicas
    encoder = lax.axis_index("section") < sections // 2
    own = w_proj.shape[2]
    own_p = -(-own // 16) * 16
    rows, width = incoming.shape[1], w_up.shape[1]
    width_p = members * own_p
    hidden = w_up.shape[2]
    ticks = crop_ids.shape[1]
    saved = pool_mixed.shape[1]

    def padded(x, axis):
        if own == own_p:
            return x
        count = x.shape[axis] // own
        shape = x.shape[:axis] + (count, own) + x.shape[axis + 1:]
        fill = [(0, 0)] * (x.ndim + 1)
        fill[axis + 1] = (0, own_p - own)
        shape_p = x.shape[:axis] + (count * own_p,) + x.shape[axis + 1:]
        return jnp.pad(x.reshape(shape), fill).reshape(shape_p)

    proj = padded(padded(w_proj[0], 1), 2)
    up, down = padded(w_up[0], 0), padded(w_down[0], 1)
    pool_own = padded(pool_mixed[0], 1)
    keep = jnp.where(encoder, 0.0, 1.0).astype(f32)[None]
    features = pool_inputs[0].transpose(1, 2, 0).reshape(2, replicas, own, saved)
    features = padded(features, 2)
    seed = padded(incoming[0].T, 0)
    loss = loss_grads.transpose(0, 2, 1).reshape(ticks - 1, replicas, own, rows)
    loss = padded(loss, 2)

    shape = jax.ShapeDtypeStruct
    vmem = pl.BlockSpec(memory_space=pltpu.VMEM)
    hbm = pl.BlockSpec(memory_space=pl.ANY)
    dma = pltpu.SemaphoreType.DMA
    square = tensors == 2 and replicas == 2 and own_p % 32 == 0
    flows = 6 if square else members - 1
    terms = 2 if square else members - 1
    scratch = [
        pltpu.VMEM(proj.shape, bf16), pltpu.VMEM(up.shape, bf16), pltpu.VMEM(down.shape, bf16),
        pltpu.VMEM(loss.shape, bf16), pltpu.VMEM((replicas,) + crop_ids.shape[1:], jnp.int32),
        pltpu.VMEM((replicas, ticks - 1, own_p, rows), bf16),
        pltpu.VMEM((replicas, saved, width_p), bf16), pltpu.VMEM((width_p, replicas * saved), bf16),
        pltpu.VMEM((hidden, replicas * saved), bf16),
        pltpu.VMEM((ticks, replicas, width_p, rows), bf16),
        pltpu.VMEM((ticks, replicas, width_p, rows), bf16),
        pltpu.VMEM((ticks, replicas, hidden, rows), bf16),
        pltpu.VMEM((ticks, replicas, members - 1, own_p, rows), bf16),
        pltpu.VMEM((ticks, replicas, 2, own_p // 2, rows), bf16),
        pltpu.VMEM((ticks, replicas, terms, own_p, rows), bf16),
        pltpu.VMEM((replicas, 2, own_p // 2, rows), f32),
        pltpu.VMEM((replicas, own_p, rows), f32),
        pltpu.VMEM((replicas, hidden, saved), bf16), pltpu.VMEM((replicas, hidden, saved), bf16),
        pltpu.VMEM((replicas, hidden, rows), f32),
        pltpu.VMEM((ticks, replicas, 2, own_p, rows), bf16),
        pltpu.VMEM((ticks - 1, replicas, 2, own_p, rows), bf16),
        pltpu.VMEM((replicas, saved, hidden), f32), pltpu.VMEM((replicas, saved, width_p), f32),
        pltpu.VMEM((replicas, saved, width_p), f32),
        pltpu.VMEM((replicas * saved, hidden), bf16), pltpu.VMEM((replicas * saved, width_p), bf16),
        pltpu.VMEM((replicas * saved, width_p), bf16),
        dma((8,)), dma((6,)), dma((2, max(2, replicas - 1))), dma((2, replicas - 1)),
        dma((2, replicas - 1)), dma((2, replicas - 1)), dma((2, flows)),
        dma((2, ticks, replicas, flows)), dma((2, ticks, replicas, flows)),
        dma((2, ticks - 1, replicas, flows)), dma((2, ticks - 1, replicas, 2)),
        dma((2, replicas - 1, 2)),
    ]
    in_got, pool_t, act_t, sum_hidden, sum_grad, sum_up, out = pl.pallas_call(
        functools.partial(ticks_kernel, sections, tensors, replicas, own_p, ticks),
        out_shape=(
            shape((replicas, 2, own_p, saved), bf16),
            shape((width_p, replicas * saved), bf16),
            shape((hidden, replicas * saved), bf16),
            shape((replicas * saved, hidden), bf16),
            shape((replicas * saved, width_p), bf16),
            shape((replicas * saved, width_p), bf16),
            shape((2, replicas, own_p, rows), bf16),
        ),
        in_specs=[hbm] * 8,
        out_specs=(hbm,) * 7,
        scratch_shapes=scratch,
        compiler_params=pltpu.CompilerParams(
            collective_id=0, has_side_effects=True, vmem_limit_bytes=60 * 1024 * 1024
        ),
        name="ticks",
    )(features, pool_own, crop_ids[0], seed, loss, proj, up, down)

    def trimmed(x, axis):
        if own == own_p:
            return x
        count = x.shape[axis] // own_p
        x = x.reshape(x.shape[:axis] + (count, own_p) + x.shape[axis + 1:])
        x = lax.slice_in_dim(x, 0, own, axis=axis + 1)
        return x.reshape(x.shape[:axis] + (count * own,) + x.shape[axis + 2:])

    kept = (act_t, sum_up, pool_t, sum_hidden)
    grad_down, grad_up, grad_proj, outgoing = pl.pallas_call(
        functools.partial(tail_kernel, replicas),
        out_shape=(
            shape((hidden, width_p), bf16), shape((width_p, hidden), bf16),
            shape((2, own_p, width_p), bf16), shape(out.shape, bf16),
        ),
        in_specs=[pl.BlockSpec(memory_space=pltpu.SMEM)] + [hbm] * 8,
        out_specs=(hbm,) * 4,
        scratch_shapes=[pltpu.VMEM(x.shape, bf16) for x in kept] + [
            pltpu.VMEM((2, own_p, replicas * saved), bf16), pltpu.VMEM(sum_grad.shape, bf16),
            pltpu.VMEM(out.shape, bf16),
            pltpu.VMEM((hidden, width_p), bf16), pltpu.VMEM((width_p, hidden), bf16),
            pltpu.VMEM((2, own_p, width_p), bf16),
            dma((6 + replicas,)),
            dma((-(-hidden // 128) - (-width_p // 128) + 5,)),
        ],
        compiler_params=pltpu.CompilerParams(vmem_limit_bytes=60 * 1024 * 1024),
        name="tail",
    )(keep, *kept, features, in_got, sum_grad, out)
    grad_down = trimmed(grad_down, 1)[None]
    grad_up = trimmed(grad_up, 0)[None]
    grad_proj = trimmed(trimmed(grad_proj, 1), 2)[None]
    outgoing = trimmed(outgoing, 2).reshape(2, replicas * own, rows).transpose(2, 0, 1)
    return grad_proj, grad_up, grad_down, outgoing[None]


def solution(mesh):
    in_specs = (
        P("section", "replica", None, "tensor"),
        P("section", "replica", None),
        P("section", "replica", None),
        P("section", "replica", "tensor"),
        P(None, "replica", "tensor"),
        P("section", None, ("tensor", "replica"), None),
        P("section", None, ("tensor", "replica")),
        P("section", ("tensor", "replica"), None),
    )
    out_specs = (
        P("section", None, ("tensor", "replica"), None),
        P("section", None, ("tensor", "replica")),
        P("section", ("tensor", "replica"), None),
        P("section", "replica", None, "tensor"),
    )
    return jax.shard_map(body, mesh=mesh, in_specs=in_specs, out_specs=out_specs, check_vma=False)
```

```python
import functools

import jax
import jax.numpy as jnp
from jax import lax
from jax.experimental import pallas as pl
from jax.experimental.pallas import tpu as pltpu
from jax.sharding import PartitionSpec as P

gelu_scale = 0.7978845608
gelu_cubic = 0.044715
bf16, f32 = jnp.bfloat16, jnp.float32
MESH = pl.DeviceIdType.MESH


def gelu_pair(pre_gelu):
    inner = gelu_scale * (pre_gelu + gelu_cubic * pre_gelu * pre_gelu * pre_gelu)
    tanh_part = jnp.tanh(inner)
    gelu_value = 0.5 * pre_gelu * (1.0 + tanh_part)
    gelu_slope = 0.5 * (1.0 + tanh_part) + 0.5 * pre_gelu * (
        1.0 - tanh_part * tanh_part
    ) * gelu_scale * (1.0 + 3.0 * gelu_cubic * pre_gelu * pre_gelu)
    return (gelu_value, gelu_slope)


def dot(a, b):
    return jnp.dot(a, b, preferred_element_type=f32)


def dot_nt(a, b):
    return lax.dot_general(a, b, (((1,), (1,)), ((), ())), preferred_element_type=f32)


def ticks_kernel(
    sections, tensors, replicas, own, ticks,
    inputs_hbm, pool_hbm, ids_hbm, seed_hbm, loss_hbm, proj_hbm, up_hbm, down_hbm,
    in_got, pool_out, act_out, hidden_out, grad_out, up_out, out,
    proj, up, down, loss_src, ids, loss_t, pool, pool_t, act_t,
    upstream, grads, hidden, part, relay, got, keep_part, own_part, slope_hi, slope_lo, slope,
    edge, edge_got, acc_hidden, acc_grad, acc_up, sum_hidden, sum_grad, sum_up,
    load_sem, out_sem, send_sems, pool_sems, inputs_sems, ids_sems, loss_sems, seed_sems,
    part_sems, grad_sems, up_sems, edge_sems, outgoing_sems, up_near,
):
    members = tensors * replicas
    square = tensors == 2 and replicas == 2 and own % 32 == 0
    half = own // 2
    section = lax.axis_index("section")
    tensor = lax.axis_index("tensor")
    replica = lax.axis_index("replica")
    me = tensor * replicas + replica
    hidden_rows = down.shape[0]
    saved = pool.shape[1]
    last = ticks - 1
    along = (1 - tensor) * replicas + replica
    across = tensor * replicas + (1 - replica)
    far = (1 - tensor) * replicas + (1 - replica)

    def device(s, member):
        return {
            "section": s,
            "tensor": lax.div(member, replicas),
            "replica": lax.rem(member, replicas),
        }

    def member_at(by):
        return lax.rem(me + by, members)

    def replica_at(by):
        return lax.rem(replica + by, replicas)

    def slab_of(member):
        return pl.ds(pl.multiple_of(member * own, 16), own)

    loads = []

    def load(src, dst):
        copy = pltpu.make_async_copy(src, dst, load_sem.at[len(loads)])
        copy.start()
        loads.append(copy)
        return copy

    wide = pl.ds(pl.multiple_of(tensor * (replicas * own), 16), replicas * own)
    ld_pool = load(pool_hbm, pool.at[replica])
    ld_seed = load(seed_hbm, upstream.at[0, replica, wide])
    ld_ids = load(ids_hbm, ids.at[replica])
    ld_up = load(up_hbm, up)
    ld_down = load(down_hbm, down)
    near = []
    if square:
        for i, member in enumerate((far, along, across, me)):
            near.append(load(up_hbm.at[slab_of(member)], up_near.at[pl.ds(i * own, own)]))
    ld_loss = load(loss_hbm, loss_src)
    ld_loss_own = load(loss_hbm.at[:, replica], loss_t.at[replica])
    ld_proj = load(proj_hbm, proj)

    barrier = pltpu.get_barrier_semaphore()
    above = lax.rem(section + 1, sections)
    below = lax.rem(section + sections - 1, sections)
    mirror = sections - 1 - section
    for by in range(1, members):
        pl.semaphore_signal(barrier, 1, device_id=device(section, member_at(by)), device_id_type=MESH)
    for other in (above, below, mirror):
        pl.semaphore_signal(barrier, 1, device_id=device(other, me), device_id_type=MESH)
    pl.semaphore_wait(barrier, members - 1 + 3)

    written = []
    POOL, IDS, SEED, PART, GRAD, UP, INPUTS, DOWN, SKIP, LOSS, OUT = range(11)

    def remote(src, dst, kind, recv_sem, s, member):
        return pltpu.make_async_remote_copy(
            src_ref=src, dst_ref=dst, send_sem=send_sems.at[kind], recv_sem=recv_sem,
            device_id=device(s, member), device_id_type=MESH,
        )

    def send(src, dst, kind, recv_sem, member):
        copy = remote(src, dst, kind, recv_sem, section, member)
        copy.start()
        return copy

    def over_replicas(src_of, dst, kind, sems):
        return [
            send(src_of(replica_at(by)), dst, kind, sems.at[by - 1], tensor * replicas + replica_at(by))
            for by in range(1, replicas)
        ]

    def all_sent(kind, ref):
        pltpu.make_async_copy(ref, ref, send_sems.at[kind]).wait()

    def write(src, dst):
        copy = pltpu.make_async_copy(src, dst, out_sem.at[len(written)])
        copy.start()
        written.append(copy)

    class Gather:
        def __init__(self, at, whole, kind, sems):
            self.at, self.kind, self.sems = at, kind, sems
            if square:
                self.copies = [self.put(me, 0, 0, along), self.put(me, 1, 1, across)]
            else:
                self.copies = [
                    send(whole, whole, kind, sems.at[by - 1], member_at(by))
                    for by in range(1, members)
                ]

        def put(self, member, h, i, to):
            ref = self.at(member, h)
            return send(ref, ref, self.kind, self.sems.at[i], to)

        def follow(self):
            if square:
                self.copies += [self.put(me, 1, 2, along), self.put(me, 0, 3, across)]

        def forward(self):
            if square:
                self.copies[0].wait_recv()
                self.copies.append(self.put(along, 0, 4, across))
                self.copies[1].wait_recv()
                self.copies.append(self.put(across, 1, 5, along))

        def finish(self):
            for copy in self.copies[2 if square else 0:]:
                copy.wait_recv()

    def halves_of(ref):
        return lambda member, h: ref.at[pl.ds(pl.multiple_of(member * own + h * half, 16), half)]

    def seed_at(member, h):
        return upstream.at[0, lax.rem(member, replicas),
                           pl.ds(pl.multiple_of(lax.div(member, replicas) * (replicas * own) + h * own, 16), own)]

    slab = slab_of(me)
    low, high = pl.ds(0, half), pl.ds(half, half)
    ld_pool.wait()
    pieces = 2
    if square:
        rows = saved // (2 * pieces)

        def piece(r, p):
            return pool.at[r, pl.ds(pl.multiple_of((tensor * pieces + p) * rows, 8), rows)]

        pool_in = [
            send(piece(replica, p), piece(replica, p), POOL, pool_sems.at[p], across)
            for p in range(pieces)
        ]
    else:
        pool_in = over_replicas(lambda r: pool.at[replica], pool.at[replica], POOL, pool_sems)
    ld_seed.wait()
    seed_in = Gather(seed_at, upstream.at[0, replica, wide], SEED, seed_sems)
    seed_in.follow()
    ld_ids.wait()
    ids_in = over_replicas(lambda r: ids.at[replica], ids.at[replica], IDS, ids_sems)
    is_top = section == sections - 1

    step = 256 if hidden_rows % 256 == 0 else 128

    def pre_slopes(r):
        def pre_at(start, size):
            cols = pl.ds(start, size)
            value, gelu_slope = gelu_pair(dot(pool[r], up[:, cols]).T)
            act_t[cols, pl.ds(pl.multiple_of(r * saved, 128), saved)] = value.astype(bf16)
            high = gelu_slope.astype(bf16)
            slope_hi[r, cols, :] = high
            slope_lo[r, cols, :] = (gelu_slope - high.astype(f32)).astype(bf16)

        @pl.loop(0, hidden_rows // step)
        def _(c):
            pre_at(pl.multiple_of(c * step, step), step)

        if hidden_rows % step:
            pre_at(hidden_rows - hidden_rows % step, hidden_rows % step)

    ld_up.wait()
    pre_slopes(replica)
    if square:
        pool_over = []
        for p in range(pieces):
            pool_in[p].wait_recv()
            come = piece(1 - replica, p)
            pool_over.append(send(come, come, POOL, pool_sems.at[pieces + p], along))
        seed_in.forward()
        for copy in pool_over:
            copy.wait_recv()
        pre_slopes(1 - replica)
    else:
        for by in range(1, replicas):
            pool_in[by - 1].wait_recv()
            pre_slopes(lax.rem(replica + replicas - by, replicas))
    write(act_t, act_out)
    for copy in ids_in:
        copy.wait_recv()

    def picks(t, r):
        row = ids[r, pl.ds(t, 1), :]
        place_of = lax.broadcasted_iota(jnp.int32, (saved, row.shape[1]), 0)
        return jnp.where(place_of == row, 1.0, 0.0).astype(bf16)

    def pick_slope(t, r):
        chosen = picks(t, r)
        slope[r] = dot(slope_hi[r], chosen) + dot(slope_lo[r], chosen)

    for r in range(replicas):
        pick_slope(0, r)

    ld_down.wait()
    for copy in near:
        copy.wait()
    seed_in.finish()

    up_in, part_in, grad_in, edge_in = {}, {}, {}, {}

    def stage_hidden(t, r):
        if t > 0:
            up_in[t, r].finish()
        hidden[t, r] = (dot(down[...], upstream[t, r]) * slope[r]).astype(bf16)
        if square:
            part[t, r, 0] = dot(up_near[:own, :], hidden[t, r]).astype(bf16)
            part_in[t, r] = [
                send(part.at[t, r, 0, low], relay.at[t, r, 0], PART, part_sems.at[r, 0], across),
                send(part.at[t, r, 0, high], relay.at[t, r, 1], PART, part_sems.at[r, 1], along),
            ]

    def stage_parts(t, r):
        if square:
            near_terms = dot(up_near[own:, :], hidden[t, r])
            part[t, r, 1, high] = near_terms[half:own].astype(bf16)
            part[t, r, 2, low] = near_terms[own:own + half].astype(bf16)
            part_in[t, r] += [
                send(part.at[t, r, 1, high], got.at[t, r, 0, high], PART, part_sems.at[r, 2], along),
                send(part.at[t, r, 2, low], got.at[t, r, 1, low], PART, part_sems.at[r, 3], across),
            ]
            keep_part[r, 0] = near_terms[:half]
            keep_part[r, 1] = near_terms[own + half:2 * own]
            own_term = near_terms[2 * own:]
        else:
            part_in[t, r] = []
            for by in range(1, members):
                to = member_at(by)
                part[t, r, by - 1] = dot(up[slab_of(to), :], hidden[t, r]).astype(bf16)
                part_in[t, r].append(send(part.at[t, r, by - 1], got.at[t, r, by - 1], PART,
                                          part_sems.at[r, by - 1], to))
            own_term = dot(up[slab, :], hidden[t, r])
        own_part[r] = own_term + upstream[t, r, slab, :].astype(f32)

    def stage_relay(t, r):
        if square:
            for k, (to, rows) in enumerate(((along, low), (across, high))):
                part_in[t, r][k].wait_recv()
                part[t, r, k + 1, rows] = (keep_part[r, k] + relay[t, r, k].astype(f32)).astype(bf16)
                part_in[t, r].append(send(part.at[t, r, k + 1, rows], got.at[t, r, k, rows], PART,
                                          part_sems.at[r, 4 + k], to))

    def stage_sum(t, r):
        for copy in part_in[t, r][2 if square else 0:]:
            copy.wait_recv()
        total = own_part[r]
        for k in range(got.shape[2]):
            total = total + got[t, r, k].astype(f32)
        grads[t, r, slab, :] = total.astype(bf16)
        grad_in[t, r] = Gather(halves_of(grads.at[t, r]), grads.at[t, r, slab], GRAD, grad_sems.at[r])

    def stage_project(t, r):
        grad_in[t, r].finish()
        edge[t, r, 0] = dot(proj[0], grads[t, r]).astype(bf16)
        if t == last:
            return
        down_copy = remote(edge.at[t, r, 0], edge_got.at[t, r, 0], DOWN, edge_sems.at[t, r, 0], below, me)
        pl.when(section > 0)(down_copy.start)
        skip = remote(edge.at[t, r, 1], edge_got.at[t, r, 1], SKIP, edge_sems.at[t, r, 1], mirror, me)

        @pl.when(section >= sections // 2)
        def _():
            edge[t, r, 1] = dot(proj[1], grads[t, r]).astype(bf16)
            skip.start()

        edge_in[t, r] = (down_copy, skip)

    def stage_next(t, r):
        down_copy, skip = edge_in[t, r]

        @pl.when(section < sections // 2)
        def _():
            down_copy.wait_recv()
            skip.wait_recv()
            summed = edge_got[t, r, 0].astype(f32) + edge_got[t, r, 1].astype(f32)
            upstream[t + 1, r, slab, :] = summed.astype(bf16)

        @pl.when((section >= sections // 2) & (section < sections - 1))
        def _():
            down_copy.wait_recv()
            upstream[t + 1, r, slab, :] = edge_got[t, r, 0]

        @pl.when(is_top)
        def _():
            if r == 0:
                for copy in loss_in[t]:
                    copy.wait_recv()
            upstream[t + 1, r, slab, :] = loss_t[r, t]

        up_in[t + 1, r] = Gather(halves_of(upstream.at[t + 1, r]), upstream.at[t + 1, r, slab], UP, up_sems.at[r])

    def add(t, r, acc, total, term):
        rows = pl.ds(r * saved, saved)
        value = term if t == 0 else acc[r] + term
        if t == last:
            total[rows, :] = value.astype(bf16)
        else:
            acc[r] = value

    def settle(t, r):
        chosen = picks(t, r)
        add(t, r, acc_hidden, sum_hidden, dot_nt(chosen, hidden[t, r]))
        add(t, r, acc_up, sum_up, dot_nt(chosen, upstream[t, r]))

    every = range(replicas)
    loss_in, inputs_in = [], []
    slices = [(k, rows) for k in range(2) for rows in (low, pl.ds(half, own - half))]
    for t in range(ticks):
        for r in every:
            stage_hidden(t, r)
            if r > 0:
                stage_relay(t, r - 1)
            stage_parts(t, r)
        if t < last:
            if t == 0:
                ld_loss.wait()
                ld_loss_own.wait()
            loss_in.append([
                remote(loss_src.at[t, replica_at(by)], loss_t.at[replica, t], LOSS,
                       loss_sems.at[t, by - 1], section, tensor * replicas + replica_at(by))
                for by in range(1, replicas)
            ])
            for copy in loss_in[t]:
                pl.when(is_top)(copy.start)
        settle(t, 0)
        stage_relay(t, replicas - 1)
        for r in every:
            stage_sum(t, r)
            if r == 0:
                grad_in[t, r].follow()
            if r + 1 < replicas:
                settle(t, r + 1)
        if t == last:
            write(sum_hidden, hidden_out)
            write(sum_up, up_out)
        else:
            for r in every:
                pick_slope(t + 1, r)
        for r in every:
            grad_in[t, r].forward()
            if r + 1 < replicas:
                grad_in[t, r + 1].follow()
            if t == 0:
                pool_t[:, pl.ds(r * saved, saved)] = pool[r].T
        if t == 0:
            write(pool_t, pool_out)
            ld_proj.wait()
        if t == last:
            break
        for i, (k, rows) in enumerate(slices):
            if i * last // len(slices) == t:
                inputs_in += over_replicas(lambda r: inputs_hbm.at[k, r, rows], in_got.at[replica, k, rows],
                                           INPUTS, inputs_sems.at[i])
        for r in every:
            stage_project(t, r)
        for r in every:
            stage_next(t, r)
            if r == 0:
                up_in[t + 1, r].follow()
        for r in every:
            add(t, r, acc_grad, sum_grad, dot_nt(picks(t, r), grads[t, r]))
            up_in[t + 1, r].forward()
            if r + 1 < replicas:
                up_in[t + 1, r + 1].follow()

    outs = [
        [
            remote(edge.at[last, replica_at(by), k], out.at[k, replica], OUT,
                   outgoing_sems.at[by - 1, k], section, tensor * replicas + replica_at(by))
            for k in range(2)
        ]
        for by in range(1, replicas)
    ]
    for r in every:
        grad_in[last, r].finish()
        for k in range(2):
            edge[last, r, k] = dot(proj[k], grads[last, r]).astype(bf16)
            for by in range(1, replicas):
                pl.when(replica_at(by) == r)(outs[by - 1][k].start)
        add(last, r, acc_grad, sum_grad, dot_nt(picks(last, r), grads[last, r]))
    write(sum_grad, grad_out)
    write(edge.at[last, replica], out.at[:, replica])
    for copy in inputs_in + [copy for pair in outs for copy in pair]:
        copy.wait_recv()
    for copy in written:
        copy.wait()
    all_sent(POOL, pool.at[pl.ds(0, replicas - 1)])
    all_sent(IDS, ids.at[pl.ds(0, replicas - 1)])
    all_sent(SEED, part.at[0])
    all_sent(PART, part)
    all_sent(GRAD, part)
    all_sent(UP, part.at[pl.ds(0, last)])
    all_sent(INPUTS, in_got.at[pl.ds(0, replicas - 1)])
    all_sent(OUT, edge.at[last, pl.ds(0, replicas - 1)])
    pl.when(section > 0)(lambda: all_sent(DOWN, edge_got.at[:, :, 0]))
    pl.when(section >= sections // 2)(lambda: all_sent(SKIP, edge_got.at[:, :, 1]))
    pl.when(is_top)(lambda: all_sent(LOSS, loss_t.at[pl.ds(0, replicas - 1)]))


def tail_kernel(
    replicas, keep_ref, act_hbm, sum_up_hbm, pool_hbm, sum_hidden_hbm, inputs_hbm, in_got_hbm,
    sum_grad_hbm, outgoing_hbm,
    down_out, up_out, proj_out, outgoing_out,
    act, sum_up, pool, sum_hidden, inputs, sum_grad, outgoing, down_v, up_v, proj_v, load_sems, sems,
):
    replica = lax.axis_index("replica")
    saved = sum_up.shape[0] // replicas
    copies = []

    def lanes(r):
        return inputs.at[:, :, pl.ds(pl.multiple_of(r * saved, 128), saved)]

    pairs = [
        (act_hbm, act), (sum_up_hbm, sum_up), (pool_hbm, pool), (sum_hidden_hbm, sum_hidden),
        (sum_grad_hbm, sum_grad), (outgoing_hbm, outgoing),
        (inputs_hbm.at[:, replica], lanes(replica)),
    ]
    for by in range(1, replicas):
        r = lax.rem(replica + by, replicas)
        pairs.append((in_got_hbm.at[r], lanes(r)))
    loads = [
        pltpu.make_async_copy(src, dst, load_sems.at[i]) for i, (src, dst) in enumerate(pairs)
    ]
    for copy in loads:
        copy.start()

    def put(src, dst):
        copy = pltpu.make_async_copy(src, dst, sems.at[len(copies)])
        copy.start()
        copies.append(copy)

    def finish(a, b, rows, kept, out, scale=None):
        total = dot(a[rows], b[...])
        if scale is not None:
            total = total * scale
        kept.at[rows][...] = total.astype(bf16)
        put(kept.at[rows], out.at[rows])

    loads[0].wait()
    loads[1].wait()
    for start in range(0, down_v.shape[0], 128):
        finish(act, sum_up, pl.ds(start, min(128, down_v.shape[0] - start)), down_v, down_out)
    loads[2].wait()
    loads[3].wait()
    for start in range(0, up_v.shape[0], 128):
        finish(pool, sum_hidden, pl.ds(start, min(128, up_v.shape[0] - start)), up_v, up_out)
    loads[5].wait()
    put(outgoing, outgoing_out)
    loads[4].wait()
    for copy in loads[6:]:
        copy.wait()
    half = proj_v.shape[1] // 2
    for k in range(2):
        for start in (0, half):
            finish(inputs, sum_grad, (k, pl.ds(start, half)), proj_v, proj_out, keep_ref[0] if k else None)
    for copy in copies:
        copy.wait()


def body(pool_inputs, pool_mixed, crop_ids, incoming, loss_grads, w_proj, w_up, w_down):
    sections = lax.axis_size("section")
    tensors, replicas = lax.axis_size("tensor"), lax.axis_size("replica")
    members = tensors * replicas
    encoder = lax.axis_index("section") < sections // 2
    own = w_proj.shape[2]
    own_p = -(-own // 16) * 16
    rows, width = incoming.shape[1], w_up.shape[1]
    width_p = members * own_p
    hidden = w_up.shape[2]
    ticks = crop_ids.shape[1]
    saved = pool_mixed.shape[1]

    def padded(x, axis):
        if own == own_p:
            return x
        count = x.shape[axis] // own
        shape = x.shape[:axis] + (count, own) + x.shape[axis + 1:]
        fill = [(0, 0)] * (x.ndim + 1)
        fill[axis + 1] = (0, own_p - own)
        shape_p = x.shape[:axis] + (count * own_p,) + x.shape[axis + 1:]
        return jnp.pad(x.reshape(shape), fill).reshape(shape_p)

    proj = padded(padded(w_proj[0], 1), 2)
    up, down = padded(w_up[0], 0), padded(w_down[0], 1)
    pool_own = padded(pool_mixed[0], 1)
    keep = jnp.where(encoder, 0.0, 1.0).astype(f32)[None]
    features = pool_inputs[0].transpose(1, 2, 0).reshape(2, replicas, own, saved)
    features = padded(features, 2)
    seed = padded(incoming[0].T, 0)
    loss = loss_grads.transpose(0, 2, 1).reshape(ticks - 1, replicas, own, rows)
    loss = padded(loss, 2)

    shape = jax.ShapeDtypeStruct
    vmem = pl.BlockSpec(memory_space=pltpu.VMEM)
    hbm = pl.BlockSpec(memory_space=pl.ANY)
    dma = pltpu.SemaphoreType.DMA
    square = tensors == 2 and replicas == 2 and own_p % 32 == 0
    flows = 6 if square else members - 1
    terms = 2 if square else members - 1
    scratch = [
        pltpu.VMEM(proj.shape, bf16), pltpu.VMEM(up.shape, bf16), pltpu.VMEM(down.shape, bf16),
        pltpu.VMEM(loss.shape, bf16), pltpu.VMEM((replicas,) + crop_ids.shape[1:], jnp.int32),
        pltpu.VMEM((replicas, ticks - 1, own_p, rows), bf16),
        pltpu.VMEM((replicas, saved, width_p), bf16), pltpu.VMEM((width_p, replicas * saved), bf16),
        pltpu.VMEM((hidden, replicas * saved), bf16),
        pltpu.VMEM((ticks, replicas, width_p, rows), bf16),
        pltpu.VMEM((ticks, replicas, width_p, rows), bf16),
        pltpu.VMEM((ticks, replicas, hidden, rows), bf16),
        pltpu.VMEM((ticks, replicas, members - 1, own_p, rows), bf16),
        pltpu.VMEM((ticks, replicas, 2, own_p // 2, rows), bf16),
        pltpu.VMEM((ticks, replicas, terms, own_p, rows), bf16),
        pltpu.VMEM((replicas, 2, own_p // 2, rows), f32),
        pltpu.VMEM((replicas, own_p, rows), f32),
        pltpu.VMEM((replicas, hidden, saved), bf16), pltpu.VMEM((replicas, hidden, saved), bf16),
        pltpu.VMEM((replicas, hidden, rows), f32),
        pltpu.VMEM((ticks, replicas, 2, own_p, rows), bf16),
        pltpu.VMEM((ticks - 1, replicas, 2, own_p, rows), bf16),
        pltpu.VMEM((replicas, saved, hidden), f32), pltpu.VMEM((replicas, saved, width_p), f32),
        pltpu.VMEM((replicas, saved, width_p), f32),
        pltpu.VMEM((replicas * saved, hidden), bf16), pltpu.VMEM((replicas * saved, width_p), bf16),
        pltpu.VMEM((replicas * saved, width_p), bf16),
        dma((12,)), dma((6,)), dma((11,)), dma((max(4, replicas - 1),)), dma((4, replicas - 1)),
        dma((replicas - 1,)), dma((ticks - 1, replicas - 1)), dma((flows,)),
        dma((replicas, flows)), dma((replicas, flows)), dma((replicas, flows)),
        dma((ticks - 1, replicas, 2)), dma((replicas - 1, 2)),
        pltpu.VMEM(up.shape if square else (16, 128), bf16),
    ]
    in_got, pool_t, act_t, sum_hidden, sum_grad, sum_up, out = pl.pallas_call(
        functools.partial(ticks_kernel, sections, tensors, replicas, own_p, ticks),
        out_shape=(
            shape((replicas, 2, own_p, saved), bf16),
            shape((width_p, replicas * saved), bf16),
            shape((hidden, replicas * saved), bf16),
            shape((replicas * saved, hidden), bf16),
            shape((replicas * saved, width_p), bf16),
            shape((replicas * saved, width_p), bf16),
            shape((2, replicas, own_p, rows), bf16),
        ),
        in_specs=[hbm] * 8,
        out_specs=(hbm,) * 7,
        scratch_shapes=scratch,
        compiler_params=pltpu.CompilerParams(
            collective_id=0, has_side_effects=True, vmem_limit_bytes=60 * 1024 * 1024
        ),
        name="ticks",
    )(features, pool_own, crop_ids[0], seed, loss, proj, up, down)

    def trimmed(x, axis):
        if own == own_p:
            return x
        count = x.shape[axis] // own_p
        x = x.reshape(x.shape[:axis] + (count, own_p) + x.shape[axis + 1:])
        x = lax.slice_in_dim(x, 0, own, axis=axis + 1)
        return x.reshape(x.shape[:axis] + (count * own,) + x.shape[axis + 2:])

    kept = (act_t, sum_up, pool_t, sum_hidden)
    grad_down, grad_up, grad_proj, outgoing = pl.pallas_call(
        functools.partial(tail_kernel, replicas),
        out_shape=(
            shape((hidden, width_p), bf16), shape((width_p, hidden), bf16),
            shape((2, own_p, width_p), bf16), shape(out.shape, bf16),
        ),
        in_specs=[pl.BlockSpec(memory_space=pltpu.SMEM)] + [hbm] * 8,
        out_specs=(hbm,) * 4,
        scratch_shapes=[pltpu.VMEM(x.shape, bf16) for x in kept] + [
            pltpu.VMEM((2, own_p, replicas * saved), bf16), pltpu.VMEM(sum_grad.shape, bf16),
            pltpu.VMEM(out.shape, bf16),
            pltpu.VMEM((hidden, width_p), bf16), pltpu.VMEM((width_p, hidden), bf16),
            pltpu.VMEM((2, own_p, width_p), bf16),
            dma((6 + replicas,)),
            dma((-(-hidden // 128) - (-width_p // 128) + 5,)),
        ],
        compiler_params=pltpu.CompilerParams(vmem_limit_bytes=60 * 1024 * 1024),
        name="tail",
    )(keep, *kept, features, in_got, sum_grad, out)
    grad_down = trimmed(grad_down, 1)[None]
    grad_up = trimmed(grad_up, 0)[None]
    grad_proj = trimmed(trimmed(grad_proj, 1), 2)[None]
    outgoing = trimmed(outgoing, 2).reshape(2, replicas * own, rows).transpose(2, 0, 1)
    return grad_proj, grad_up, grad_down, outgoing[None]


def solution(mesh):
    in_specs = (
        P("section", "replica", None, "tensor"),
        P("section", "replica", None),
        P("section", "replica", None),
        P("section", "replica", "tensor"),
        P(None, "replica", "tensor"),
        P("section", None, ("tensor", "replica"), None),
        P("section", None, ("tensor", "replica")),
        P("section", ("tensor", "replica"), None),
    )
    out_specs = (
        P("section", None, ("tensor", "replica"), None),
        P("section", None, ("tensor", "replica")),
        P("section", ("tensor", "replica"), None),
        P("section", "replica", None, "tensor"),
    )
    return jax.shard_map(body, mesh=mesh, in_specs=in_specs, out_specs=out_specs, check_vma=False)
```

```python
import functools

import jax
import jax.numpy as jnp
from jax import lax
from jax.experimental import pallas as pl
from jax.experimental.pallas import tpu as pltpu
from jax.sharding import PartitionSpec as P

gelu_scale = 0.7978845608
gelu_cubic = 0.044715
bf16, f32 = jnp.bfloat16, jnp.float32
MESH = pl.DeviceIdType.MESH


def gelu_pair(pre_gelu):
    inner = gelu_scale * (pre_gelu + gelu_cubic * pre_gelu * pre_gelu * pre_gelu)
    tanh_part = jnp.tanh(inner)
    gelu_value = 0.5 * pre_gelu * (1.0 + tanh_part)
    gelu_slope = 0.5 * (1.0 + tanh_part) + 0.5 * pre_gelu * (
        1.0 - tanh_part * tanh_part
    ) * gelu_scale * (1.0 + 3.0 * gelu_cubic * pre_gelu * pre_gelu)
    return (gelu_value, gelu_slope)


def dot(a, b):
    return jnp.dot(a, b, preferred_element_type=f32)


def dot_nt(a, b):
    return lax.dot_general(a, b, (((1,), (1,)), ((), ())), preferred_element_type=f32)


def ticks_kernel(
    sections, tensors, replicas, own, ticks,
    inputs_hbm, pool_hbm, ids_hbm, seed_hbm, loss_hbm, proj_hbm, up_hbm, down_hbm,
    in_got, pool_out, act_out, hidden_out, grad_out, up_out, out,
    proj, up, down, loss_src, ids, loss_t, pool, pool_t, act_t,
    upstream, grads, hidden, part, relay, got, keep_part, own_part, slope_hi, slope_lo, slope,
    edge, edge_got, acc_hidden, acc_grad, acc_up, sum_hidden, sum_grad, sum_up,
    load_sem, out_sem, send_sems, pool_sems, inputs_sems, ids_sems, loss_sems, seed_sems,
    part_sems, grad_sems, up_sems, edge_sems, outgoing_sems, up_near,
):
    members = tensors * replicas
    square = tensors == 2 and replicas == 2 and own % 32 == 0
    half = own // 2
    section = lax.axis_index("section")
    tensor = lax.axis_index("tensor")
    replica = lax.axis_index("replica")
    me = tensor * replicas + replica
    hidden_rows = down.shape[0]
    saved = pool.shape[1]
    last = ticks - 1
    along = (1 - tensor) * replicas + replica
    across = tensor * replicas + (1 - replica)

    def device(s, member):
        return {
            "section": s,
            "tensor": lax.div(member, replicas),
            "replica": lax.rem(member, replicas),
        }

    def member_at(by):
        return lax.rem(me + by, members)

    def replica_at(by):
        return lax.rem(replica + by, replicas)

    def slab_of(member):
        return pl.ds(pl.multiple_of(member * own, 16), own)

    loads = []

    def load(src, dst):
        copy = pltpu.make_async_copy(src, dst, load_sem.at[len(loads)])
        copy.start()
        loads.append(copy)
        return copy

    near_order = {1: ((0, 0), (1, 0), (0, 1), (1, 1)), 0: ((0, 0), (0, 1), (1, 0), (1, 1))}

    def term(k, p, side):
        if k == 0:
            member = lax.rem(tensor + side, tensors) * replicas + p
        else:
            member = p * replicas + lax.rem(replica + side, replicas)
        return pl.ds(pl.multiple_of(member * own + k * half, 16), half)

    wide = pl.ds(pl.multiple_of(tensor * (replicas * own), 16), replicas * own)
    ld_pool = load(pool_hbm, pool.at[replica])
    ld_seed = load(seed_hbm, upstream.at[0, replica, wide])
    ld_ids = load(ids_hbm, ids.at[replica])
    ld_up = load(up_hbm, up)
    ld_down = load(down_hbm, down)
    near = []
    if square:
        order = [term(k, p, side) for side in (1, 0) for k, p in near_order[side]]
        for i, rows in enumerate(order):
            near.append(load(up_hbm.at[rows], up_near.at[pl.ds(i * half, half)]))
    ld_loss = load(loss_hbm, loss_src)
    ld_loss_own = load(loss_hbm.at[:, replica], loss_t.at[replica])
    ld_proj = load(proj_hbm, proj)

    barrier = pltpu.get_barrier_semaphore()
    above = lax.rem(section + 1, sections)
    below = lax.rem(section + sections - 1, sections)
    mirror = sections - 1 - section
    for by in range(1, members):
        pl.semaphore_signal(barrier, 1, device_id=device(section, member_at(by)), device_id_type=MESH)
    for other in (above, below, mirror):
        pl.semaphore_signal(barrier, 1, device_id=device(other, me), device_id_type=MESH)
    pl.semaphore_wait(barrier, members - 1 + 3)

    written = []
    POOL, IDS, SEED, PART, GRAD, UP, INPUTS, DOWN, SKIP, LOSS, OUT = range(11)

    def remote(src, dst, kind, recv_sem, s, member):
        return pltpu.make_async_remote_copy(
            src_ref=src, dst_ref=dst, send_sem=send_sems.at[kind], recv_sem=recv_sem,
            device_id=device(s, member), device_id_type=MESH,
        )

    def send(src, dst, kind, recv_sem, member):
        copy = remote(src, dst, kind, recv_sem, section, member)
        copy.start()
        return copy

    def over_replicas(src_of, dst, kind, sems):
        return [
            send(src_of(replica_at(by)), dst, kind, sems.at[by - 1], tensor * replicas + replica_at(by))
            for by in range(1, replicas)
        ]

    def all_sent(kind, ref):
        pltpu.make_async_copy(ref, ref, send_sems.at[kind]).wait()

    def write(src, dst):
        copy = pltpu.make_async_copy(src, dst, out_sem.at[len(written)])
        copy.start()
        written.append(copy)

    class Gather:
        def __init__(self, at, whole, kind, sems):
            self.at, self.kind, self.sems = at, kind, sems
            if square:
                self.copies = [self.put(me, 0, 0, along), self.put(me, 1, 1, across)]
            else:
                self.copies = [
                    send(whole, whole, kind, sems.at[by - 1], member_at(by))
                    for by in range(1, members)
                ]

        def put(self, member, h, i, to):
            ref = self.at(member, h)
            return send(ref, ref, self.kind, self.sems.at[i], to)

        def follow(self):
            if square:
                self.copies += [self.put(me, 1, 2, along), self.put(me, 0, 3, across)]

        def forward(self):
            if square:
                self.copies[0].wait_recv()
                self.copies.append(self.put(along, 0, 4, across))
                self.copies[1].wait_recv()
                self.copies.append(self.put(across, 1, 5, along))

        def finish(self):
            for copy in self.copies[2 if square else 0:]:
                copy.wait_recv()

    def halves_of(ref):
        return lambda member, h: ref.at[pl.ds(pl.multiple_of(member * own + h * half, 16), half)]

    def seed_at(member, h):
        return upstream.at[0, lax.rem(member, replicas),
                           pl.ds(pl.multiple_of(lax.div(member, replicas) * (replicas * own) + h * own, 16), own)]

    slab = slab_of(me)
    low, high = pl.ds(0, half), pl.ds(half, half)
    ld_pool.wait()
    pieces = 2
    if square:
        rows = saved // (2 * pieces)

        def piece(r, p):
            return pool.at[r, pl.ds(pl.multiple_of((tensor * pieces + p) * rows, 8), rows)]

        pool_in = [
            send(piece(replica, p), piece(replica, p), POOL, pool_sems.at[p], across)
            for p in range(pieces)
        ]
    else:
        pool_in = over_replicas(lambda r: pool.at[replica], pool.at[replica], POOL, pool_sems)
    ld_seed.wait()
    seed_in = Gather(seed_at, upstream.at[0, replica, wide], SEED, seed_sems)
    seed_in.follow()
    ld_ids.wait()
    ids_in = over_replicas(lambda r: ids.at[replica], ids.at[replica], IDS, ids_sems)
    is_top = section == sections - 1

    step = 256 if hidden_rows % 256 == 0 else 128

    def pre_slopes(r):
        def pre_at(start, size):
            cols = pl.ds(start, size)
            value, gelu_slope = gelu_pair(dot(pool[r], up[:, cols]).T)
            act_t[cols, pl.ds(pl.multiple_of(r * saved, 128), saved)] = value.astype(bf16)
            high = gelu_slope.astype(bf16)
            slope_hi[r, cols, :] = high
            slope_lo[r, cols, :] = (gelu_slope - high.astype(f32)).astype(bf16)

        @pl.loop(0, hidden_rows // step)
        def _(c):
            pre_at(pl.multiple_of(c * step, step), step)

        if hidden_rows % step:
            pre_at(hidden_rows - hidden_rows % step, hidden_rows % step)

    ld_up.wait()
    pre_slopes(replica)
    if square:
        pool_over = []
        for p in range(pieces):
            pool_in[p].wait_recv()
            come = piece(1 - replica, p)
            pool_over.append(send(come, come, POOL, pool_sems.at[pieces + p], along))
        seed_in.forward()
        for copy in pool_over:
            copy.wait_recv()
        pre_slopes(1 - replica)
    else:
        for by in range(1, replicas):
            pool_in[by - 1].wait_recv()
            pre_slopes(lax.rem(replica + replicas - by, replicas))
    write(act_t, act_out)
    for copy in ids_in:
        copy.wait_recv()

    def picks(t, r):
        row = ids[r, pl.ds(t, 1), :]
        place_of = lax.broadcasted_iota(jnp.int32, (saved, row.shape[1]), 0)
        return jnp.where(place_of == row, 1.0, 0.0).astype(bf16)

    def pick_slope(t, r):
        chosen = picks(t, r)
        slope[r] = dot(slope_hi[r], chosen) + dot(slope_lo[r], chosen)

    for r in range(replicas):
        pick_slope(0, r)

    ld_down.wait()
    for copy in near:
        copy.wait()
    seed_in.finish()

    up_in, part_in, grad_in, edge_in = {}, {}, {}, {}

    def stage_hidden(t, r):
        if t > 0:
            up_in[t, r].finish()
        hidden[t, r] = (dot(down[...], upstream[t, r]) * slope[r]).astype(bf16)
        if square:
            part[t, r, 0] = dot(up_near[:own, :], hidden[t, r]).astype(bf16)
            part_in[t, r] = put_terms(t, r, 0)

    def put_terms(t, r, p):
        return [
            send(part.at[t, r, p, rows], relay.at[t, r, 0, k, p], PART, part_sems.at[r, 2 * p + k], to)
            for k, (to, rows) in enumerate(((along, low), (across, high)))
        ]

    def stage_parts(t, r):
        if square:
            near_terms = dot(up_near[own:, :], hidden[t, r])
            part[t, r, 1] = near_terms[:own].astype(bf16)
            part_in[t, r] += put_terms(t, r, 1)
            for k in range(2):
                for p in range(2):
                    start = own + (2 * k + p) * half
                    keep_part[r, k, p] = near_terms[start:start + half]
            return
        part_in[t, r] = []
        for by in range(1, members):
            to = member_at(by)
            part[t, r, by - 1] = dot(up[slab_of(to), :], hidden[t, r]).astype(bf16)
            part_in[t, r].append(send(part.at[t, r, by - 1], got.at[t, r, by - 1], PART,
                                      part_sems.at[r, by - 1], to))
        own_part[r] = dot(up[slab, :], hidden[t, r]) + upstream[t, r, slab, :].astype(f32)

    def stage_relay(t, r):
        if square:
            for p in range(2):
                for k, to in enumerate((across, along)):
                    part_in[t, r][2 * p + k].wait_recv()
                    total = keep_part[r, k, p] + relay[t, r, 0, k, p].astype(f32)
                    relay[t, r, 1, k, p] = total.astype(bf16)
                    part_in[t, r].append(send(relay.at[t, r, 1, k, p], relay.at[t, r, 2, k, p], PART,
                                              part_sems.at[r, 4 + 2 * p + k], to))

    def stage_sum(t, r):
        if square:
            grad_in[t, r] = []
            for p in range(2):
                for k, to in enumerate((along, across)):
                    part_in[t, r][4 + 2 * p + k].wait_recv()
                    rows = term(k, p, 0)
                    total = relay[t, r, 1, k, p].astype(f32) + relay[t, r, 2, k, p].astype(f32)
                    grads[t, r, rows, :] = (total + upstream[t, r, rows, :].astype(f32)).astype(bf16)
                    mine = grads.at[t, r, rows]
                    grad_in[t, r].append(send(mine, mine, GRAD, grad_sems.at[r, 2 * p + k], to))
            return
        for copy in part_in[t, r]:
            copy.wait_recv()
        total = own_part[r]
        for k in range(got.shape[2]):
            total = total + got[t, r, k].astype(f32)
        grads[t, r, slab, :] = total.astype(bf16)
        grad_in[t, r] = Gather(halves_of(grads.at[t, r]), grads.at[t, r, slab], GRAD, grad_sems.at[r]).copies

    def have_grads(t, r):
        for copy in grad_in[t, r]:
            copy.wait_recv()

    def stage_project(t, r):
        have_grads(t, r)
        edge[t, r, 0] = dot(proj[0], grads[t, r]).astype(bf16)
        if t == last:
            return
        down_copy = remote(edge.at[t, r, 0], edge_got.at[t, r, 0], DOWN, edge_sems.at[t, r, 0], below, me)
        pl.when(section > 0)(down_copy.start)
        skip = remote(edge.at[t, r, 1], edge_got.at[t, r, 1], SKIP, edge_sems.at[t, r, 1], mirror, me)

        @pl.when(section >= sections // 2)
        def _():
            edge[t, r, 1] = dot(proj[1], grads[t, r]).astype(bf16)
            skip.start()

        edge_in[t, r] = (down_copy, skip)

    def stage_next(t, r):
        down_copy, skip = edge_in[t, r]

        @pl.when(section < sections // 2)
        def _():
            down_copy.wait_recv()
            skip.wait_recv()
            summed = edge_got[t, r, 0].astype(f32) + edge_got[t, r, 1].astype(f32)
            upstream[t + 1, r, slab, :] = summed.astype(bf16)

        @pl.when((section >= sections // 2) & (section < sections - 1))
        def _():
            down_copy.wait_recv()
            upstream[t + 1, r, slab, :] = edge_got[t, r, 0]

        @pl.when(is_top)
        def _():
            if r == 0:
                for copy in loss_in[t]:
                    copy.wait_recv()
            upstream[t + 1, r, slab, :] = loss_t[r, t]

        up_in[t + 1, r] = Gather(halves_of(upstream.at[t + 1, r]), upstream.at[t + 1, r, slab], UP, up_sems.at[r])

    def add(t, r, acc, total, term):
        rows = pl.ds(r * saved, saved)
        value = term if t == 0 else acc[r] + term
        if t == last:
            total[rows, :] = value.astype(bf16)
        else:
            acc[r] = value

    def settle(t, r):
        chosen = picks(t, r)
        add(t, r, acc_hidden, sum_hidden, dot_nt(chosen, hidden[t, r]))
        add(t, r, acc_up, sum_up, dot_nt(chosen, upstream[t, r]))

    every = range(replicas)
    loss_in, inputs_in = [], []
    slices = [(k, rows) for k in range(2) for rows in (low, pl.ds(half, own - half))]
    for t in range(ticks):
        for r in every:
            stage_hidden(t, r)
            stage_parts(t, r)
        if t < last:
            if t == 0:
                ld_loss.wait()
                ld_loss_own.wait()
            loss_in.append([
                remote(loss_src.at[t, replica_at(by)], loss_t.at[replica, t], LOSS,
                       loss_sems.at[t, by - 1], section, tensor * replicas + replica_at(by))
                for by in range(1, replicas)
            ])
            for copy in loss_in[t]:
                pl.when(is_top)(copy.start)
        for r in every:
            stage_relay(t, r)
            if r == 0:
                settle(t, r)
        for r in every:
            stage_sum(t, r)
            if r + 1 < replicas:
                settle(t, r + 1)
        if t == last:
            write(sum_hidden, hidden_out)
            write(sum_up, up_out)
        else:
            for r in every:
                pick_slope(t + 1, r)
        if t == 0:
            for r in every:
                pool_t[:, pl.ds(r * saved, saved)] = pool[r].T
        if t == 0:
            write(pool_t, pool_out)
            ld_proj.wait()
        if t == last:
            break
        for i, (k, rows) in enumerate(slices):
            if i * last // len(slices) == t:
                inputs_in += over_replicas(lambda r: inputs_hbm.at[k, r, rows], in_got.at[replica, k, rows],
                                           INPUTS, inputs_sems.at[i])
        for r in every:
            stage_project(t, r)
        for r in every:
            stage_next(t, r)
            if r == 0:
                up_in[t + 1, r].follow()
        for r in every:
            add(t, r, acc_grad, sum_grad, dot_nt(picks(t, r), grads[t, r]))
            up_in[t + 1, r].forward()
            if r + 1 < replicas:
                up_in[t + 1, r + 1].follow()

    outs = [
        [
            remote(edge.at[last, replica_at(by), k], out.at[k, replica], OUT,
                   outgoing_sems.at[by - 1, k], section, tensor * replicas + replica_at(by))
            for k in range(2)
        ]
        for by in range(1, replicas)
    ]
    for r in every:
        have_grads(last, r)
        for k in range(2):
            edge[last, r, k] = dot(proj[k], grads[last, r]).astype(bf16)
            for by in range(1, replicas):
                pl.when(replica_at(by) == r)(outs[by - 1][k].start)
        add(last, r, acc_grad, sum_grad, dot_nt(picks(last, r), grads[last, r]))
    write(sum_grad, grad_out)
    write(edge.at[last, replica], out.at[:, replica])
    for copy in inputs_in + [copy for pair in outs for copy in pair]:
        copy.wait_recv()
    for copy in written:
        copy.wait()
    all_sent(POOL, pool.at[pl.ds(0, replicas - 1)])
    all_sent(IDS, ids.at[pl.ds(0, replicas - 1)])
    others = pl.ds(0, (members - 1) * own)
    all_sent(SEED, upstream.at[0, :, others])
    all_sent(PART, upstream if square else part)
    all_sent(GRAD, upstream.at[:, :, pl.ds(0, 2 * own)] if square else part)
    all_sent(UP, upstream.at[pl.ds(0, last), :, others])
    all_sent(INPUTS, in_got.at[pl.ds(0, replicas - 1)])
    all_sent(OUT, edge.at[last, pl.ds(0, replicas - 1)])
    pl.when(section > 0)(lambda: all_sent(DOWN, edge_got.at[:, :, 0]))
    pl.when(section >= sections // 2)(lambda: all_sent(SKIP, edge_got.at[:, :, 1]))
    pl.when(is_top)(lambda: all_sent(LOSS, loss_t.at[pl.ds(0, replicas - 1)]))


def tail_kernel(
    replicas, keep_ref, act_hbm, sum_up_hbm, pool_hbm, sum_hidden_hbm, inputs_hbm, in_got_hbm,
    sum_grad_hbm, outgoing_hbm,
    down_out, up_out, proj_out, outgoing_out,
    act, sum_up, pool, sum_hidden, inputs, sum_grad, outgoing, down_v, up_v, proj_v, load_sems, sems,
):
    replica = lax.axis_index("replica")
    saved = sum_up.shape[0] // replicas
    copies = []

    def lanes(r):
        return inputs.at[:, :, pl.ds(pl.multiple_of(r * saved, 128), saved)]

    pairs = [
        (act_hbm, act), (sum_up_hbm, sum_up), (pool_hbm, pool), (sum_hidden_hbm, sum_hidden),
        (sum_grad_hbm, sum_grad), (outgoing_hbm, outgoing),
        (inputs_hbm.at[:, replica], lanes(replica)),
    ]
    for by in range(1, replicas):
        r = lax.rem(replica + by, replicas)
        pairs.append((in_got_hbm.at[r], lanes(r)))
    loads = [
        pltpu.make_async_copy(src, dst, load_sems.at[i]) for i, (src, dst) in enumerate(pairs)
    ]
    for copy in loads:
        copy.start()

    def put(src, dst):
        copy = pltpu.make_async_copy(src, dst, sems.at[len(copies)])
        copy.start()
        copies.append(copy)

    def finish(a, b, rows, kept, out, scale=None):
        total = dot(a[rows], b[...])
        if scale is not None:
            total = total * scale
        kept.at[rows][...] = total.astype(bf16)
        put(kept.at[rows], out.at[rows])

    loads[0].wait()
    loads[1].wait()
    for start in range(0, down_v.shape[0], 128):
        finish(act, sum_up, pl.ds(start, min(128, down_v.shape[0] - start)), down_v, down_out)
    loads[2].wait()
    loads[3].wait()
    for start in range(0, up_v.shape[0], 128):
        finish(pool, sum_hidden, pl.ds(start, min(128, up_v.shape[0] - start)), up_v, up_out)
    loads[5].wait()
    put(outgoing, outgoing_out)
    loads[4].wait()
    for copy in loads[6:]:
        copy.wait()
    half = proj_v.shape[1] // 2
    for k in range(2):
        for start in (0, half):
            finish(inputs, sum_grad, (k, pl.ds(start, half)), proj_v, proj_out, keep_ref[0] if k else None)
    for copy in copies:
        copy.wait()


def body(pool_inputs, pool_mixed, crop_ids, incoming, loss_grads, w_proj, w_up, w_down):
    sections = lax.axis_size("section")
    tensors, replicas = lax.axis_size("tensor"), lax.axis_size("replica")
    members = tensors * replicas
    encoder = lax.axis_index("section") < sections // 2
    own = w_proj.shape[2]
    own_p = -(-own // 16) * 16
    rows, width = incoming.shape[1], w_up.shape[1]
    width_p = members * own_p
    hidden = w_up.shape[2]
    ticks = crop_ids.shape[1]
    saved = pool_mixed.shape[1]

    def padded(x, axis):
        if own == own_p:
            return x
        count = x.shape[axis] // own
        shape = x.shape[:axis] + (count, own) + x.shape[axis + 1:]
        fill = [(0, 0)] * (x.ndim + 1)
        fill[axis + 1] = (0, own_p - own)
        shape_p = x.shape[:axis] + (count * own_p,) + x.shape[axis + 1:]
        return jnp.pad(x.reshape(shape), fill).reshape(shape_p)

    proj = padded(padded(w_proj[0], 1), 2)
    up, down = padded(w_up[0], 0), padded(w_down[0], 1)
    pool_own = padded(pool_mixed[0], 1)
    keep = jnp.where(encoder, 0.0, 1.0).astype(f32)[None]
    features = pool_inputs[0].transpose(1, 2, 0).reshape(2, replicas, own, saved)
    features = padded(features, 2)
    seed = padded(incoming[0].T, 0)
    loss = loss_grads.transpose(0, 2, 1).reshape(ticks - 1, replicas, own, rows)
    loss = padded(loss, 2)

    shape = jax.ShapeDtypeStruct
    vmem = pl.BlockSpec(memory_space=pltpu.VMEM)
    hbm = pl.BlockSpec(memory_space=pl.ANY)
    dma = pltpu.SemaphoreType.DMA
    square = tensors == 2 and replicas == 2 and own_p % 32 == 0
    flows = 6 if square else members - 1
    terms = 8 if square else members - 1
    scratch = [
        pltpu.VMEM(proj.shape, bf16), pltpu.VMEM(up.shape, bf16), pltpu.VMEM(down.shape, bf16),
        pltpu.VMEM(loss.shape, bf16), pltpu.VMEM((replicas,) + crop_ids.shape[1:], jnp.int32),
        pltpu.VMEM((replicas, ticks - 1, own_p, rows), bf16),
        pltpu.VMEM((replicas, saved, width_p), bf16), pltpu.VMEM((width_p, replicas * saved), bf16),
        pltpu.VMEM((hidden, replicas * saved), bf16),
        pltpu.VMEM((ticks, replicas, width_p, rows), bf16),
        pltpu.VMEM((ticks, replicas, width_p, rows), bf16),
        pltpu.VMEM((ticks, replicas, hidden, rows), bf16),
        pltpu.VMEM((ticks, replicas, 2 if square else members - 1, own_p, rows), bf16),
        pltpu.VMEM((ticks, replicas, 3, 2, 2, own_p // 2, rows) if square else (16, 128), bf16),
        pltpu.VMEM((16, 128) if square else (ticks, replicas, members - 1, own_p, rows), bf16),
        pltpu.VMEM((replicas, 2, 2, own_p // 2, rows) if square else (8, 128), f32),
        pltpu.VMEM((replicas, own_p, rows), f32),
        pltpu.VMEM((replicas, hidden, saved), bf16), pltpu.VMEM((replicas, hidden, saved), bf16),
        pltpu.VMEM((replicas, hidden, rows), f32),
        pltpu.VMEM((ticks, replicas, 2, own_p, rows), bf16),
        pltpu.VMEM((ticks - 1, replicas, 2, own_p, rows), bf16),
        pltpu.VMEM((replicas, saved, hidden), f32), pltpu.VMEM((replicas, saved, width_p), f32),
        pltpu.VMEM((replicas, saved, width_p), f32),
        pltpu.VMEM((replicas * saved, hidden), bf16), pltpu.VMEM((replicas * saved, width_p), bf16),
        pltpu.VMEM((replicas * saved, width_p), bf16),
        dma((16,)), dma((6,)), dma((11,)), dma((max(4, replicas - 1),)), dma((4, replicas - 1)),
        dma((replicas - 1,)), dma((ticks - 1, replicas - 1)), dma((flows,)),
        dma((replicas, terms)), dma((replicas, 4 if square else flows)), dma((replicas, flows)),
        dma((ticks - 1, replicas, 2)), dma((replicas - 1, 2)),
        pltpu.VMEM(up.shape if square else (16, 128), bf16),
    ]
    in_got, pool_t, act_t, sum_hidden, sum_grad, sum_up, out = pl.pallas_call(
        functools.partial(ticks_kernel, sections, tensors, replicas, own_p, ticks),
        out_shape=(
            shape((replicas, 2, own_p, saved), bf16),
            shape((width_p, replicas * saved), bf16),
            shape((hidden, replicas * saved), bf16),
            shape((replicas * saved, hidden), bf16),
            shape((replicas * saved, width_p), bf16),
            shape((replicas * saved, width_p), bf16),
            shape((2, replicas, own_p, rows), bf16),
        ),
        in_specs=[hbm] * 8,
        out_specs=(hbm,) * 7,
        scratch_shapes=scratch,
        compiler_params=pltpu.CompilerParams(
            collective_id=0, has_side_effects=True, vmem_limit_bytes=60 * 1024 * 1024
        ),
        name="ticks",
    )(features, pool_own, crop_ids[0], seed, loss, proj, up, down)

    def trimmed(x, axis):
        if own == own_p:
            return x
        count = x.shape[axis] // own_p
        x = x.reshape(x.shape[:axis] + (count, own_p) + x.shape[axis + 1:])
        x = lax.slice_in_dim(x, 0, own, axis=axis + 1)
        return x.reshape(x.shape[:axis] + (count * own,) + x.shape[axis + 2:])

    kept = (act_t, sum_up, pool_t, sum_hidden)
    grad_down, grad_up, grad_proj, outgoing = pl.pallas_call(
        functools.partial(tail_kernel, replicas),
        out_shape=(
            shape((hidden, width_p), bf16), shape((width_p, hidden), bf16),
            shape((2, own_p, width_p), bf16), shape(out.shape, bf16),
        ),
        in_specs=[pl.BlockSpec(memory_space=pltpu.SMEM)] + [hbm] * 8,
        out_specs=(hbm,) * 4,
        scratch_shapes=[pltpu.VMEM(x.shape, bf16) for x in kept] + [
            pltpu.VMEM((2, own_p, replicas * saved), bf16), pltpu.VMEM(sum_grad.shape, bf16),
            pltpu.VMEM(out.shape, bf16),
            pltpu.VMEM((hidden, width_p), bf16), pltpu.VMEM((width_p, hidden), bf16),
            pltpu.VMEM((2, own_p, width_p), bf16),
            dma((6 + replicas,)),
            dma((-(-hidden // 128) - (-width_p // 128) + 5,)),
        ],
        compiler_params=pltpu.CompilerParams(vmem_limit_bytes=60 * 1024 * 1024),
        name="tail",
    )(keep, *kept, features, in_got, sum_grad, out)
    grad_down = trimmed(grad_down, 1)[None]
    grad_up = trimmed(grad_up, 0)[None]
    grad_proj = trimmed(trimmed(grad_proj, 1), 2)[None]
    outgoing = trimmed(outgoing, 2).reshape(2, replicas * own, rows).transpose(2, 0, 1)
    return grad_proj, grad_up, grad_down, outgoing[None]


def solution(mesh):
    in_specs = (
        P("section", "replica", None, "tensor"),
        P("section", "replica", None),
        P("section", "replica", None),
        P("section", "replica", "tensor"),
        P(None, "replica", "tensor"),
        P("section", None, ("tensor", "replica"), None),
        P("section", None, ("tensor", "replica")),
        P("section", ("tensor", "replica"), None),
    )
    out_specs = (
        P("section", None, ("tensor", "replica"), None),
        P("section", None, ("tensor", "replica")),
        P("section", ("tensor", "replica"), None),
        P("section", "replica", None, "tensor"),
    )
    return jax.shard_map(body, mesh=mesh, in_specs=in_specs, out_specs=out_specs, check_vma=False)
```

```python
import functools
import math

import jax
import jax.numpy as jnp
from jax import lax
from jax.experimental import pallas as pl
from jax.experimental.pallas import tpu as pltpu
from jax.sharding import PartitionSpec as P

gelu_scale = 0.7978845608
gelu_cubic = 0.044715
bf16, f32 = jnp.bfloat16, jnp.float32
MESH = pl.DeviceIdType.MESH


def gelu_pair(pre_gelu):
    inner = gelu_scale * (pre_gelu + gelu_cubic * pre_gelu * pre_gelu * pre_gelu)
    tanh_part = jnp.tanh(inner)
    gelu_value = 0.5 * pre_gelu * (1.0 + tanh_part)
    gelu_slope = 0.5 * (1.0 + tanh_part) + 0.5 * pre_gelu * (
        1.0 - tanh_part * tanh_part
    ) * gelu_scale * (1.0 + 3.0 * gelu_cubic * pre_gelu * pre_gelu)
    return (gelu_value, gelu_slope)


def dot(a, b):
    return jnp.dot(a, b, preferred_element_type=f32)


def dot_nt(a, b):
    return lax.dot_general(a, b, (((1,), (1,)), ((), ())), preferred_element_type=f32)


def ticks_kernel(
    sections, tensors, replicas, own, ticks,
    inputs_hbm, pool_hbm, ids_hbm, seed_hbm, loss_hbm, proj_hbm, up_hbm, down_hbm,
    in_got, down_grad, up_grad, proj_grad, out,
    proj, up, down, loss_src, ids, loss_t, pool, pool_t, act_t,
    upstream, grads, hidden, part, relay, got, keep_part, own_part, slope_hi, slope_lo, slope,
    edge, edge_got, acc_hidden, acc_grad, acc_up, sum_hidden, sum_grad, sum_up,
    load_sem, out_sem, send_sems, pool_sems, inputs_sems, ids_sems, loss_sems,
    part_sems, grad_sems, up_sems, edge_sems, outgoing_sems, up_near, inputs,
):
    members = tensors * replicas
    square = tensors == 2 and replicas == 2 and own % 32 == 0
    half = own // 2
    section = lax.axis_index("section")
    tensor = lax.axis_index("tensor")
    replica = lax.axis_index("replica")
    me = tensor * replicas + replica
    hidden_rows = down.shape[0]
    saved = pool.shape[1]
    last = ticks - 1
    mid = sections // 2
    along = (1 - tensor) * replicas + replica
    across = tensor * replicas + (1 - replica)

    def device(s, member):
        return {
            "section": s,
            "tensor": lax.div(member, replicas),
            "replica": lax.rem(member, replicas),
        }

    def member_at(by):
        return lax.rem(me + by, members)

    def replica_at(by):
        return lax.rem(replica + by, replicas)

    def slab_of(member):
        return pl.ds(pl.multiple_of(member * own, 16), own)

    loads = []

    def load(src, dst):
        copy = pltpu.make_async_copy(src, dst, load_sem.at[len(loads)])
        copy.start()
        loads.append(copy)
        return copy

    near_order = {1: ((0, 0), (1, 0), (0, 1), (1, 1)), 0: ((0, 0), (0, 1), (1, 0), (1, 1))}

    def term(k, p, side):
        if k == 0:
            member = lax.rem(tensor + side, tensors) * replicas + p
        else:
            member = p * replicas + lax.rem(replica + side, replicas)
        return pl.ds(pl.multiple_of(member * own + k * half, 16), half)

    wide = pl.ds(pl.multiple_of(tensor * (replicas * own), 16), replicas * own)
    ld_pool = load(pool_hbm, pool.at[replica])
    ld_seed = load(seed_hbm, upstream.at[0, replica, wide])
    ld_ids = load(ids_hbm, ids.at[replica])
    ld_up = load(up_hbm, up)
    ld_down = load(down_hbm, down)
    if square:
        order = [term(k, p, side) for side in (1, 0) for k, p in near_order[side]]
        for i, rows in enumerate(order):
            pltpu.make_async_copy(up_hbm.at[rows], up_near.at[pl.ds(i * half, half)], out_sem.at[0]).start()
    ld_loss = load(loss_hbm, loss_src)
    ld_loss_own = load(loss_hbm.at[:, replica], loss_t.at[replica])
    ld_proj = load(proj_hbm, proj)

    barrier = pltpu.get_barrier_semaphore()
    above = lax.rem(section + 1, sections)
    below = lax.rem(section + sections - 1, sections)
    mirror = sections - 1 - section
    for by in range(1, members):
        pl.semaphore_signal(barrier, 1, device_id=device(section, member_at(by)), device_id_type=MESH)
    for other in (above, below, mirror):
        pl.semaphore_signal(barrier, 1, device_id=device(other, me), device_id_type=MESH)
    pl.semaphore_wait(barrier, members - 1 + 3)

    POOL, IDS, SEED, PART, GRAD, UP, INPUTS, DOWN, SKIP, LOSS, OUT = range(11)

    def remote(src, dst, kind, recv_sem, s, member):
        return pltpu.make_async_remote_copy(
            src_ref=src, dst_ref=dst, send_sem=send_sems.at[kind], recv_sem=recv_sem,
            device_id=device(s, member), device_id_type=MESH,
        )

    def send(src, dst, kind, recv_sem, member):
        copy = remote(src, dst, kind, recv_sem, section, member)
        copy.start()
        return copy

    def over_replicas(src_of, dst, kind, sems):
        return [
            send(src_of(replica_at(by)), dst, kind, sems.at[by - 1], tensor * replicas + replica_at(by))
            for by in range(1, replicas)
        ]

    def all_sent(kind, ref):
        pltpu.make_async_copy(ref, ref, send_sems.at[kind]).wait()

    def lanes(r):
        return inputs.at[:, :, pl.ds(pl.multiple_of(r * saved, 128), saved)]

    chunk = 128
    down_steps = [(start, min(chunk, hidden_rows - start)) for start in range(0, hidden_rows, chunk)]
    up_steps = [(start, min(chunk, up_grad.shape[0] - start)) for start in range(0, up_grad.shape[0], chunk)]

    def fill(count):
        for _ in range(count):
            if down_steps:
                start, size = down_steps.pop(0)
                down_grad[pl.ds(start, size), :] = dot(act_t[pl.ds(start, size), :], sum_up[...]).astype(bf16)
            elif up_steps:
                start, size = up_steps.pop(0)
                up_grad[pl.ds(start, size), :] = dot(pool_t[pl.ds(start, size), :], sum_hidden[...]).astype(bf16)

    class Gather:
        def __init__(self, at, whole, kind, sems):
            self.at, self.kind, self.sems = at, kind, sems
            if square:
                self.copies = [self.put(me, 0, 0, along), self.put(me, 1, 1, across)]
            else:
                self.copies = [
                    send(whole, whole, kind, sems.at[by - 1], member_at(by))
                    for by in range(1, members)
                ]

        def put(self, member, h, i, to):
            ref = self.at(member, h)
            return send(ref, ref, self.kind, self.sems.at[i], to)

        def follow(self):
            if square:
                self.copies += [self.put(me, 1, 2, along), self.put(me, 0, 3, across)]

        def forward(self):
            if square:
                self.copies[0].wait_recv()
                self.copies.append(self.put(along, 0, 4, across))
                self.copies[1].wait_recv()
                self.copies.append(self.put(across, 1, 5, along))

        def finish(self):
            for copy in self.copies[2 if square else 0:]:
                copy.wait_recv()

    def halves_of(ref):
        return lambda member, h: ref.at[pl.ds(pl.multiple_of(member * own + h * half, 16), half)]

    def seed_at(member, h):
        return upstream.at[0, lax.rem(member, replicas),
                           pl.ds(pl.multiple_of(lax.div(member, replicas) * (replicas * own) + h * own, 16), own)]

    slab = slab_of(me)
    low, high = pl.ds(0, half), pl.ds(half, half)
    ld_pool.wait()
    pieces = 2
    if square:
        rows = saved // (2 * pieces)

        def piece(r, p):
            return pool.at[r, pl.ds(pl.multiple_of((tensor * pieces + p) * rows, 8), rows)]

        pool_in = [
            send(piece(replica, p), piece(replica, p), POOL, pool_sems.at[p], across)
            for p in range(pieces)
        ]
    else:
        pool_in = over_replicas(lambda r: pool.at[replica], pool.at[replica], POOL, pool_sems)
    ld_seed.wait()
    seed_in = Gather(seed_at, upstream.at[0, replica, wide], SEED, up_sems.at[0])
    seed_in.follow()
    ld_ids.wait()
    ids_in = over_replicas(lambda r: ids.at[replica], ids.at[replica], IDS, ids_sems)
    is_top = section == sections - 1

    step = 256 if hidden_rows % 256 == 0 else 128

    def pre_slopes(r):
        def pre_at(start, size):
            cols = pl.ds(start, size)
            value, gelu_slope = gelu_pair(dot(pool[r], up[:, cols]).T)
            act_t[cols, pl.ds(pl.multiple_of(r * saved, 128), saved)] = value.astype(bf16)
            high = gelu_slope.astype(bf16)
            slope_hi[r, cols, :] = high
            slope_lo[r, cols, :] = (gelu_slope - high.astype(f32)).astype(bf16)

        @pl.loop(0, hidden_rows // step)
        def _(c):
            pre_at(pl.multiple_of(c * step, step), step)

        if hidden_rows % step:
            pre_at(hidden_rows - hidden_rows % step, hidden_rows % step)

    def picks(t, r):
        row = ids[r, pl.ds(t, 1), :]
        place_of = lax.broadcasted_iota(jnp.int32, (saved, row.shape[1]), 0)
        return jnp.where(place_of == row, 1.0, 0.0).astype(bf16)

    def pick_slope(t, r):
        chosen = picks(t, r)
        slope[r] = dot(slope_hi[r], chosen) + dot(slope_lo[r], chosen)

    ld_up.wait()
    pre_slopes(replica)
    pick_slope(0, replica)
    if square:
        pool_over = []
        for p in range(pieces):
            pool_in[p].wait_recv()
            come = piece(1 - replica, p)
            pool_over.append(send(come, come, POOL, pool_sems.at[pieces + p], along))
        seed_in.forward()
        for copy in pool_over:
            copy.wait_recv()
        pre_slopes(1 - replica)
    else:
        for by in range(1, replicas):
            pool_in[by - 1].wait_recv()
            pre_slopes(lax.rem(replica + replicas - by, replicas))
    for copy in ids_in:
        copy.wait_recv()
    for by in range(1, replicas):
        pick_slope(0, lax.rem(replica + by, replicas))

    ld_down.wait()
    if square:
        pltpu.make_async_copy(up_hbm, up_near, out_sem.at[0]).wait()
    seed_in.finish()

    up_in, part_in, grad_in, edge_in = {}, {}, {}, {}

    def stage_hidden(t, r):
        if t > 0:
            up_in[t, r].finish()
        hidden[t, r] = (dot(down[...], upstream[t, r]) * slope[r]).astype(bf16)
        if square:
            part[t, r, 0] = dot(up_near[:own, :], hidden[t, r]).astype(bf16)
            part_in[t, r] = put_terms(t, r, 0)

    def put_terms(t, r, p):
        return [
            send(part.at[t, r, p, rows], relay.at[t, r, 0, k, p], PART, part_sems.at[r, 2 * p + k], to)
            for k, (to, rows) in enumerate(((along, low), (across, high)))
        ]

    def stage_parts(t, r):
        if square:
            near_terms = dot(up_near[own:, :], hidden[t, r])
            part[t, r, 1] = near_terms[:own].astype(bf16)
            part_in[t, r] += put_terms(t, r, 1)
            for k in range(2):
                for p in range(2):
                    start = own + (2 * k + p) * half
                    keep_part[r, k, p] = near_terms[start:start + half]
            return
        part_in[t, r] = []
        for by in range(1, members):
            to = member_at(by)
            part[t, r, by - 1] = dot(up[slab_of(to), :], hidden[t, r]).astype(bf16)
            part_in[t, r].append(send(part.at[t, r, by - 1], got.at[t, r, by - 1], PART,
                                      part_sems.at[r, by - 1], to))
        own_part[r] = dot(up[slab, :], hidden[t, r]) + upstream[t, r, slab, :].astype(f32)

    def stage_relay(t, r):
        if square:
            for p in range(2):
                for k, to in enumerate((across, along)):
                    part_in[t, r][2 * p + k].wait_recv()
                    total = keep_part[r, k, p] + relay[t, r, 0, k, p].astype(f32)
                    relay[t, r, 1, k, p] = total.astype(bf16)
                    part_in[t, r].append(send(relay.at[t, r, 1, k, p], relay.at[t, r, 2, k, p], PART,
                                              part_sems.at[r, 4 + 2 * p + k], to))

    def stage_sum(t, r):
        if square:
            grad_in[t, r] = []
            for p in range(2):
                for k, to in enumerate((along, across)):
                    part_in[t, r][4 + 2 * p + k].wait_recv()
                    rows = term(k, p, 0)
                    total = relay[t, r, 1, k, p].astype(f32) + relay[t, r, 2, k, p].astype(f32)
                    grads[t, r, rows, :] = (total + upstream[t, r, rows, :].astype(f32)).astype(bf16)
                    mine = grads.at[t, r, rows]
                    grad_in[t, r].append(send(mine, mine, GRAD, grad_sems.at[r, 2 * p + k], to))
            return
        for copy in part_in[t, r]:
            copy.wait_recv()
        total = own_part[r]
        for k in range(got.shape[2]):
            total = total + got[t, r, k].astype(f32)
        grads[t, r, slab, :] = total.astype(bf16)
        grad_in[t, r] = Gather(halves_of(grads.at[t, r]), grads.at[t, r, slab], GRAD, grad_sems.at[r]).copies

    def have_grads(t, r):
        for copy in grad_in[t, r]:
            copy.wait_recv()

    def stage_project(t, r):
        have_grads(t, r)
        edge[t, r, 0] = dot(proj[0], grads[t, r]).astype(bf16)
        if t == last:
            return
        down_copy = remote(edge.at[t, r, 0], edge_got.at[t, r, 0], DOWN, edge_sems.at[t, r, 0], below, me)
        pl.when((section > 0) & (section != mid))(down_copy.start)
        skip = remote(edge.at[t, r, 1], edge_got.at[t, r, 1], SKIP, edge_sems.at[t, r, 1], mirror, me)

        @pl.when(section > mid)
        def _():
            edge[t, r, 1] = dot(proj[1], grads[t, r]).astype(bf16)
            skip.start()

        @pl.when(section == mid)
        def _():
            second = dot(proj[1], grads[t, r]).astype(bf16)
            edge[t, r, 0] = (edge[t, r, 0].astype(f32) + second.astype(f32)).astype(bf16)
            down_copy.start()

        edge_in[t, r] = (down_copy, skip)

    def stage_next(t, r):
        down_copy, skip = edge_in[t, r]

        @pl.when(section < mid - 1)
        def _():
            down_copy.wait_recv()
            skip.wait_recv()
            summed = edge_got[t, r, 0].astype(f32) + edge_got[t, r, 1].astype(f32)
            upstream[t + 1, r, slab, :] = summed.astype(bf16)

        @pl.when((section >= mid - 1) & (section < sections - 1))
        def _():
            down_copy.wait_recv()
            upstream[t + 1, r, slab, :] = edge_got[t, r, 0]

        @pl.when(is_top)
        def _():
            if r == 0:
                for copy in loss_in[t]:
                    copy.wait_recv()
            upstream[t + 1, r, slab, :] = loss_t[r, t]

        up_in[t + 1, r] = Gather(halves_of(upstream.at[t + 1, r]), upstream.at[t + 1, r, slab], UP, up_sems.at[r])

    def add(t, r, acc, total, term):
        rows = pl.ds(r * saved, saved)
        value = term if t == 0 else acc[r] + term
        if t == last:
            total[rows, :] = value.astype(bf16)
        else:
            acc[r] = value

    def settle(t, r):
        chosen = picks(t, r)
        add(t, r, acc_hidden, sum_hidden, dot_nt(chosen, hidden[t, r]))
        add(t, r, acc_up, sum_up, dot_nt(chosen, upstream[t, r]))

    def give_loss(t):
        if t == 0:
            ld_loss.wait()
            ld_loss_own.wait()
        loss_in.append([
            remote(loss_src.at[t, replica_at(by)], loss_t.at[replica, t], LOSS,
                   loss_sems.at[t, by - 1], section, tensor * replicas + replica_at(by))
            for by in range(1, replicas)
        ])
        for copy in loss_in[t]:
            pl.when(is_top)(copy.start)

    def give_inputs(t):
        if t in (0, last):
            for copy in inputs_in:
                pl.when(section < mid if t == 0 else section >= mid)(copy.start)

    outs = [
        [
            remote(edge.at[last, replica_at(by), k], out.at[k, replica], OUT,
                   outgoing_sems.at[by - 1, k], section, tensor * replicas + replica_at(by))
            for k in range(2)
        ]
        for by in range(1, replicas)
    ]

    def stage_outgoing(r):
        have_grads(last, r)
        for k in range(2):
            edge[last, r, k] = dot(proj[k], grads[last, r]).astype(bf16)
            for by in range(1, replicas):
                pl.when(replica_at(by) == r)(outs[by - 1][k].start)
        add(last, r, acc_grad, sum_grad, dot_nt(picks(last, r), grads[last, r]))

    every = range(replicas)
    end = replicas - 1
    loss_in, gathered = [], []
    inputs_in = [
        remote(inputs_hbm.at[k, replica_at(by), rows], in_got.at[replica, k, rows], INPUTS,
               inputs_sems.at[2 * k + h, by - 1], section, tensor * replicas + replica_at(by))
        for by in range(1, replicas)
        for k in range(2)
        for h, rows in enumerate((low, pl.ds(half, own - half)))
    ]
    for t in range(ticks):
        project = stage_project if t < last else lambda t, r: stage_outgoing(r)
        for r in every:
            stage_hidden(t, r)
            stage_parts(t, r)
        if t < last:
            give_loss(t)
        for r in every:
            stage_relay(t, r)
            if r == 0:
                settle(t, r)
        for r in every:
            stage_sum(t, r)
            if r < end:
                settle(t, r + 1)
        if t < last:
            for r in every:
                pick_slope(t + 1, r)
        else:
            fill(10)
        if t == 0:
            for r in every:
                pool_t[:, pl.ds(r * saved, saved)] = pool[r].T
            ld_proj.wait()
        give_inputs(t)
        for r in every:
            project(t, r)
            if t == last and r < end:
                fill(2)
        if t == last:
            break
        for r in every:
            stage_next(t, r)
            if r == 0:
                up_in[t + 1, r].follow()
        for r in every:
            add(t, r, acc_grad, sum_grad, dot_nt(picks(t, r), grads[t, r]))
            up_in[t + 1, r].forward()
            if r < end:
                up_in[t + 1, r + 1].follow()

    for copy in inputs_in:
        copy.wait_recv()
    for by in range(replicas):
        r = replica_at(by)
        src = inputs_hbm.at[:, r] if by == 0 else in_got.at[r]
        gathered.append(pltpu.make_async_copy(src, lanes(r), out_sem.at[1 + by]))
        gathered[by].start()
    place = pltpu.make_async_copy(edge.at[last, replica], out.at[:, replica], out_sem.at[0])
    place.start()
    fill(len(down_steps) + len(up_steps))
    for copy in gathered:
        copy.wait()
    keep = jnp.where(section < sections // 2, 0.0, 1.0).astype(f32)
    for k in range(2):
        for start, size in ((0, half), (half, own - half)):
            total = dot(inputs[k, pl.ds(start, size), :], sum_grad[...])
            proj_grad[k, pl.ds(start, size), :] = (total * keep if k else total).astype(bf16)
    place.wait()
    for pair in outs:
        for copy in pair:
            copy.wait_recv()
    all_sent(POOL, pool.at[pl.ds(0, replicas - 1)])
    all_sent(IDS, ids.at[pl.ds(0, replicas - 1)])
    others = pl.ds(0, (members - 1) * own)
    all_sent(SEED, upstream.at[0, :, others])
    all_sent(PART, upstream if square else part)
    all_sent(GRAD, upstream.at[:, :, pl.ds(0, 2 * own)] if square else part)
    all_sent(UP, upstream.at[pl.ds(0, last), :, others])
    all_sent(INPUTS, in_got.at[pl.ds(0, replicas - 1)])
    all_sent(OUT, edge.at[last, pl.ds(0, replicas - 1)])
    pl.when(section > 0)(lambda: all_sent(DOWN, edge_got.at[:, :, 0]))
    pl.when(section > mid)(lambda: all_sent(SKIP, edge_got.at[:, :, 1]))
    pl.when(is_top)(lambda: all_sent(LOSS, loss_t.at[pl.ds(0, replicas - 1)]))


def tail_kernel(*refs):
    pairs, sems = list(zip(refs[:4], refs[4:8])), refs[8]
    copies = [pltpu.make_async_copy(src, dst, sems.at[i]) for i, (src, dst) in enumerate(pairs)]
    for copy in copies:
        copy.start()
    for copy in copies:
        copy.wait()


def body(pool_inputs, pool_mixed, crop_ids, incoming, loss_grads, w_proj, w_up, w_down):
    sections = lax.axis_size("section")
    tensors, replicas = lax.axis_size("tensor"), lax.axis_size("replica")
    members = tensors * replicas
    own = w_proj.shape[2]
    own_p = -(-own // 16) * 16
    rows, width = incoming.shape[1], w_up.shape[1]
    width_p = members * own_p
    hidden = w_up.shape[2]
    ticks = crop_ids.shape[1]
    saved = pool_mixed.shape[1]

    def padded(x, axis):
        if own == own_p:
            return x
        count = x.shape[axis] // own
        shape = x.shape[:axis] + (count, own) + x.shape[axis + 1:]
        fill = [(0, 0)] * (x.ndim + 1)
        fill[axis + 1] = (0, own_p - own)
        shape_p = x.shape[:axis] + (count * own_p,) + x.shape[axis + 1:]
        return jnp.pad(x.reshape(shape), fill).reshape(shape_p)

    proj = padded(padded(w_proj[0], 1), 2)
    up, down = padded(w_up[0], 0), padded(w_down[0], 1)
    pool_own = padded(pool_mixed[0], 1)
    features = pool_inputs[0].transpose(1, 2, 0).reshape(2, replicas, own, saved)
    features = padded(features, 2)
    seed = padded(incoming[0].T, 0)
    loss = loss_grads.transpose(0, 2, 1).reshape(ticks - 1, replicas, own, rows)
    loss = padded(loss, 2)

    shape = jax.ShapeDtypeStruct
    vmem = pl.BlockSpec(memory_space=pltpu.VMEM)
    hbm = pl.BlockSpec(memory_space=pl.ANY)
    dma = pltpu.SemaphoreType.DMA
    square = tensors == 2 and replicas == 2 and own_p % 32 == 0
    flows = 6 if square else members - 1
    terms = 8 if square else members - 1
    scratch = [
        pltpu.VMEM(proj.shape, bf16), pltpu.VMEM(up.shape, bf16), pltpu.VMEM(down.shape, bf16),
        pltpu.VMEM(loss.shape, bf16), pltpu.VMEM((replicas,) + crop_ids.shape[1:], jnp.int32),
        pltpu.VMEM((replicas, ticks - 1, own_p, rows), bf16),
        pltpu.VMEM((replicas, saved, width_p), bf16), pltpu.VMEM((width_p, replicas * saved), bf16),
        pltpu.VMEM((hidden, replicas * saved), bf16),
        pltpu.VMEM((ticks, replicas, width_p, rows), bf16),
        pltpu.VMEM((ticks, replicas, width_p, rows), bf16),
        pltpu.VMEM((ticks, replicas, hidden, rows), bf16),
        pltpu.VMEM((ticks, replicas, 2 if square else members - 1, own_p, rows), bf16),
        pltpu.VMEM((ticks, replicas, 3, 2, 2, own_p // 2, rows) if square else (16, 128), bf16),
        pltpu.VMEM((16, 128) if square else (ticks, replicas, members - 1, own_p, rows), bf16),
        pltpu.VMEM((replicas, 2, 2, own_p // 2, rows) if square else (8, 128), f32),
        pltpu.VMEM((replicas, own_p, rows), f32),
        pltpu.VMEM((replicas, hidden, saved), bf16), pltpu.VMEM((replicas, hidden, saved), bf16),
        pltpu.VMEM((replicas, hidden, rows), f32),
        pltpu.VMEM((ticks, replicas, 2, own_p, rows), bf16),
        pltpu.VMEM((ticks - 1, replicas, 2, own_p, rows), bf16),
        pltpu.VMEM((replicas, saved, hidden), f32), pltpu.VMEM((replicas, saved, width_p), f32),
        pltpu.VMEM((replicas, saved, width_p), f32),
        pltpu.VMEM((replicas * saved, hidden), bf16), pltpu.VMEM((replicas * saved, width_p), bf16),
        pltpu.VMEM((replicas * saved, width_p), bf16),
        dma((8,)), dma((1 + replicas,)), dma((11,)), dma((max(4, replicas - 1),)), dma((4, replicas - 1)),
        dma((replicas - 1,)), dma((ticks - 1, replicas - 1)),
        dma((replicas, terms)), dma((replicas, 4 if square else flows)), dma((replicas, flows)),
        dma((ticks - 1, replicas, 2)), dma((replicas - 1, 2)),
        pltpu.VMEM(up.shape if square else (16, 128), bf16),
        pltpu.VMEM((2, own_p, replicas * saved), bf16),
    ]

    kept_shapes = ((hidden, width_p), (width_p, hidden), (2, own_p, width_p), (2, replicas, own_p, rows))
    vmem_limit = 66_800_000 - sum(2 * math.prod(dims) for dims in kept_shapes)
    _, *kept = pl.pallas_call(
        functools.partial(ticks_kernel, sections, tensors, replicas, own_p, ticks),
        out_shape=(
            shape((replicas, 2, own_p, saved), bf16),
            *(pltpu.VMEM(dims, bf16) for dims in kept_shapes),
        ),
        in_specs=[hbm] * 8,
        out_specs=(hbm,) + (vmem,) * 4,
        scratch_shapes=scratch,
        compiler_params=pltpu.CompilerParams(
            collective_id=0, has_side_effects=True, vmem_limit_bytes=vmem_limit
        ),
        name="ticks",
    )(features, pool_own, crop_ids[0], seed, loss, proj, up, down)

    def trimmed(x, axis):
        if own == own_p:
            return x
        count = x.shape[axis] // own_p
        x = x.reshape(x.shape[:axis] + (count, own_p) + x.shape[axis + 1:])
        x = lax.slice_in_dim(x, 0, own, axis=axis + 1)
        return x.reshape(x.shape[:axis] + (count * own,) + x.shape[axis + 2:])

    grad_down, grad_up, grad_proj, outgoing = pl.pallas_call(
        tail_kernel,
        out_shape=tuple(shape(dims, bf16) for dims in kept_shapes),
        in_specs=[vmem] * 4,
        out_specs=(hbm,) * 4,
        scratch_shapes=[dma((4,))],
        compiler_params=pltpu.CompilerParams(vmem_limit_bytes=128 * 1024),
        name="tail",
    )(*kept)
    grad_down = trimmed(grad_down, 1)[None]
    grad_up = trimmed(grad_up, 0)[None]
    grad_proj = trimmed(trimmed(grad_proj, 1), 2)[None]
    outgoing = trimmed(outgoing, 2).reshape(2, replicas * own, rows).transpose(2, 0, 1)
    return grad_proj, grad_up, grad_down, outgoing[None]


def solution(mesh):
    in_specs = (
        P("section", "replica", None, "tensor"),
        P("section", "replica", None),
        P("section", "replica", None),
        P("section", "replica", "tensor"),
        P(None, "replica", "tensor"),
        P("section", None, ("tensor", "replica"), None),
        P("section", None, ("tensor", "replica")),
        P("section", ("tensor", "replica"), None),
    )
    out_specs = (
        P("section", None, ("tensor", "replica"), None),
        P("section", None, ("tensor", "replica")),
        P("section", ("tensor", "replica"), None),
        P("section", "replica", None, "tensor"),
    )
    return jax.shard_map(body, mesh=mesh, in_specs=in_specs, out_specs=out_specs, check_vma=False)
```

```python
import functools
import math

import jax
import jax.numpy as jnp
from jax import lax
from jax.experimental import pallas as pl
from jax.experimental.pallas import tpu as pltpu
from jax.sharding import PartitionSpec as P

gelu_scale = 0.7978845608
gelu_cubic = 0.044715
bf16, f32 = jnp.bfloat16, jnp.float32
MESH = pl.DeviceIdType.MESH


def gelu_pair(pre_gelu):
    inner = gelu_scale * (pre_gelu + gelu_cubic * pre_gelu * pre_gelu * pre_gelu)
    tanh_part = jnp.tanh(inner)
    gelu_value = 0.5 * pre_gelu * (1.0 + tanh_part)
    gelu_slope = 0.5 * (1.0 + tanh_part) + 0.5 * pre_gelu * (
        1.0 - tanh_part * tanh_part
    ) * gelu_scale * (1.0 + 3.0 * gelu_cubic * pre_gelu * pre_gelu)
    return (gelu_value, gelu_slope)


def dot(a, b):
    return jnp.dot(a, b, preferred_element_type=f32)


def dot_nt(a, b):
    return lax.dot_general(a, b, (((1,), (1,)), ((), ())), preferred_element_type=f32)


def ticks_kernel(
    sections, tensors, replicas, own, ticks,
    inputs_hbm, pool_hbm, ids_hbm, seed_hbm, loss_hbm, proj_hbm, up_hbm, down_hbm,
    in_got, down_grad, up_grad, proj_grad, out,
    proj, up, down, loss_src, ids, loss_t, pool, pool_t, act_t,
    upstream, grads, hidden, part, relay, got, keep_part, own_part, slope_hi, slope_lo, slope,
    edge, edge_got, acc_hidden, acc_grad, acc_up, sum_hidden, sum_grad, sum_up,
    load_sem, out_sem, send_sems, pool_sems, inputs_sems, ids_sems, loss_sems,
    part_sems, grad_sems, up_sems, edge_sems, outgoing_sems, up_near, inputs,
):
    members = tensors * replicas
    square = tensors == 2 and replicas == 2 and own % 32 == 0
    half = own // 2
    section = lax.axis_index("section")
    tensor = lax.axis_index("tensor")
    replica = lax.axis_index("replica")
    me = tensor * replicas + replica
    hidden_rows = down.shape[0]
    saved = pool.shape[1]
    last = ticks - 1
    mid = sections // 2
    along = (1 - tensor) * replicas + replica
    across = tensor * replicas + (1 - replica)

    def device(s, member):
        return {
            "section": s,
            "tensor": lax.div(member, replicas),
            "replica": lax.rem(member, replicas),
        }

    def member_at(by):
        return lax.rem(me + by, members)

    def replica_at(by):
        return lax.rem(replica + by, replicas)

    def slab_of(member):
        return pl.ds(pl.multiple_of(member * own, 16), own)

    loads = []

    def load(src, dst):
        copy = pltpu.make_async_copy(src, dst, load_sem.at[len(loads)])
        copy.start()
        loads.append(copy)
        return copy

    near_order = {1: ((0, 0), (1, 0), (0, 1), (1, 1)), 0: ((0, 0), (0, 1), (1, 0), (1, 1))}

    def term(k, p, side):
        if k == 0:
            member = lax.rem(tensor + side, tensors) * replicas + p
        else:
            member = p * replicas + lax.rem(replica + side, replicas)
        return pl.ds(pl.multiple_of(member * own + k * half, 16), half)

    wide = pl.ds(pl.multiple_of(tensor * (replicas * own), 16), replicas * own)
    ld_pool = load(pool_hbm, pool.at[replica])
    ld_seed = load(seed_hbm, upstream.at[0, replica, wide])
    ld_ids = load(ids_hbm, ids.at[replica])
    ld_up = load(up_hbm, up)
    ld_down = load(down_hbm, down)
    if square:
        order = [term(k, p, side) for side in (1, 0) for k, p in near_order[side]]
        for i, rows in enumerate(order):
            pltpu.make_async_copy(up_hbm.at[rows], up_near.at[pl.ds(i * half, half)], out_sem.at[0]).start()
    ld_loss = load(loss_hbm, loss_src)
    ld_loss_own = load(loss_hbm.at[:, replica], loss_t.at[replica])
    ld_proj = load(proj_hbm, proj)

    barrier = pltpu.get_barrier_semaphore()
    above = lax.rem(section + 1, sections)
    below = lax.rem(section + sections - 1, sections)
    mirror = sections - 1 - section
    for by in range(1, members):
        pl.semaphore_signal(barrier, 1, device_id=device(section, member_at(by)), device_id_type=MESH)
    for other in (above, below, mirror):
        pl.semaphore_signal(barrier, 1, device_id=device(other, me), device_id_type=MESH)
    pl.semaphore_wait(barrier, members - 1 + 3)

    POOL, IDS, SEED, PART, GRAD, UP, INPUTS, DOWN, SKIP, LOSS, OUT = range(11)

    def remote(src, dst, kind, recv_sem, s, member):
        return pltpu.make_async_remote_copy(
            src_ref=src, dst_ref=dst, send_sem=send_sems.at[kind], recv_sem=recv_sem,
            device_id=device(s, member), device_id_type=MESH,
        )

    def send(src, dst, kind, recv_sem, member):
        copy = remote(src, dst, kind, recv_sem, section, member)
        copy.start()
        return copy

    def over_replicas(src_of, dst, kind, sems):
        return [
            send(src_of(replica_at(by)), dst, kind, sems.at[by - 1], tensor * replicas + replica_at(by))
            for by in range(1, replicas)
        ]

    def all_sent(kind, ref):
        pltpu.make_async_copy(ref, ref, send_sems.at[kind]).wait()

    def lanes(r):
        return inputs.at[:, :, pl.ds(pl.multiple_of(r * saved, 128), saved)]

    chunk = 128
    down_steps = [(start, min(chunk, hidden_rows - start)) for start in range(0, hidden_rows, chunk)]
    up_steps = [(start, min(chunk, up_grad.shape[0] - start)) for start in range(0, up_grad.shape[0], chunk)]

    def fill(count):
        for _ in range(count):
            if down_steps:
                start, size = down_steps.pop(0)
                down_grad[pl.ds(start, size), :] = dot(act_t[pl.ds(start, size), :], sum_up[...]).astype(bf16)
            elif up_steps:
                start, size = up_steps.pop(0)
                up_grad[pl.ds(start, size), :] = dot(pool_t[pl.ds(start, size), :], sum_hidden[...]).astype(bf16)

    class Gather:
        def __init__(self, at, whole, kind, sems):
            if square:
                flows = ((me, 0, along), (me, 1, across), (me, 1, along), (me, 0, across),
                         (along, 0, across), (across, 1, along))
                self.copies = [
                    remote(at(member, h), at(member, h), kind, sems.at[i], section, to)
                    for i, (member, h, to) in enumerate(flows)
                ]
            else:
                self.copies = [
                    remote(whole, whole, kind, sems.at[by - 1], section, member_at(by))
                    for by in range(1, members)
                ]

        def lead(self):
            for copy in self.copies[:2 if square else None]:
                copy.start()

        def follow(self):
            if square:
                self.copies[2].start()
                self.copies[3].start()

        def forward(self):
            if square:
                for i in range(2):
                    self.copies[i].wait_recv()
                    self.copies[4 + i].start()

        def finish(self):
            for copy in self.copies[2 if square else 0:]:
                copy.wait_recv()

    def halves_of(ref):
        return lambda member, h: ref.at[pl.ds(pl.multiple_of(member * own + h * half, 16), half)]

    def seed_at(member, h):
        return upstream.at[0, lax.rem(member, replicas),
                           pl.ds(pl.multiple_of(lax.div(member, replicas) * (replicas * own) + h * own, 16), own)]

    slab = slab_of(me)
    low, high = pl.ds(0, half), pl.ds(half, half)
    ld_pool.wait()
    pieces = 2
    if square:
        rows = saved // (2 * pieces)

        def piece(r, p):
            return pool.at[r, pl.ds(pl.multiple_of((tensor * pieces + p) * rows, 8), rows)]

        pool_in = [
            send(piece(replica, p), piece(replica, p), POOL, pool_sems.at[p], across)
            for p in range(pieces)
        ]
    else:
        pool_in = over_replicas(lambda r: pool.at[replica], pool.at[replica], POOL, pool_sems)
    ld_seed.wait()
    seed_in = Gather(seed_at, upstream.at[0, replica, wide], SEED, up_sems.at[0])
    seed_in.lead()
    seed_in.follow()
    ld_ids.wait()
    ids_in = over_replicas(lambda r: ids.at[replica], ids.at[replica], IDS, ids_sems)
    is_top = section == sections - 1

    step = 256 if hidden_rows % 256 == 0 else 128

    def pre_slopes(r):
        def pre_at(start, size):
            cols = pl.ds(start, size)
            value, gelu_slope = gelu_pair(dot(pool[r], up[:, cols]).T)
            act_t[cols, pl.ds(pl.multiple_of(r * saved, 128), saved)] = value.astype(bf16)
            high = gelu_slope.astype(bf16)
            slope_hi[r, cols, :] = high
            slope_lo[r, cols, :] = (gelu_slope - high.astype(f32)).astype(bf16)

        @pl.loop(0, hidden_rows // step)
        def _(c):
            pre_at(pl.multiple_of(c * step, step), step)

        if hidden_rows % step:
            pre_at(hidden_rows - hidden_rows % step, hidden_rows % step)

    def picks(t, r):
        row = ids[r, pl.ds(t, 1), :]
        place_of = lax.broadcasted_iota(jnp.int32, (saved, row.shape[1]), 0)
        return jnp.where(place_of == row, 1.0, 0.0).astype(bf16)

    def pick_slope(t, r):
        chosen = picks(t, r)
        slope[r] = dot(slope_hi[r], chosen) + dot(slope_lo[r], chosen)

    ld_up.wait()
    pre_slopes(replica)
    pick_slope(0, replica)
    if square:
        pool_over = []
        for p in range(pieces):
            pool_in[p].wait_recv()
            come = piece(1 - replica, p)
            pool_over.append(send(come, come, POOL, pool_sems.at[pieces + p], along))
        seed_in.forward()
        for copy in pool_over:
            copy.wait_recv()
        pre_slopes(1 - replica)
    else:
        for by in range(1, replicas):
            pool_in[by - 1].wait_recv()
            pre_slopes(lax.rem(replica + replicas - by, replicas))
    for copy in ids_in:
        copy.wait_recv()
    for by in range(1, replicas):
        pick_slope(0, lax.rem(replica + by, replicas))

    ld_down.wait()
    if square:
        pltpu.make_async_copy(up_hbm, up_near, out_sem.at[0]).wait()
    seed_in.finish()

    up_in, part_in, grad_in, edge_in = {}, {}, {}, {}

    def stage_hidden(t, r):
        if t > 0:
            up_in[t, r].finish()
        hidden[t, r] = (dot(down[...], upstream[t, r]) * slope[r]).astype(bf16)
        if square:
            part[t, r, 0] = dot(up_near[:own, :], hidden[t, r]).astype(bf16)
            part_in[t, r] = put_terms(t, r, 0)

    def put_terms(t, r, p):
        return [
            send(part.at[t, r, p, rows], relay.at[t, r, 0, k, p], PART, part_sems.at[r, 2 * p + k], to)
            for k, (to, rows) in enumerate(((along, low), (across, high)))
        ]

    def stage_parts(t, r):
        if square:
            near_terms = dot(up_near[own:, :], hidden[t, r])
            part[t, r, 1] = near_terms[:own].astype(bf16)
            part_in[t, r] += put_terms(t, r, 1)
            for k in range(2):
                for p in range(2):
                    start = own + (2 * k + p) * half
                    keep_part[r, k, p] = near_terms[start:start + half]
            return
        part_in[t, r] = []
        for by in range(1, members):
            to = member_at(by)
            part[t, r, by - 1] = dot(up[slab_of(to), :], hidden[t, r]).astype(bf16)
            part_in[t, r].append(send(part.at[t, r, by - 1], got.at[t, r, by - 1], PART,
                                      part_sems.at[r, by - 1], to))
        own_part[r] = dot(up[slab, :], hidden[t, r]) + upstream[t, r, slab, :].astype(f32)

    def stage_relay(t, r):
        if square:
            for p in range(2):
                for k, to in enumerate((across, along)):
                    part_in[t, r][2 * p + k].wait_recv()
                    total = keep_part[r, k, p] + relay[t, r, 0, k, p].astype(f32)
                    relay[t, r, 1, k, p] = total.astype(bf16)
                    part_in[t, r].append(send(relay.at[t, r, 1, k, p], relay.at[t, r, 2, k, p], PART,
                                              part_sems.at[r, 4 + 2 * p + k], to))

    def stage_sum(t, r):
        if square:
            grad_in[t, r] = []
            for p in range(2):
                for k, to in enumerate((along, across)):
                    part_in[t, r][4 + 2 * p + k].wait_recv()
                    rows = term(k, p, 0)
                    total = relay[t, r, 1, k, p].astype(f32) + relay[t, r, 2, k, p].astype(f32)
                    grads[t, r, rows, :] = (total + upstream[t, r, rows, :].astype(f32)).astype(bf16)
                    mine = grads.at[t, r, rows]
                    grad_in[t, r].append(send(mine, mine, GRAD, grad_sems.at[r, 2 * p + k], to))
            return
        for copy in part_in[t, r]:
            copy.wait_recv()
        total = own_part[r]
        for k in range(got.shape[2]):
            total = total + got[t, r, k].astype(f32)
        grads[t, r, slab, :] = total.astype(bf16)
        gather = Gather(halves_of(grads.at[t, r]), grads.at[t, r, slab], GRAD, grad_sems.at[r])
        gather.lead()
        grad_in[t, r] = gather.copies

    def have_grads(t, r):
        for copy in grad_in[t, r]:
            copy.wait_recv()

    def stage_project(t, r):
        have_grads(t, r)
        edge[t, r, 0] = dot(proj[0], grads[t, r]).astype(bf16)
        if t == last:
            return
        down_copy, skip = edge_in[t, r]
        pl.when((section > 0) & (section != mid))(down_copy.start)
        @pl.when(section > mid)
        def _():
            edge[t, r, 1] = dot(proj[1], grads[t, r]).astype(bf16)
            skip.start()

        @pl.when(section == mid)
        def _():
            second = dot(proj[1], grads[t, r]).astype(bf16)
            edge[t, r, 0] = (edge[t, r, 0].astype(f32) + second.astype(f32)).astype(bf16)
            down_copy.start()


    def from_above(t, r):
        @pl.when((section >= mid - 1) & (section < sections - 1))
        def _():
            edge_in[t, r][0].wait_recv()
            upstream[t + 1, r, slab, :] = edge_got[t, r, 0]

        @pl.when(is_top)
        def _():
            if r == 0:
                for copy in loss_in[t]:
                    copy.wait_recv()
            upstream[t + 1, r, slab, :] = loss_t[r, t]

    def stage_next(t, r):
        @pl.when(section < mid - 1)
        def _():
            for copy in edge_in[t, r]:
                copy.wait_recv()
            summed = edge_got[t, r, 0].astype(f32) + edge_got[t, r, 1].astype(f32)
            upstream[t + 1, r, slab, :] = summed.astype(bf16)

        from_above(t, r)
        up_in[t + 1, r].lead()

    def add(t, r, acc, total, term):
        rows = pl.ds(r * saved, saved)
        value = term if t == 0 else acc[r] + term
        if t == last:
            total[rows, :] = value.astype(bf16)
        else:
            acc[r] = value

    def settle(t, r):
        chosen = picks(t, r)
        add(t, r, acc_hidden, sum_hidden, dot_nt(chosen, hidden[t, r]))
        add(t, r, acc_up, sum_up, dot_nt(chosen, upstream[t, r]))

    def give_loss(t):
        if t == 0:
            ld_loss.wait()
            ld_loss_own.wait()
        loss_in.append([
            remote(loss_src.at[t, replica_at(by)], loss_t.at[replica, t], LOSS,
                   loss_sems.at[t, by - 1], section, tensor * replicas + replica_at(by))
            for by in range(1, replicas)
        ])
        for copy in loss_in[t]:
            pl.when(is_top)(copy.start)

    def give_inputs(t):
        if t in (0, last):
            for copy in inputs_in:
                pl.when(section < mid if t == 0 else section >= mid)(copy.start)

    outs = [
        [
            remote(edge.at[last, replica_at(by), k], out.at[k, replica], OUT,
                   outgoing_sems.at[by - 1, k], section, tensor * replicas + replica_at(by))
            for k in range(2)
        ]
        for by in range(1, replicas)
    ]

    def stage_outgoing(r):
        have_grads(last, r)
        for k in range(2):
            edge[last, r, k] = dot(proj[k], grads[last, r]).astype(bf16)
            for by in range(1, replicas):
                pl.when(replica_at(by) == r)(outs[by - 1][k].start)
        add(last, r, acc_grad, sum_grad, dot_nt(picks(last, r), grads[last, r]))

    def early(t):
        return section >= sections - 1 - t

    for t in range(last):
        for r in range(replicas):
            edge_in[t, r] = (
                remote(edge.at[t, r, 0], edge_got.at[t, r, 0], DOWN, edge_sems.at[t, r, 0], below, me),
                remote(edge.at[t, r, 1], edge_got.at[t, r, 1], SKIP, edge_sems.at[t, r, 1], mirror, me),
            )
            up_in[t + 1, r] = Gather(halves_of(upstream.at[t + 1, r]), upstream.at[t + 1, r, slab], UP, up_sems.at[r])

    every = range(replicas)
    end = replicas - 1
    loss_in = []
    inputs_in = [
        remote(inputs_hbm.at[k, replica_at(by), rows], in_got.at[replica, k, rows], INPUTS,
               inputs_sems.at[2 * k + h, by - 1], section, tensor * replicas + replica_at(by))
        for by in range(1, replicas)
        for k in range(2)
        for h, rows in enumerate((low, pl.ds(half, own - half)))
    ]
    gathered = [
        pltpu.make_async_copy(
            inputs_hbm.at[:, replica] if by == 0 else in_got.at[replica_at(by)], lanes(replica_at(by)), out_sem.at[1 + by]
        )
        for by in range(replicas)
    ]

    def take_inputs():
        for copy in inputs_in:
            copy.wait_recv()
        for copy in gathered:
            copy.start()

    for t in range(ticks):
        project = stage_project if t < last else lambda t, r: stage_outgoing(r)
        for r in every:
            stage_hidden(t, r)
            stage_parts(t, r)
        if t < last:
            give_loss(t)
        for r in every:
            stage_relay(t, r)
            if r == 0:
                settle(t, r)
            if t == last and r == 0:
                for other in range(1, replicas):
                    settle(t, other)
        for r in every:
            stage_sum(t, r)
            if r < end:
                fill(4) if t == last else settle(t, r + 1)
        if t < last:
            @pl.when(early(t))
            def _():
                for r in every:
                    from_above(t, r)
                    up_in[t + 1, r].lead()
                    up_in[t + 1, r].follow()

            for r in every:
                pick_slope(t + 1, r)
        else:
            fill(8)
        if t == 0:
            for r in every:
                pool_t[:, pl.ds(r * saved, saved)] = pool[r].T
            ld_proj.wait()
        give_inputs(t)
        if t == last:
            pl.when(section < mid)(take_inputs)
        for r in every:
            project(t, r)
            if t == last and r < end:
                fill(2)
        if t == last:
            break
        pl.when(early(t))(lambda: [up_in[t + 1, r].forward() for r in every] and None)

        @pl.when(jnp.logical_not(early(t)))
        def _():
            for r in every:
                stage_next(t, r)
                if r == 0:
                    up_in[t + 1, r].follow()

        for r in every:
            add(t, r, acc_grad, sum_grad, dot_nt(picks(t, r), grads[t, r]))

            @pl.when(jnp.logical_not(early(t)))
            def _():
                up_in[t + 1, r].forward()
                if r < end:
                    up_in[t + 1, r + 1].follow()

    pl.when(section >= mid)(take_inputs)
    place = pltpu.make_async_copy(edge.at[last, replica], out.at[:, replica], out_sem.at[0])
    place.start()
    fill(len(down_steps) + len(up_steps))
    for copy in gathered:
        copy.wait()
    keep = jnp.where(section < sections // 2, 0.0, 1.0).astype(f32)
    for k in range(2):
        for start, size in ((0, half), (half, own - half)):
            total = dot(inputs[k, pl.ds(start, size), :], sum_grad[...])
            proj_grad[k, pl.ds(start, size), :] = (total * keep if k else total).astype(bf16)
    place.wait()
    for pair in outs:
        for copy in pair:
            copy.wait_recv()
    all_sent(POOL, pool.at[pl.ds(0, replicas - 1)])
    all_sent(IDS, ids.at[pl.ds(0, replicas - 1)])
    others = pl.ds(0, (members - 1) * own)
    all_sent(SEED, upstream.at[0, :, others])
    all_sent(PART, upstream if square else part)
    all_sent(GRAD, upstream.at[:, :, pl.ds(0, 2 * own)] if square else part)
    all_sent(UP, upstream.at[pl.ds(0, last), :, others])
    all_sent(INPUTS, in_got.at[pl.ds(0, replicas - 1)])
    all_sent(OUT, edge.at[last, pl.ds(0, replicas - 1)])
    pl.when(section > 0)(lambda: all_sent(DOWN, edge_got.at[:, :, 0]))
    pl.when(section > mid)(lambda: all_sent(SKIP, edge_got.at[:, :, 1]))
    pl.when(is_top)(lambda: all_sent(LOSS, loss_t.at[pl.ds(0, replicas - 1)]))


def tail_kernel(*refs):
    pairs, sems = list(zip(refs[:4], refs[4:8])), refs[8]
    copies = [pltpu.make_async_copy(src, dst, sems.at[i]) for i, (src, dst) in enumerate(pairs)]
    for copy in copies:
        copy.start()
    for copy in copies:
        copy.wait()


def body(pool_inputs, pool_mixed, crop_ids, incoming, loss_grads, w_proj, w_up, w_down):
    sections = lax.axis_size("section")
    tensors, replicas = lax.axis_size("tensor"), lax.axis_size("replica")
    members = tensors * replicas
    own = w_proj.shape[2]
    own_p = -(-own // 16) * 16
    rows, width = incoming.shape[1], w_up.shape[1]
    width_p = members * own_p
    hidden = w_up.shape[2]
    ticks = crop_ids.shape[1]
    saved = pool_mixed.shape[1]

    def padded(x, axis):
        if own == own_p:
            return x
        count = x.shape[axis] // own
        shape = x.shape[:axis] + (count, own) + x.shape[axis + 1:]
        fill = [(0, 0)] * (x.ndim + 1)
        fill[axis + 1] = (0, own_p - own)
        shape_p = x.shape[:axis] + (count * own_p,) + x.shape[axis + 1:]
        return jnp.pad(x.reshape(shape), fill).reshape(shape_p)

    proj = padded(padded(w_proj[0], 1), 2)
    up, down = padded(w_up[0], 0), padded(w_down[0], 1)
    pool_own = padded(pool_mixed[0], 1)
    features = pool_inputs[0].transpose(1, 2, 0).reshape(2, replicas, own, saved)
    features = padded(features, 2)
    seed = padded(incoming[0].T, 0)
    loss = loss_grads.transpose(0, 2, 1).reshape(ticks - 1, replicas, own, rows)
    loss = padded(loss, 2)

    shape = jax.ShapeDtypeStruct
    vmem = pl.BlockSpec(memory_space=pltpu.VMEM)
    hbm = pl.BlockSpec(memory_space=pl.ANY)
    dma = pltpu.SemaphoreType.DMA
    square = tensors == 2 and replicas == 2 and own_p % 32 == 0
    flows = 6 if square else members - 1
    terms = 8 if square else members - 1
    scratch = [
        pltpu.VMEM(proj.shape, bf16), pltpu.VMEM(up.shape, bf16), pltpu.VMEM(down.shape, bf16),
        pltpu.VMEM(loss.shape, bf16), pltpu.VMEM((replicas,) + crop_ids.shape[1:], jnp.int32),
        pltpu.VMEM((replicas, ticks - 1, own_p, rows), bf16),
        pltpu.VMEM((replicas, saved, width_p), bf16), pltpu.VMEM((width_p, replicas * saved), bf16),
        pltpu.VMEM((hidden, replicas * saved), bf16),
        pltpu.VMEM((ticks, replicas, width_p, rows), bf16),
        pltpu.VMEM((ticks, replicas, width_p, rows), bf16),
        pltpu.VMEM((ticks, replicas, hidden, rows), bf16),
        pltpu.VMEM((ticks, replicas, 2 if square else members - 1, own_p, rows), bf16),
        pltpu.VMEM((ticks, replicas, 3, 2, 2, own_p // 2, rows) if square else (16, 128), bf16),
        pltpu.VMEM((16, 128) if square else (ticks, replicas, members - 1, own_p, rows), bf16),
        pltpu.VMEM((replicas, 2, 2, own_p // 2, rows) if square else (8, 128), f32),
        pltpu.VMEM((replicas, own_p, rows), f32),
        pltpu.VMEM((replicas, hidden, saved), bf16), pltpu.VMEM((replicas, hidden, saved), bf16),
        pltpu.VMEM((replicas, hidden, rows), f32),
        pltpu.VMEM((ticks, replicas, 2, own_p, rows), bf16),
        pltpu.VMEM((ticks - 1, replicas, 2, own_p, rows), bf16),
        pltpu.VMEM((replicas, saved, hidden), f32), pltpu.VMEM((replicas, saved, width_p), f32),
        pltpu.VMEM((replicas, saved, width_p), f32),
        pltpu.VMEM((replicas * saved, hidden), bf16), pltpu.VMEM((replicas * saved, width_p), bf16),
        pltpu.VMEM((replicas * saved, width_p), bf16),
        dma((8,)), dma((1 + replicas,)), dma((11,)), dma((max(4, replicas - 1),)), dma((4, replicas - 1)),
        dma((replicas - 1,)), dma((ticks - 1, replicas - 1)),
        dma((replicas, terms)), dma((replicas, 4 if square else flows)), dma((replicas, flows)),
        dma((ticks - 1, replicas, 2)), dma((replicas - 1, 2)),
        pltpu.VMEM(up.shape if square else (16, 128), bf16),
        pltpu.VMEM((2, own_p, replicas * saved), bf16),
    ]

    kept_shapes = ((hidden, width_p), (width_p, hidden), (2, own_p, width_p), (2, replicas, own_p, rows))
    vmem_limit = 66_800_000 - sum(2 * math.prod(dims) for dims in kept_shapes)
    _, *kept = pl.pallas_call(
        functools.partial(ticks_kernel, sections, tensors, replicas, own_p, ticks),
        out_shape=(
            shape((replicas, 2, own_p, saved), bf16),
            *(pltpu.VMEM(dims, bf16) for dims in kept_shapes),
        ),
        in_specs=[hbm] * 8,
        out_specs=(hbm,) + (vmem,) * 4,
        scratch_shapes=scratch,
        compiler_params=pltpu.CompilerParams(
            collective_id=0, has_side_effects=True, vmem_limit_bytes=vmem_limit
        ),
        name="ticks",
    )(features, pool_own, crop_ids[0], seed, loss, proj, up, down)

    def trimmed(x, axis):
        if own == own_p:
            return x
        count = x.shape[axis] // own_p
        x = x.reshape(x.shape[:axis] + (count, own_p) + x.shape[axis + 1:])
        x = lax.slice_in_dim(x, 0, own, axis=axis + 1)
        return x.reshape(x.shape[:axis] + (count * own,) + x.shape[axis + 2:])

    grad_down, grad_up, grad_proj, outgoing = pl.pallas_call(
        tail_kernel,
        out_shape=tuple(shape(dims, bf16) for dims in kept_shapes),
        in_specs=[vmem] * 4,
        out_specs=(hbm,) * 4,
        scratch_shapes=[dma((4,))],
        compiler_params=pltpu.CompilerParams(vmem_limit_bytes=128 * 1024),
        name="tail",
    )(*kept)
    grad_down = trimmed(grad_down, 1)[None]
    grad_up = trimmed(grad_up, 0)[None]
    grad_proj = trimmed(trimmed(grad_proj, 1), 2)[None]
    outgoing = trimmed(outgoing, 2).reshape(2, replicas * own, rows).transpose(2, 0, 1)
    return grad_proj, grad_up, grad_down, outgoing[None]


def solution(mesh):
    in_specs = (
        P("section", "replica", None, "tensor"),
        P("section", "replica", None),
        P("section", "replica", None),
        P("section", "replica", "tensor"),
        P(None, "replica", "tensor"),
        P("section", None, ("tensor", "replica"), None),
        P("section", None, ("tensor", "replica")),
        P("section", ("tensor", "replica"), None),
    )
    out_specs = (
        P("section", None, ("tensor", "replica"), None),
        P("section", None, ("tensor", "replica")),
        P("section", ("tensor", "replica"), None),
        P("section", "replica", None, "tensor"),
    )
    return jax.shard_map(body, mesh=mesh, in_specs=in_specs, out_specs=out_specs, check_vma=False)
```

```python
import functools
import math

import jax
import jax.numpy as jnp
from jax import lax
from jax.experimental import pallas as pl
from jax.experimental.pallas import tpu as pltpu
from jax.sharding import PartitionSpec as P

gelu_scale = 0.7978845608
gelu_cubic = 0.044715
bf16, f32 = jnp.bfloat16, jnp.float32
MESH = pl.DeviceIdType.MESH


def gelu_pair(pre_gelu):
    inner = gelu_scale * (pre_gelu + gelu_cubic * pre_gelu * pre_gelu * pre_gelu)
    tanh_part = jnp.tanh(inner)
    gelu_value = 0.5 * pre_gelu * (1.0 + tanh_part)
    gelu_slope = 0.5 * (1.0 + tanh_part) + 0.5 * pre_gelu * (
        1.0 - tanh_part * tanh_part
    ) * gelu_scale * (1.0 + 3.0 * gelu_cubic * pre_gelu * pre_gelu)
    return (gelu_value, gelu_slope)


def dot(a, b):
    return jnp.dot(a, b, preferred_element_type=f32)


def dot_nt(a, b):
    return lax.dot_general(a, b, (((1,), (1,)), ((), ())), preferred_element_type=f32)


def ticks_kernel(
    sections, tensors, replicas, own, ticks,
    inputs_hbm, pool_hbm, ids_hbm, seed_hbm, loss_hbm, proj_hbm, up_hbm, down_hbm,
    in_got, down_grad, up_grad, proj_grad, out,
    proj, up, down, loss_src, ids, loss_t, pool, pool_t, act_t,
    upstream, grads, hidden, part, relay, got, keep_part, own_part, slope_hi, slope_lo, slope,
    edge, edge_got, acc_hidden, acc_grad, acc_up, sum_hidden, sum_grad, sum_up,
    load_sem, out_sem, send_sems, pool_sems, inputs_sems, ids_sems, loss_sems,
    part_sems, grad_sems, up_sems, edge_sems, outgoing_sems, up_near, inputs,
):
    members = tensors * replicas
    square = tensors == 2 and replicas == 2 and own % 32 == 0
    half = own // 2
    section = lax.axis_index("section")
    tensor = lax.axis_index("tensor")
    replica = lax.axis_index("replica")
    me = tensor * replicas + replica
    hidden_rows = down.shape[0]
    saved = pool.shape[1]
    last = ticks - 1
    mid = sections // 2
    along = (1 - tensor) * replicas + replica
    across = tensor * replicas + (1 - replica)

    def device(s, member):
        return {
            "section": s,
            "tensor": lax.div(member, replicas),
            "replica": lax.rem(member, replicas),
        }

    def member_at(by):
        return lax.rem(me + by, members)

    def replica_at(by):
        return lax.rem(replica + by, replicas)

    def slab_of(member):
        return pl.ds(pl.multiple_of(member * own, 16), own)

    loads = []

    def load(src, dst):
        copy = pltpu.make_async_copy(src, dst, load_sem.at[len(loads)])
        copy.start()
        loads.append(copy)
        return copy

    near_order = {1: ((0, 0), (1, 0), (0, 1), (1, 1)), 0: ((0, 0), (0, 1), (1, 0), (1, 1))}

    def term(k, p, side):
        if k == 0:
            member = lax.rem(tensor + side, tensors) * replicas + p
        else:
            member = p * replicas + lax.rem(replica + side, replicas)
        return pl.ds(pl.multiple_of(member * own + k * half, 16), half)

    wide = pl.ds(pl.multiple_of(tensor * (replicas * own), 16), replicas * own)
    ld_pool = load(pool_hbm, pool.at[replica])
    ld_seed = load(seed_hbm, upstream.at[0, replica, wide])
    ld_ids = load(ids_hbm, ids.at[replica])
    ld_up = load(up_hbm, up)
    ld_down = load(down_hbm, down)
    if square:
        order = [term(k, p, side) for side in (1, 0) for k, p in near_order[side]]
        for i, rows in enumerate(order):
            pltpu.make_async_copy(up_hbm.at[rows], up_near.at[pl.ds(i * half, half)], out_sem.at[0]).start()
    ld_loss = load(loss_hbm, loss_src)
    ld_loss_own = load(loss_hbm.at[:, replica], loss_t.at[replica])
    ld_proj = load(proj_hbm, proj)

    barrier = pltpu.get_barrier_semaphore()
    above = lax.rem(section + 1, sections)
    below = lax.rem(section + sections - 1, sections)
    mirror = sections - 1 - section
    for by in range(1, members):
        pl.semaphore_signal(barrier, 1, device_id=device(section, member_at(by)), device_id_type=MESH)
    for other in (above, below, mirror):
        pl.semaphore_signal(barrier, 1, device_id=device(other, me), device_id_type=MESH)
    pl.semaphore_wait(barrier, members - 1 + 3)

    POOL, IDS, SEED, PART, GRAD, UP, INPUTS, DOWN, SKIP, LOSS, OUT = range(11)

    def remote(src, dst, kind, recv_sem, s, member):
        return pltpu.make_async_remote_copy(
            src_ref=src, dst_ref=dst, send_sem=send_sems.at[kind], recv_sem=recv_sem,
            device_id=device(s, member), device_id_type=MESH,
        )

    def send(src, dst, kind, recv_sem, member):
        copy = remote(src, dst, kind, recv_sem, section, member)
        copy.start()
        return copy

    def over_replicas(src_of, dst, kind, sems):
        return [
            send(src_of(replica_at(by)), dst, kind, sems.at[by - 1], tensor * replicas + replica_at(by))
            for by in range(1, replicas)
        ]

    def all_sent(kind, ref):
        pltpu.make_async_copy(ref, ref, send_sems.at[kind]).wait()

    def lanes(r):
        return inputs.at[:, :, pl.ds(pl.multiple_of(r * saved, 128), saved)]

    chunk = 128
    down_steps = [(start, min(chunk, hidden_rows - start)) for start in range(0, hidden_rows, chunk)]
    up_steps = [(start, min(chunk, up_grad.shape[0] - start)) for start in range(0, up_grad.shape[0], chunk)]

    def fill(count):
        for _ in range(count):
            if down_steps:
                start, size = down_steps.pop(0)
                down_grad[pl.ds(start, size), :] = dot(act_t[pl.ds(start, size), :], sum_up[...]).astype(bf16)
            elif up_steps:
                start, size = up_steps.pop(0)
                up_grad[pl.ds(start, size), :] = dot(pool_t[pl.ds(start, size), :], sum_hidden[...]).astype(bf16)

    class Gather:
        def __init__(self, at, whole, kind, sems):
            if square:
                flows = ((me, 0, along), (me, 1, across), (me, 1, along), (me, 0, across),
                         (along, 0, across), (across, 1, along))
                self.copies = [
                    remote(at(member, h), at(member, h), kind, sems.at[i], section, to)
                    for i, (member, h, to) in enumerate(flows)
                ]
            else:
                self.copies = [
                    remote(whole, whole, kind, sems.at[by - 1], section, member_at(by))
                    for by in range(1, members)
                ]

        def lead(self):
            for copy in self.copies[:2 if square else None]:
                copy.start()

        def follow(self):
            if square:
                self.copies[2].start()
                self.copies[3].start()

        def forward(self):
            if square:
                for i in range(2):
                    self.copies[i].wait_recv()
                    self.copies[4 + i].start()

        def finish(self):
            for copy in self.copies[2 if square else 0:]:
                copy.wait_recv()

    def halves_of(ref):
        return lambda member, h: ref.at[pl.ds(pl.multiple_of(member * own + h * half, 16), half)]

    def seed_at(member, h):
        return upstream.at[0, lax.rem(member, replicas),
                           pl.ds(pl.multiple_of(lax.div(member, replicas) * (replicas * own) + h * own, 16), own)]

    slab = slab_of(me)
    low, high = pl.ds(0, half), pl.ds(half, half)
    ld_pool.wait()
    pieces = 2
    if square:
        rows = saved // (2 * pieces)

        def piece(r, p):
            return pool.at[r, pl.ds(pl.multiple_of((tensor * pieces + p) * rows, 8), rows)]

        pool_in = [
            send(piece(replica, p), piece(replica, p), POOL, pool_sems.at[p], across)
            for p in range(pieces)
        ]
    else:
        pool_in = over_replicas(lambda r: pool.at[replica], pool.at[replica], POOL, pool_sems)
    ld_seed.wait()
    seed_in = Gather(seed_at, upstream.at[0, replica, wide], SEED, up_sems.at[0])
    seed_in.lead()
    seed_in.follow()
    ld_ids.wait()
    ids_in = over_replicas(lambda r: ids.at[replica], ids.at[replica], IDS, ids_sems)
    is_top = section == sections - 1

    step = 256 if hidden_rows % 256 == 0 else 128

    def pre_slopes(r):
        def pre_at(start, size):
            cols = pl.ds(start, size)
            value, gelu_slope = gelu_pair(dot(pool[r], up[:, cols]).T)
            act_t[cols, pl.ds(pl.multiple_of(r * saved, 128), saved)] = value.astype(bf16)
            high = gelu_slope.astype(bf16)
            slope_hi[r, cols, :] = high
            slope_lo[r, cols, :] = (gelu_slope - high.astype(f32)).astype(bf16)

        @pl.loop(0, hidden_rows // step)
        def _(c):
            pre_at(pl.multiple_of(c * step, step), step)

        if hidden_rows % step:
            pre_at(hidden_rows - hidden_rows % step, hidden_rows % step)

    def picks(t, r):
        row = ids[r, pl.ds(t, 1), :]
        place_of = lax.broadcasted_iota(jnp.int32, (saved, row.shape[1]), 0)
        return jnp.where(place_of == row, 1.0, 0.0).astype(bf16)

    def pick_slope(t, r):
        chosen = picks(t, r)
        slope[r] = dot(slope_hi[r], chosen) + dot(slope_lo[r], chosen)

    ld_up.wait()
    pre_slopes(replica)
    pick_slope(0, replica)
    if square:
        pool_over = []
        for p in range(pieces):
            pool_in[p].wait_recv()
            come = piece(1 - replica, p)
            pool_over.append(send(come, come, POOL, pool_sems.at[pieces + p], along))
        seed_in.forward()
        for copy in pool_over:
            copy.wait_recv()
        pre_slopes(1 - replica)
    else:
        for by in range(1, replicas):
            pool_in[by - 1].wait_recv()
            pre_slopes(lax.rem(replica + replicas - by, replicas))
    for copy in ids_in:
        copy.wait_recv()
    for by in range(1, replicas):
        pick_slope(0, lax.rem(replica + by, replicas))

    ld_down.wait()
    if square:
        pltpu.make_async_copy(up_hbm, up_near, out_sem.at[0]).wait()
    seed_in.finish()

    up_in, part_in, grad_in, edge_in = {}, {}, {}, {}

    def stage_hidden(t, r):
        if t > 0:
            up_in[t, r].finish()
        hidden[t, r] = (dot(down[...], upstream[t, r]) * slope[r]).astype(bf16)
        if square:
            part[t, r, 0] = dot(up_near[:own, :], hidden[t, r]).astype(bf16)
            part_in[t, r] = put_terms(t, r, 0)

    def put_terms(t, r, p):
        return [
            send(part.at[t, r, p, rows], relay.at[t, r, 0, k, p], PART, part_sems.at[r, 2 * p + k], to)
            for k, (to, rows) in enumerate(((along, low), (across, high)))
        ]

    def stage_parts(t, r):
        if square:
            near_terms = dot(up_near[own:, :], hidden[t, r])
            part[t, r, 1] = near_terms[:own].astype(bf16)
            part_in[t, r] += put_terms(t, r, 1)
            for k in range(2):
                for p in range(2):
                    start = own + (2 * k + p) * half
                    keep_part[r, k, p] = near_terms[start:start + half]
            return
        part_in[t, r] = []
        for by in range(1, members):
            to = member_at(by)
            part[t, r, by - 1] = dot(up[slab_of(to), :], hidden[t, r]).astype(bf16)
            part_in[t, r].append(send(part.at[t, r, by - 1], got.at[t, r, by - 1], PART,
                                      part_sems.at[r, by - 1], to))
        own_part[r] = dot(up[slab, :], hidden[t, r]) + upstream[t, r, slab, :].astype(f32)

    def stage_relay(t, r):
        if square:
            for p in range(2):
                for k, to in enumerate((across, along)):
                    part_in[t, r][2 * p + k].wait_recv()
                    total = keep_part[r, k, p] + relay[t, r, 0, k, p].astype(f32)
                    relay[t, r, 1, k, p] = total.astype(bf16)
                    part_in[t, r].append(send(relay.at[t, r, 1, k, p], relay.at[t, r, 2, k, p], PART,
                                              part_sems.at[r, 4 + 2 * p + k], to))

    def stage_sum(t, r):
        if square:
            grad_in[t, r] = []
            for p in range(2):
                for k, to in enumerate((along, across)):
                    part_in[t, r][4 + 2 * p + k].wait_recv()
                    rows = term(k, p, 0)
                    total = relay[t, r, 1, k, p].astype(f32) + relay[t, r, 2, k, p].astype(f32)
                    grads[t, r, rows, :] = (total + upstream[t, r, rows, :].astype(f32)).astype(bf16)
                    mine = grads.at[t, r, rows]
                    grad_in[t, r].append(send(mine, mine, GRAD, grad_sems.at[r, 2 * p + k], to))
            return
        for copy in part_in[t, r]:
            copy.wait_recv()
        total = own_part[r]
        for k in range(got.shape[2]):
            total = total + got[t, r, k].astype(f32)
        grads[t, r, slab, :] = total.astype(bf16)
        gather = Gather(halves_of(grads.at[t, r]), grads.at[t, r, slab], GRAD, grad_sems.at[r])
        gather.lead()
        grad_in[t, r] = gather.copies

    def have_grads(t, r):
        for copy in grad_in[t, r]:
            copy.wait_recv()

    def stage_project(t, r):
        have_grads(t, r)
        down_copy, skip = edge_in[t, r]

        @pl.when(section > mid)
        def _():
            edge[t, r, 1] = dot(proj[1], grads[t, r]).astype(bf16)
            skip.start()

        edge[t, r, 0] = dot(proj[0], grads[t, r]).astype(bf16)
        pl.when((section > 0) & (section != mid))(down_copy.start)
        @pl.when(section == mid)
        def _():
            second = dot(proj[1], grads[t, r]).astype(bf16)
            edge[t, r, 0] = (edge[t, r, 0].astype(f32) + second.astype(f32)).astype(bf16)
            down_copy.start()


    def from_above(t, r):
        @pl.when((section >= mid - 1) & (section < sections - 1))
        def _():
            edge_in[t, r][0].wait_recv()
            upstream[t + 1, r, slab, :] = edge_got[t, r, 0]

        @pl.when(is_top)
        def _():
            if r == 0:
                for copy in loss_in[t]:
                    copy.wait_recv()
            upstream[t + 1, r, slab, :] = loss_t[r, t]

    def stage_next(t, r):
        @pl.when(section < mid - 1)
        def _():
            for copy in edge_in[t, r]:
                copy.wait_recv()
            summed = edge_got[t, r, 0].astype(f32) + edge_got[t, r, 1].astype(f32)
            upstream[t + 1, r, slab, :] = summed.astype(bf16)

        from_above(t, r)
        up_in[t + 1, r].lead()

    def add(t, r, acc, total, term):
        rows = pl.ds(r * saved, saved)
        value = term if t == 0 else acc[r] + term
        if t == last:
            total[rows, :] = value.astype(bf16)
        else:
            acc[r] = value

    def settle(t, r):
        chosen = picks(t, r)
        add(t, r, acc_hidden, sum_hidden, dot_nt(chosen, hidden[t, r]))
        add(t, r, acc_up, sum_up, dot_nt(chosen, upstream[t, r]))

    def give_loss(t):
        if t == 0:
            ld_loss.wait()
            ld_loss_own.wait()
        loss_in.append([
            remote(loss_src.at[t, replica_at(by)], loss_t.at[replica, t], LOSS,
                   loss_sems.at[t, by - 1], section, tensor * replicas + replica_at(by))
            for by in range(1, replicas)
        ])
        for copy in loss_in[t]:
            pl.when(is_top)(copy.start)

    def give_inputs(t):
        if t in (0, last):
            for copy in inputs_in:
                pl.when(section < mid if t == 0 else section >= mid)(copy.start)

    outs = [
        [
            remote(edge.at[last, replica_at(by), k], out.at[k, replica], OUT,
                   outgoing_sems.at[by - 1, k], section, tensor * replicas + replica_at(by))
            for k in range(2)
        ]
        for by in range(1, replicas)
    ]

    def stage_outgoing(r):
        have_grads(last, r)
        for k in range(2):
            edge[last, r, k] = dot(proj[k], grads[last, r]).astype(bf16)
            for by in range(1, replicas):
                pl.when(replica_at(by) == r)(outs[by - 1][k].start)
        add(last, r, acc_grad, sum_grad, dot_nt(picks(last, r), grads[last, r]))

    def early(t):
        return section >= sections - 1 - t

    for t in range(last):
        for r in range(replicas):
            edge_in[t, r] = (
                remote(edge.at[t, r, 0], edge_got.at[t, r, 0], DOWN, edge_sems.at[t, r, 0], below, me),
                remote(edge.at[t, r, 1], edge_got.at[t, r, 1], SKIP, edge_sems.at[t, r, 1], mirror, me),
            )
            up_in[t + 1, r] = Gather(halves_of(upstream.at[t + 1, r]), upstream.at[t + 1, r, slab], UP, up_sems.at[r])

    every = range(replicas)
    end = replicas - 1
    loss_in = []
    inputs_in = [
        remote(inputs_hbm.at[k, replica_at(by), rows], in_got.at[replica, k, rows], INPUTS,
               inputs_sems.at[2 * k + h, by - 1], section, tensor * replicas + replica_at(by))
        for by in range(1, replicas)
        for k in range(2)
        for h, rows in enumerate((low, pl.ds(half, own - half)))
    ]
    gathered = [
        pltpu.make_async_copy(
            inputs_hbm.at[:, replica] if by == 0 else in_got.at[replica_at(by)], lanes(replica_at(by)), out_sem.at[1 + by]
        )
        for by in range(replicas)
    ]

    def take_inputs():
        for copy in inputs_in:
            copy.wait_recv()
        for copy in gathered:
            copy.start()

    for t in range(ticks):
        project = stage_project if t < last else lambda t, r: stage_outgoing(r)
        for r in every:
            stage_hidden(t, r)
            stage_parts(t, r)
        if t < last:
            give_loss(t)
        for r in every:
            stage_relay(t, r)
            if r == 0:
                settle(t, r)
            if t == last and r == 0:
                for other in range(1, replicas):
                    settle(t, other)
        for r in every:
            stage_sum(t, r)
            if r < end:
                fill(4) if t == last else settle(t, r + 1)
        if t < last:
            @pl.when(early(t))
            def _():
                for r in every:
                    from_above(t, r)
                    up_in[t + 1, r].lead()
                    up_in[t + 1, r].follow()

            for r in every:
                pick_slope(t + 1, r)
        else:
            fill(8)
        if t == 0:
            for r in every:
                pool_t[:, pl.ds(r * saved, saved)] = pool[r].T
            ld_proj.wait()
        give_inputs(t)
        if t == last:
            pl.when(section < mid)(take_inputs)
        for r in every:
            project(t, r)
            if t == last and r < end:
                fill(2)
        if t == last:
            break
        pl.when(early(t))(lambda: [up_in[t + 1, r].forward() for r in every] and None)

        @pl.when(jnp.logical_not(early(t)))
        def _():
            for r in every:
                stage_next(t, r)
                if r == 0:
                    up_in[t + 1, r].follow()

        for r in every:
            add(t, r, acc_grad, sum_grad, dot_nt(picks(t, r), grads[t, r]))

            @pl.when(jnp.logical_not(early(t)))
            def _():
                up_in[t + 1, r].forward()
                if r < end:
                    up_in[t + 1, r + 1].follow()

    pl.when(section >= mid)(take_inputs)
    place = pltpu.make_async_copy(edge.at[last, replica], out.at[:, replica], out_sem.at[0])
    place.start()
    fill(len(down_steps) + len(up_steps))
    for copy in gathered:
        copy.wait()
    keep = jnp.where(section < sections // 2, 0.0, 1.0).astype(f32)
    for k in range(2):
        for start, size in ((0, half), (half, own - half)):
            total = dot(inputs[k, pl.ds(start, size), :], sum_grad[...])
            proj_grad[k, pl.ds(start, size), :] = (total * keep if k else total).astype(bf16)
    place.wait()
    for pair in outs:
        for copy in pair:
            copy.wait_recv()
    all_sent(POOL, pool.at[pl.ds(0, replicas - 1)])
    all_sent(IDS, ids.at[pl.ds(0, replicas - 1)])
    others = pl.ds(0, (members - 1) * own)
    all_sent(SEED, upstream.at[0, :, others])
    all_sent(PART, upstream if square else part)
    all_sent(GRAD, upstream.at[:, :, pl.ds(0, 2 * own)] if square else part)
    all_sent(UP, upstream.at[pl.ds(0, last), :, others])
    all_sent(INPUTS, in_got.at[pl.ds(0, replicas - 1)])
    all_sent(OUT, edge.at[last, pl.ds(0, replicas - 1)])
    pl.when(section > 0)(lambda: all_sent(DOWN, edge_got.at[:, :, 0]))
    pl.when(section > mid)(lambda: all_sent(SKIP, edge_got.at[:, :, 1]))
    pl.when(is_top)(lambda: all_sent(LOSS, loss_t.at[pl.ds(0, replicas - 1)]))


def tail_kernel(*refs):
    pairs, sems = list(zip(refs[:4], refs[4:8])), refs[8]
    copies = [pltpu.make_async_copy(src, dst, sems.at[i]) for i, (src, dst) in enumerate(pairs)]
    for copy in copies:
        copy.start()
    for copy in copies:
        copy.wait()


def body(pool_inputs, pool_mixed, crop_ids, incoming, loss_grads, w_proj, w_up, w_down):
    sections = lax.axis_size("section")
    tensors, replicas = lax.axis_size("tensor"), lax.axis_size("replica")
    members = tensors * replicas
    own = w_proj.shape[2]
    own_p = -(-own // 16) * 16
    rows, width = incoming.shape[1], w_up.shape[1]
    width_p = members * own_p
    hidden = w_up.shape[2]
    ticks = crop_ids.shape[1]
    saved = pool_mixed.shape[1]

    def padded(x, axis):
        if own == own_p:
            return x
        count = x.shape[axis] // own
        shape = x.shape[:axis] + (count, own) + x.shape[axis + 1:]
        fill = [(0, 0)] * (x.ndim + 1)
        fill[axis + 1] = (0, own_p - own)
        shape_p = x.shape[:axis] + (count * own_p,) + x.shape[axis + 1:]
        return jnp.pad(x.reshape(shape), fill).reshape(shape_p)

    proj = padded(padded(w_proj[0], 1), 2)
    up, down = padded(w_up[0], 0), padded(w_down[0], 1)
    pool_own = padded(pool_mixed[0], 1)
    features = pool_inputs[0].transpose(1, 2, 0).reshape(2, replicas, own, saved)
    features = padded(features, 2)
    seed = padded(incoming[0].T, 0)
    loss = loss_grads.transpose(0, 2, 1).reshape(ticks - 1, replicas, own, rows)
    loss = padded(loss, 2)

    shape = jax.ShapeDtypeStruct
    vmem = pl.BlockSpec(memory_space=pltpu.VMEM)
    hbm = pl.BlockSpec(memory_space=pl.ANY)
    dma = pltpu.SemaphoreType.DMA
    square = tensors == 2 and replicas == 2 and own_p % 32 == 0
    flows = 6 if square else members - 1
    terms = 8 if square else members - 1
    scratch = [
        pltpu.VMEM(proj.shape, bf16), pltpu.VMEM(up.shape, bf16), pltpu.VMEM(down.shape, bf16),
        pltpu.VMEM(loss.shape, bf16), pltpu.VMEM((replicas,) + crop_ids.shape[1:], jnp.int32),
        pltpu.VMEM((replicas, ticks - 1, own_p, rows), bf16),
        pltpu.VMEM((replicas, saved, width_p), bf16), pltpu.VMEM((width_p, replicas * saved), bf16),
        pltpu.VMEM((hidden, replicas * saved), bf16),
        pltpu.VMEM((ticks, replicas, width_p, rows), bf16),
        pltpu.VMEM((ticks, replicas, width_p, rows), bf16),
        pltpu.VMEM((ticks, replicas, hidden, rows), bf16),
        pltpu.VMEM((ticks, replicas, 2 if square else members - 1, own_p, rows), bf16),
        pltpu.VMEM((ticks, replicas, 3, 2, 2, own_p // 2, rows) if square else (16, 128), bf16),
        pltpu.VMEM((16, 128) if square else (ticks, replicas, members - 1, own_p, rows), bf16),
        pltpu.VMEM((replicas, 2, 2, own_p // 2, rows) if square else (8, 128), f32),
        pltpu.VMEM((replicas, own_p, rows), f32),
        pltpu.VMEM((replicas, hidden, saved), bf16), pltpu.VMEM((replicas, hidden, saved), bf16),
        pltpu.VMEM((replicas, hidden, rows), f32),
        pltpu.VMEM((ticks, replicas, 2, own_p, rows), bf16),
        pltpu.VMEM((ticks - 1, replicas, 2, own_p, rows), bf16),
        pltpu.VMEM((replicas, saved, hidden), f32), pltpu.VMEM((replicas, saved, width_p), f32),
        pltpu.VMEM((replicas, saved, width_p), f32),
        pltpu.VMEM((replicas * saved, hidden), bf16), pltpu.VMEM((replicas * saved, width_p), bf16),
        pltpu.VMEM((replicas * saved, width_p), bf16),
        dma((8,)), dma((1 + replicas,)), dma((11,)), dma((max(4, replicas - 1),)), dma((4, replicas - 1)),
        dma((replicas - 1,)), dma((ticks - 1, replicas - 1)),
        dma((replicas, terms)), dma((replicas, 4 if square else flows)), dma((replicas, flows)),
        dma((ticks - 1, replicas, 2)), dma((replicas - 1, 2)),
        pltpu.VMEM(up.shape if square else (16, 128), bf16),
        pltpu.VMEM((2, own_p, replicas * saved), bf16),
    ]

    kept_shapes = ((hidden, width_p), (width_p, hidden), (2, own_p, width_p), (2, replicas, own_p, rows))
    vmem_limit = 66_800_000 - sum(2 * math.prod(dims) for dims in kept_shapes)
    _, *kept = pl.pallas_call(
        functools.partial(ticks_kernel, sections, tensors, replicas, own_p, ticks),
        out_shape=(
            shape((replicas, 2, own_p, saved), bf16),
            *(pltpu.VMEM(dims, bf16) for dims in kept_shapes),
        ),
        in_specs=[hbm] * 8,
        out_specs=(hbm,) + (vmem,) * 4,
        scratch_shapes=scratch,
        compiler_params=pltpu.CompilerParams(
            collective_id=0, has_side_effects=True, vmem_limit_bytes=vmem_limit
        ),
        name="ticks",
    )(features, pool_own, crop_ids[0], seed, loss, proj, up, down)

    def trimmed(x, axis):
        if own == own_p:
            return x
        count = x.shape[axis] // own_p
        x = x.reshape(x.shape[:axis] + (count, own_p) + x.shape[axis + 1:])
        x = lax.slice_in_dim(x, 0, own, axis=axis + 1)
        return x.reshape(x.shape[:axis] + (count * own,) + x.shape[axis + 2:])

    grad_down, grad_up, grad_proj, outgoing = pl.pallas_call(
        tail_kernel,
        out_shape=tuple(shape(dims, bf16) for dims in kept_shapes),
        in_specs=[vmem] * 4,
        out_specs=(hbm,) * 4,
        scratch_shapes=[dma((4,))],
        compiler_params=pltpu.CompilerParams(vmem_limit_bytes=128 * 1024),
        name="tail",
    )(*kept)
    grad_down = trimmed(grad_down, 1)[None]
    grad_up = trimmed(grad_up, 0)[None]
    grad_proj = trimmed(trimmed(grad_proj, 1), 2)[None]
    outgoing = trimmed(outgoing, 2).reshape(2, replicas * own, rows).transpose(2, 0, 1)
    return grad_proj, grad_up, grad_down, outgoing[None]


def solution(mesh):
    in_specs = (
        P("section", "replica", None, "tensor"),
        P("section", "replica", None),
        P("section", "replica", None),
        P("section", "replica", "tensor"),
        P(None, "replica", "tensor"),
        P("section", None, ("tensor", "replica"), None),
        P("section", None, ("tensor", "replica")),
        P("section", ("tensor", "replica"), None),
    )
    out_specs = (
        P("section", None, ("tensor", "replica"), None),
        P("section", None, ("tensor", "replica")),
        P("section", ("tensor", "replica"), None),
        P("section", "replica", None, "tensor"),
    )
    return jax.shard_map(body, mesh=mesh, in_specs=in_specs, out_specs=out_specs, check_vma=False)
```

```python
import functools
import math

import jax
import jax.numpy as jnp
from jax import lax
from jax.experimental import pallas as pl
from jax.experimental.pallas import tpu as pltpu
from jax.sharding import PartitionSpec as P

gelu_scale = 0.7978845608
gelu_cubic = 0.044715
bf16, f32 = jnp.bfloat16, jnp.float32
MESH = pl.DeviceIdType.MESH


def gelu_pair(pre_gelu):
    inner = gelu_scale * (pre_gelu + gelu_cubic * pre_gelu * pre_gelu * pre_gelu)
    tanh_part = jnp.tanh(inner)
    gelu_value = 0.5 * pre_gelu * (1.0 + tanh_part)
    gelu_slope = 0.5 * (1.0 + tanh_part) + 0.5 * pre_gelu * (
        1.0 - tanh_part * tanh_part
    ) * gelu_scale * (1.0 + 3.0 * gelu_cubic * pre_gelu * pre_gelu)
    return (gelu_value, gelu_slope)


def dot(a, b):
    return jnp.dot(a, b, preferred_element_type=f32)


def dot_nt(a, b):
    return lax.dot_general(a, b, (((1,), (1,)), ((), ())), preferred_element_type=f32)


def ticks_kernel(
    sections, tensors, replicas, own, ticks,
    inputs_hbm, pool_hbm, ids_hbm, seed_hbm, loss_hbm, proj_hbm, up_hbm, down_hbm,
    in_got, down_grad, up_grad, proj_grad, out,
    proj, up, down, loss_src, ids, loss_t, pool, pool_t, act_t,
    upstream, grads, hidden, part, relay, got, keep_part, own_part, slope_hi, slope_lo, slope,
    edge, edge_got, acc_hidden, acc_grad, acc_up, sum_hidden, sum_grad, sum_up,
    load_sem, out_sem, send_sems, pool_sems, inputs_sems, ids_sems, loss_sems,
    part_sems, grad_sems, up_sems, edge_sems, outgoing_sems, up_near, inputs,
):
    members = tensors * replicas
    square = tensors == 2 and replicas == 2 and own % 32 == 0
    half = own // 2
    section = lax.axis_index("section")
    tensor = lax.axis_index("tensor")
    replica = lax.axis_index("replica")
    me = tensor * replicas + replica
    hidden_rows = down.shape[0]
    saved = pool.shape[1]
    last = ticks - 1
    mid = sections // 2
    along = (1 - tensor) * replicas + replica
    across = tensor * replicas + (1 - replica)

    def device(s, member):
        return {
            "section": s,
            "tensor": lax.div(member, replicas),
            "replica": lax.rem(member, replicas),
        }

    def member_at(by):
        return lax.rem(me + by, members)

    def replica_at(by):
        return lax.rem(replica + by, replicas)

    def slab_of(member):
        return pl.ds(pl.multiple_of(member * own, 16), own)

    loads = []

    def load(src, dst):
        copy = pltpu.make_async_copy(src, dst, load_sem.at[len(loads)])
        copy.start()
        loads.append(copy)
        return copy

    near_order = {1: ((0, 0), (1, 0), (0, 1), (1, 1)), 0: ((0, 0), (0, 1), (1, 0), (1, 1))}

    def term(k, p, side):
        if k == 0:
            member = lax.rem(tensor + side, tensors) * replicas + p
        else:
            member = p * replicas + lax.rem(replica + side, replicas)
        return pl.ds(pl.multiple_of(member * own + k * half, 16), half)

    wide = pl.ds(pl.multiple_of(tensor * (replicas * own), 16), replicas * own)
    ld_pool = load(pool_hbm, pool.at[replica])
    ld_seed = load(seed_hbm, upstream.at[0, replica, wide])
    ld_ids = load(ids_hbm, ids.at[replica])
    ld_up = load(up_hbm, up)
    ld_down = load(down_hbm, down)
    if square:
        order = [term(k, p, side) for side in (1, 0) for k, p in near_order[side]]
        for i, rows in enumerate(order):
            pltpu.make_async_copy(up_hbm.at[rows], up_near.at[pl.ds(i * half, half)], out_sem.at[0]).start()
    ld_loss = load(loss_hbm, loss_src)
    ld_loss_own = load(loss_hbm.at[:, replica], loss_t.at[replica])
    ld_proj = load(proj_hbm, proj)

    barrier = pltpu.get_barrier_semaphore()
    above = lax.rem(section + 1, sections)
    below = lax.rem(section + sections - 1, sections)
    mirror = sections - 1 - section
    for by in range(1, members):
        pl.semaphore_signal(barrier, 1, device_id=device(section, member_at(by)), device_id_type=MESH)
    for other in (above, below, mirror):
        pl.semaphore_signal(barrier, 1, device_id=device(other, me), device_id_type=MESH)
    pl.semaphore_wait(barrier, members - 1 + 3)

    POOL, IDS, SEED, PART, GRAD, UP, INPUTS, DOWN, SKIP, LOSS, OUT = range(11)

    def remote(src, dst, kind, recv_sem, s, member):
        return pltpu.make_async_remote_copy(
            src_ref=src, dst_ref=dst, send_sem=send_sems.at[kind], recv_sem=recv_sem,
            device_id=device(s, member), device_id_type=MESH,
        )

    def send(src, dst, kind, recv_sem, member):
        copy = remote(src, dst, kind, recv_sem, section, member)
        copy.start()
        return copy

    def over_replicas(src_of, dst, kind, sems):
        return [
            send(src_of(replica_at(by)), dst, kind, sems.at[by - 1], tensor * replicas + replica_at(by))
            for by in range(1, replicas)
        ]

    def all_sent(kind, ref):
        pltpu.make_async_copy(ref, ref, send_sems.at[kind]).wait()

    def lanes(r):
        return inputs.at[:, :, pl.ds(pl.multiple_of(r * saved, 128), saved)]

    chunk = 128
    down_steps = [(start, min(chunk, hidden_rows - start)) for start in range(0, hidden_rows, chunk)]
    up_steps = [(start, min(chunk, up_grad.shape[0] - start)) for start in range(0, up_grad.shape[0], chunk)]

    def fill(count):
        for _ in range(count):
            if down_steps:
                start, size = down_steps.pop(0)
                down_grad[pl.ds(start, size), :] = dot(act_t[pl.ds(start, size), :], sum_up[...]).astype(bf16)
            elif up_steps:
                start, size = up_steps.pop(0)
                up_grad[pl.ds(start, size), :] = dot(pool_t[pl.ds(start, size), :], sum_hidden[...]).astype(bf16)

    class Gather:
        def __init__(self, at, whole, kind, sems):
            if square:
                flows = [(me, h, part, to) for part in range(2) for h, to in enumerate((along, across))]
                flows += [(me, 1, None, along), (me, 0, None, across)]
                flows += [(to, h, part, on) for part in range(2) for h, (to, on) in
                          enumerate(((along, across), (across, along)))]
                self.copies = [
                    remote(at(member, h, part), at(member, h, part), kind, sems.at[i], section, to)
                    for i, (member, h, part, to) in enumerate(flows)
                ]
            else:
                self.copies = [
                    remote(whole, whole, kind, sems.at[by - 1], section, member_at(by))
                    for by in range(1, members)
                ]

        def lead(self):
            for copy in self.copies[:4 if square else None]:
                copy.start()

        def follow(self):
            if square:
                self.copies[4].start()
                self.copies[5].start()

        def forward(self):
            if square:
                for i in range(4):
                    self.copies[i].wait_recv()
                    self.copies[6 + i].start()

        def finish(self):
            for copy in self.copies[4 if square else 0:]:
                copy.wait_recv()

    def part_rows(start, size, part):
        cut = -(-size // 32) * 16
        begin, count = {None: (0, size), 0: (0, cut), 1: (cut, size - cut)}[part]
        return pl.ds(pl.multiple_of(start + begin, 16), count)

    def halves_of(ref):
        return lambda member, h, part: ref.at[part_rows(member * own + h * half, half, part)]

    def seed_at(member, h, part):
        start = lax.div(member, replicas) * (replicas * own) + h * own
        return upstream.at[0, lax.rem(member, replicas), part_rows(start, own, part)]

    slab = slab_of(me)
    low, high = pl.ds(0, half), pl.ds(half, half)
    ld_pool.wait()
    pieces = 2
    if square:
        rows = saved // (2 * pieces)

        def piece(r, p):
            return pool.at[r, pl.ds(pl.multiple_of((tensor * pieces + p) * rows, 8), rows)]

        pool_in = [
            send(piece(replica, p), piece(replica, p), POOL, pool_sems.at[p], across)
            for p in range(pieces)
        ]
    else:
        pool_in = over_replicas(lambda r: pool.at[replica], pool.at[replica], POOL, pool_sems)
    ld_seed.wait()
    seed_in = Gather(seed_at, upstream.at[0, replica, wide], SEED, up_sems.at[0])
    seed_in.lead()
    seed_in.follow()
    ld_ids.wait()
    ids_in = over_replicas(lambda r: ids.at[replica], ids.at[replica], IDS, ids_sems)
    is_top = section == sections - 1

    step = 256 if hidden_rows % 256 == 0 else 128

    def pre_slopes(r):
        def pre_at(start, size):
            cols = pl.ds(start, size)
            value, gelu_slope = gelu_pair(dot(pool[r], up[:, cols]).T)
            act_t[cols, pl.ds(pl.multiple_of(r * saved, 128), saved)] = value.astype(bf16)
            high = gelu_slope.astype(bf16)
            slope_hi[r, cols, :] = high
            slope_lo[r, cols, :] = (gelu_slope - high.astype(f32)).astype(bf16)

        @pl.loop(0, hidden_rows // step)
        def _(c):
            pre_at(pl.multiple_of(c * step, step), step)

        if hidden_rows % step:
            pre_at(hidden_rows - hidden_rows % step, hidden_rows % step)

    def picks(t, r):
        row = ids[r, pl.ds(t, 1), :]
        place_of = lax.broadcasted_iota(jnp.int32, (saved, row.shape[1]), 0)
        return jnp.where(place_of == row, 1.0, 0.0).astype(bf16)

    def pick_slope(t, r):
        chosen = picks(t, r)
        slope[r] = dot(slope_hi[r], chosen) + dot(slope_lo[r], chosen)

    ld_up.wait()
    pre_slopes(replica)
    pick_slope(0, replica)
    if square:
        pool_over = []
        for p in range(pieces):
            pool_in[p].wait_recv()
            come = piece(1 - replica, p)
            pool_over.append(send(come, come, POOL, pool_sems.at[pieces + p], along))
        seed_in.forward()
        for copy in pool_over:
            copy.wait_recv()
        pre_slopes(1 - replica)
    else:
        for by in range(1, replicas):
            pool_in[by - 1].wait_recv()
            pre_slopes(lax.rem(replica + replicas - by, replicas))
    for copy in ids_in:
        copy.wait_recv()
    for by in range(1, replicas):
        pick_slope(0, lax.rem(replica + by, replicas))

    ld_down.wait()
    if square:
        pltpu.make_async_copy(up_hbm, up_near, out_sem.at[0]).wait()
    seed_in.finish()

    up_in, part_in, grad_in, edge_in = {}, {}, {}, {}

    def stage_hidden(t, r):
        if t > 0:
            up_in[t, r].finish()
        hidden[t, r] = (dot(down[...], upstream[t, r]) * slope[r]).astype(bf16)
        if square:
            part[t, r, 0] = dot(up_near[:own, :], hidden[t, r]).astype(bf16)
            part_in[t, r] = put_terms(t, r, 0)

    def put_terms(t, r, p):
        return [
            send(part.at[t, r, p, rows], relay.at[t, r, 0, k, p], PART, part_sems.at[r, 2 * p + k], to)
            for k, (to, rows) in enumerate(((along, low), (across, high)))
        ]

    def stage_parts(t, r):
        if square:
            near_terms = dot(up_near[own:, :], hidden[t, r])
            part[t, r, 1] = near_terms[:own].astype(bf16)
            part_in[t, r] += put_terms(t, r, 1)
            for k in range(2):
                for p in range(2):
                    start = own + (2 * k + p) * half
                    keep_part[r, k, p] = near_terms[start:start + half]
            return
        part_in[t, r] = []
        for by in range(1, members):
            to = member_at(by)
            part[t, r, by - 1] = dot(up[slab_of(to), :], hidden[t, r]).astype(bf16)
            part_in[t, r].append(send(part.at[t, r, by - 1], got.at[t, r, by - 1], PART,
                                      part_sems.at[r, by - 1], to))
        own_part[r] = dot(up[slab, :], hidden[t, r]) + upstream[t, r, slab, :].astype(f32)

    def stage_relay(t, r):
        if square:
            for p in range(2):
                for k, to in enumerate((across, along)):
                    part_in[t, r][2 * p + k].wait_recv()
                    total = keep_part[r, k, p] + relay[t, r, 0, k, p].astype(f32)
                    relay[t, r, 1, k, p] = total.astype(bf16)
                    part_in[t, r].append(send(relay.at[t, r, 1, k, p], relay.at[t, r, 2, k, p], PART,
                                              part_sems.at[r, 4 + 2 * p + k], to))

    def stage_sum(t, r):
        if square:
            grad_in[t, r] = []
            for p in range(2):
                for k, to in enumerate((along, across)):
                    part_in[t, r][4 + 2 * p + k].wait_recv()
                    rows = term(k, p, 0)
                    total = relay[t, r, 1, k, p].astype(f32) + relay[t, r, 2, k, p].astype(f32)
                    grads[t, r, rows, :] = (total + upstream[t, r, rows, :].astype(f32)).astype(bf16)
                    mine = grads.at[t, r, rows]
                    grad_in[t, r].append(send(mine, mine, GRAD, grad_sems.at[r, 2 * p + k], to))
            return
        for copy in part_in[t, r]:
            copy.wait_recv()
        total = own_part[r]
        for k in range(got.shape[2]):
            total = total + got[t, r, k].astype(f32)
        grads[t, r, slab, :] = total.astype(bf16)
        gather = Gather(halves_of(grads.at[t, r]), grads.at[t, r, slab], GRAD, grad_sems.at[r])
        gather.lead()
        grad_in[t, r] = gather.copies

    def have_grads(t, r):
        for copy in grad_in[t, r]:
            copy.wait_recv()

    def stage_project(t, r):
        have_grads(t, r)
        down_copy, skip = edge_in[t, r]

        @pl.when(section > mid)
        def _():
            edge[t, r, 1] = dot(proj[1], grads[t, r]).astype(bf16)
            skip.start()

        edge[t, r, 0] = dot(proj[0], grads[t, r]).astype(bf16)
        pl.when((section > 0) & (section != mid))(down_copy.start)
        @pl.when(section == mid)
        def _():
            second = dot(proj[1], grads[t, r]).astype(bf16)
            edge[t, r, 0] = (edge[t, r, 0].astype(f32) + second.astype(f32)).astype(bf16)
            down_copy.start()


    def from_above(t, r):
        @pl.when((section >= mid - 1) & (section < sections - 1))
        def _():
            edge_in[t, r][0].wait_recv()
            upstream[t + 1, r, slab, :] = edge_got[t, r, 0]

        @pl.when(is_top)
        def _():
            if r == 0:
                for copy in loss_in[t]:
                    copy.wait_recv()
            upstream[t + 1, r, slab, :] = loss_t[r, t]

    def stage_next(t, r):
        @pl.when(section < mid - 1)
        def _():
            for copy in edge_in[t, r]:
                copy.wait_recv()
            summed = edge_got[t, r, 0].astype(f32) + edge_got[t, r, 1].astype(f32)
            upstream[t + 1, r, slab, :] = summed.astype(bf16)

        from_above(t, r)
        up_in[t + 1, r].lead()

    def add(t, r, acc, total, term):
        rows = pl.ds(r * saved, saved)
        value = term if t == 0 else acc[r] + term
        if t == last:
            total[rows, :] = value.astype(bf16)
        else:
            acc[r] = value

    def settle(t, r):
        chosen = picks(t, r)
        add(t, r, acc_hidden, sum_hidden, dot_nt(chosen, hidden[t, r]))
        add(t, r, acc_up, sum_up, dot_nt(chosen, upstream[t, r]))

    def give_loss(t):
        if t == 0:
            ld_loss.wait()
            ld_loss_own.wait()
        loss_in.append([
            remote(loss_src.at[t, replica_at(by)], loss_t.at[replica, t], LOSS,
                   loss_sems.at[t, by - 1], section, tensor * replicas + replica_at(by))
            for by in range(1, replicas)
        ])
        for copy in loss_in[t]:
            pl.when(is_top)(copy.start)

    def give_inputs(t):
        if t in (0, last):
            for copy in inputs_in:
                pl.when(section < mid if t == 0 else section >= mid)(copy.start)

    outs = [
        [
            remote(edge.at[last, replica_at(by), k, rows], out.at[k, replica, rows], OUT,
                   outgoing_sems.at[by - 1, 2 * k + h], section, tensor * replicas + replica_at(by))
            for k in range(2)
            for h, rows in enumerate((low, pl.ds(half, own - half)))
        ]
        for by in range(1, replicas)
    ]

    def stage_outgoing(r):
        have_grads(last, r)
        for k in range(2):
            for h, (start, size) in enumerate(((0, half), (half, own - half))):
                rows = pl.ds(start, size)
                edge[last, r, k, rows] = dot(proj[k, rows], grads[last, r]).astype(bf16)
                for by in range(1, replicas):
                    pl.when(replica_at(by) == r)(outs[by - 1][2 * k + h].start)

    def early(t):
        return section >= sections - 1 - t

    for t in range(last):
        for r in range(replicas):
            edge_in[t, r] = (
                remote(edge.at[t, r, 0], edge_got.at[t, r, 0], DOWN, edge_sems.at[t, r, 0], below, me),
                remote(edge.at[t, r, 1], edge_got.at[t, r, 1], SKIP, edge_sems.at[t, r, 1], mirror, me),
            )
            up_in[t + 1, r] = Gather(halves_of(upstream.at[t + 1, r]), upstream.at[t + 1, r, slab], UP, up_sems.at[r])

    every = range(replicas)
    end = replicas - 1
    loss_in = []
    inputs_in = [
        remote(inputs_hbm.at[k, replica_at(by), rows], in_got.at[replica, k, rows], INPUTS,
               inputs_sems.at[2 * k + h, by - 1], section, tensor * replicas + replica_at(by))
        for by in range(1, replicas)
        for k in range(2)
        for h, rows in enumerate((low, pl.ds(half, own - half)))
    ]
    gathered = [
        pltpu.make_async_copy(
            inputs_hbm.at[:, replica] if by == 0 else in_got.at[replica_at(by)], lanes(replica_at(by)), out_sem.at[1 + by]
        )
        for by in range(replicas)
    ]

    def take_inputs():
        for copy in inputs_in:
            copy.wait_recv()
        for copy in gathered:
            copy.start()

    for t in range(ticks):
        project = stage_project if t < last else lambda t, r: stage_outgoing(r)
        for r in every:
            stage_hidden(t, r)
            stage_parts(t, r)
        if t < last:
            give_loss(t)
        for r in every:
            stage_relay(t, r)
            if r == 0:
                settle(t, r)
            if t == last and r == 0:
                for other in range(1, replicas):
                    settle(t, other)
        for r in every:
            stage_sum(t, r)
            if r < end:
                fill(4) if t == last else settle(t, r + 1)
        if t < last:
            @pl.when(early(t))
            def _():
                for r in every:
                    from_above(t, r)
                    up_in[t + 1, r].lead()
                    up_in[t + 1, r].follow()

            for r in every:
                pick_slope(t + 1, r)
        else:
            fill(8)
        if t == 0:
            for r in every:
                pool_t[:, pl.ds(r * saved, saved)] = pool[r].T
            ld_proj.wait()
        give_inputs(t)
        if t == last:
            pl.when(section < mid)(take_inputs)
        for r in every:
            project(t, r)
        if t == last:
            break
        pl.when(early(t))(lambda: [up_in[t + 1, r].forward() for r in every] and None)

        @pl.when(jnp.logical_not(early(t)))
        def _():
            for r in every:
                stage_next(t, r)
                if r == 0:
                    up_in[t + 1, r].follow()

        for r in every:
            add(t, r, acc_grad, sum_grad, dot_nt(picks(t, r), grads[t, r]))

            @pl.when(jnp.logical_not(early(t)))
            def _():
                up_in[t + 1, r].forward()
                if r < end:
                    up_in[t + 1, r + 1].follow()

    pl.when(section >= mid)(take_inputs)
    for r in every:
        add(last, r, acc_grad, sum_grad, dot_nt(picks(last, r), grads[last, r]))
    place = pltpu.make_async_copy(edge.at[last, replica], out.at[:, replica], out_sem.at[0])
    place.start()
    fill(len(down_steps) + len(up_steps))
    for copy in gathered:
        copy.wait()
    keep = jnp.where(section < sections // 2, 0.0, 1.0).astype(f32)
    for k in range(2):
        for start, size in ((0, half), (half, own - half)):
            total = dot(inputs[k, pl.ds(start, size), :], sum_grad[...])
            proj_grad[k, pl.ds(start, size), :] = (total * keep if k else total).astype(bf16)
    place.wait()
    for pair in outs:
        for copy in pair:
            copy.wait_recv()
    all_sent(POOL, pool.at[pl.ds(0, replicas - 1)])
    all_sent(IDS, ids.at[pl.ds(0, replicas - 1)])
    others = pl.ds(0, (members - 1) * own)
    all_sent(SEED, upstream.at[0, :, others])
    all_sent(PART, upstream if square else part)
    all_sent(GRAD, upstream.at[:, :, pl.ds(0, 2 * own)] if square else part)
    all_sent(UP, upstream.at[pl.ds(0, last), :, others])
    all_sent(INPUTS, in_got.at[pl.ds(0, replicas - 1)])
    all_sent(OUT, edge.at[last, pl.ds(0, replicas - 1)])
    pl.when(section > 0)(lambda: all_sent(DOWN, edge_got.at[:, :, 0]))
    pl.when(section > mid)(lambda: all_sent(SKIP, edge_got.at[:, :, 1]))
    pl.when(is_top)(lambda: all_sent(LOSS, loss_t.at[pl.ds(0, replicas - 1)]))


def tail_kernel(*refs):
    pairs, sems = list(zip(refs[:4], refs[4:8])), refs[8]
    copies = [pltpu.make_async_copy(src, dst, sems.at[i]) for i, (src, dst) in enumerate(pairs)]
    for copy in copies:
        copy.start()
    for copy in copies:
        copy.wait()


def body(pool_inputs, pool_mixed, crop_ids, incoming, loss_grads, w_proj, w_up, w_down):
    sections = lax.axis_size("section")
    tensors, replicas = lax.axis_size("tensor"), lax.axis_size("replica")
    members = tensors * replicas
    own = w_proj.shape[2]
    own_p = -(-own // 16) * 16
    rows, width = incoming.shape[1], w_up.shape[1]
    width_p = members * own_p
    hidden = w_up.shape[2]
    ticks = crop_ids.shape[1]
    saved = pool_mixed.shape[1]

    def padded(x, axis):
        if own == own_p:
            return x
        count = x.shape[axis] // own
        shape = x.shape[:axis] + (count, own) + x.shape[axis + 1:]
        fill = [(0, 0)] * (x.ndim + 1)
        fill[axis + 1] = (0, own_p - own)
        shape_p = x.shape[:axis] + (count * own_p,) + x.shape[axis + 1:]
        return jnp.pad(x.reshape(shape), fill).reshape(shape_p)

    proj = padded(padded(w_proj[0], 1), 2)
    up, down = padded(w_up[0], 0), padded(w_down[0], 1)
    pool_own = padded(pool_mixed[0], 1)
    features = pool_inputs[0].transpose(1, 2, 0).reshape(2, replicas, own, saved)
    features = padded(features, 2)
    seed = padded(incoming[0].T, 0)
    loss = loss_grads.transpose(0, 2, 1).reshape(ticks - 1, replicas, own, rows)
    loss = padded(loss, 2)

    shape = jax.ShapeDtypeStruct
    vmem = pl.BlockSpec(memory_space=pltpu.VMEM)
    hbm = pl.BlockSpec(memory_space=pl.ANY)
    dma = pltpu.SemaphoreType.DMA
    square = tensors == 2 and replicas == 2 and own_p % 32 == 0
    flows = 10 if square else members - 1
    terms = 8 if square else members - 1
    scratch = [
        pltpu.VMEM(proj.shape, bf16), pltpu.VMEM(up.shape, bf16), pltpu.VMEM(down.shape, bf16),
        pltpu.VMEM(loss.shape, bf16), pltpu.VMEM((replicas,) + crop_ids.shape[1:], jnp.int32),
        pltpu.VMEM((replicas, ticks - 1, own_p, rows), bf16),
        pltpu.VMEM((replicas, saved, width_p), bf16), pltpu.VMEM((width_p, replicas * saved), bf16),
        pltpu.VMEM((hidden, replicas * saved), bf16),
        pltpu.VMEM((ticks, replicas, width_p, rows), bf16),
        pltpu.VMEM((ticks, replicas, width_p, rows), bf16),
        pltpu.VMEM((ticks, replicas, hidden, rows), bf16),
        pltpu.VMEM((ticks, replicas, 2 if square else members - 1, own_p, rows), bf16),
        pltpu.VMEM((ticks, replicas, 3, 2, 2, own_p // 2, rows) if square else (16, 128), bf16),
        pltpu.VMEM((16, 128) if square else (ticks, replicas, members - 1, own_p, rows), bf16),
        pltpu.VMEM((replicas, 2, 2, own_p // 2, rows) if square else (8, 128), f32),
        pltpu.VMEM((replicas, own_p, rows), f32),
        pltpu.VMEM((replicas, hidden, saved), bf16), pltpu.VMEM((replicas, hidden, saved), bf16),
        pltpu.VMEM((replicas, hidden, rows), f32),
        pltpu.VMEM((ticks, replicas, 2, own_p, rows), bf16),
        pltpu.VMEM((ticks - 1, replicas, 2, own_p, rows), bf16),
        pltpu.VMEM((replicas, saved, hidden), f32), pltpu.VMEM((replicas, saved, width_p), f32),
        pltpu.VMEM((replicas, saved, width_p), f32),
        pltpu.VMEM((replicas * saved, hidden), bf16), pltpu.VMEM((replicas * saved, width_p), bf16),
        pltpu.VMEM((replicas * saved, width_p), bf16),
        dma((8,)), dma((1 + replicas,)), dma((11,)), dma((max(4, replicas - 1),)), dma((4, replicas - 1)),
        dma((replicas - 1,)), dma((ticks - 1, replicas - 1)),
        dma((replicas, terms)), dma((replicas, 4 if square else flows)), dma((replicas, flows)),
        dma((ticks - 1, replicas, 2)), dma((replicas - 1, 4)),
        pltpu.VMEM(up.shape if square else (16, 128), bf16),
        pltpu.VMEM((2, own_p, replicas * saved), bf16),
    ]

    kept_shapes = ((hidden, width_p), (width_p, hidden), (2, own_p, width_p), (2, replicas, own_p, rows))
    vmem_limit = 66_800_000 - sum(2 * math.prod(dims) for dims in kept_shapes)
    _, *kept = pl.pallas_call(
        functools.partial(ticks_kernel, sections, tensors, replicas, own_p, ticks),
        out_shape=(
            shape((replicas, 2, own_p, saved), bf16),
            *(pltpu.VMEM(dims, bf16) for dims in kept_shapes),
        ),
        in_specs=[hbm] * 8,
        out_specs=(hbm,) + (vmem,) * 4,
        scratch_shapes=scratch,
        compiler_params=pltpu.CompilerParams(
            collective_id=0, has_side_effects=True, vmem_limit_bytes=vmem_limit
        ),
        name="ticks",
    )(features, pool_own, crop_ids[0], seed, loss, proj, up, down)

    def trimmed(x, axis):
        if own == own_p:
            return x
        count = x.shape[axis] // own_p
        x = x.reshape(x.shape[:axis] + (count, own_p) + x.shape[axis + 1:])
        x = lax.slice_in_dim(x, 0, own, axis=axis + 1)
        return x.reshape(x.shape[:axis] + (count * own,) + x.shape[axis + 2:])

    grad_down, grad_up, grad_proj, outgoing = pl.pallas_call(
        tail_kernel,
        out_shape=tuple(shape(dims, bf16) for dims in kept_shapes),
        in_specs=[vmem] * 4,
        out_specs=(hbm,) * 4,
        scratch_shapes=[dma((4,))],
        compiler_params=pltpu.CompilerParams(vmem_limit_bytes=128 * 1024),
        name="tail",
    )(*kept)
    grad_down = trimmed(grad_down, 1)[None]
    grad_up = trimmed(grad_up, 0)[None]
    grad_proj = trimmed(trimmed(grad_proj, 1), 2)[None]
    outgoing = trimmed(outgoing, 2).reshape(2, replicas * own, rows).transpose(2, 0, 1)
    return grad_proj, grad_up, grad_down, outgoing[None]


def solution(mesh):
    in_specs = (
        P("section", "replica", None, "tensor"),
        P("section", "replica", None),
        P("section", "replica", None),
        P("section", "replica", "tensor"),
        P(None, "replica", "tensor"),
        P("section", None, ("tensor", "replica"), None),
        P("section", None, ("tensor", "replica")),
        P("section", ("tensor", "replica"), None),
    )
    out_specs = (
        P("section", None, ("tensor", "replica"), None),
        P("section", None, ("tensor", "replica")),
        P("section", ("tensor", "replica"), None),
        P("section", "replica", None, "tensor"),
    )
    return jax.shard_map(body, mesh=mesh, in_specs=in_specs, out_specs=out_specs, check_vma=False)
```

```python
import functools
import math

import jax
import jax.numpy as jnp
from jax import lax
from jax.experimental import pallas as pl
from jax.experimental.pallas import tpu as pltpu
from jax.sharding import PartitionSpec as P

gelu_scale = 0.7978845608
gelu_cubic = 0.044715
bf16, f32 = jnp.bfloat16, jnp.float32
MESH = pl.DeviceIdType.MESH


def gelu_pair(pre_gelu):
    inner = gelu_scale * (pre_gelu + gelu_cubic * pre_gelu * pre_gelu * pre_gelu)
    tanh_part = jnp.tanh(inner)
    gelu_value = 0.5 * pre_gelu * (1.0 + tanh_part)
    gelu_slope = 0.5 * (1.0 + tanh_part) + 0.5 * pre_gelu * (
        1.0 - tanh_part * tanh_part
    ) * gelu_scale * (1.0 + 3.0 * gelu_cubic * pre_gelu * pre_gelu)
    return (gelu_value, gelu_slope)


def dot(a, b):
    return jnp.dot(a, b, preferred_element_type=f32)


def dot_nt(a, b):
    return lax.dot_general(a, b, (((1,), (1,)), ((), ())), preferred_element_type=f32)


def ticks_kernel(
    sections, tensors, replicas, own, ticks,
    inputs_hbm, pool_hbm, ids_hbm, seed_hbm, loss_hbm, proj_hbm, up_hbm, down_hbm,
    in_got, down_grad, up_grad, proj_grad, out,
    proj, up, down, loss_src, ids, loss_t, pool, pool_t, act_t,
    upstream, grads, hidden, part, relay, got, keep_part, own_part, slope_hi, slope_lo, slope,
    edge, edge_got, acc_hidden, acc_grad, acc_up, sum_hidden, sum_grad, sum_up,
    load_sem, out_sem, send_sems, pool_sems, inputs_sems, ids_sems, loss_sems,
    part_sems, grad_sems, up_sems, edge_sems, outgoing_sems, up_near, inputs,
):
    members = tensors * replicas
    square = tensors == 2 and replicas == 2 and own % 32 == 0
    half = own // 2
    section = lax.axis_index("section")
    tensor = lax.axis_index("tensor")
    replica = lax.axis_index("replica")
    me = tensor * replicas + replica
    hidden_rows = down.shape[0]
    saved = pool.shape[1]
    last = ticks - 1
    mid = sections // 2
    along = (1 - tensor) * replicas + replica
    across = tensor * replicas + (1 - replica)

    def device(s, member):
        return {
            "section": s,
            "tensor": lax.div(member, replicas),
            "replica": lax.rem(member, replicas),
        }

    def member_at(by):
        return lax.rem(me + by, members)

    def replica_at(by):
        return lax.rem(replica + by, replicas)

    def slab_of(member):
        return pl.ds(pl.multiple_of(member * own, 16), own)

    loads = []

    def load(src, dst):
        copy = pltpu.make_async_copy(src, dst, load_sem.at[len(loads)])
        copy.start()
        loads.append(copy)
        return copy

    near_order = {1: ((0, 0), (1, 0), (0, 1), (1, 1)), 0: ((0, 0), (0, 1), (1, 0), (1, 1))}

    def term(k, p, side):
        if k == 0:
            member = lax.rem(tensor + side, tensors) * replicas + p
        else:
            member = p * replicas + lax.rem(replica + side, replicas)
        return pl.ds(pl.multiple_of(member * own + k * half, 16), half)

    wide = pl.ds(pl.multiple_of(tensor * (replicas * own), 16), replicas * own)
    ld_pool = load(pool_hbm, pool.at[replica])
    ld_seed = load(seed_hbm, upstream.at[0, replica, wide])
    ld_ids = load(ids_hbm, ids.at[replica])
    ld_up = load(up_hbm, up)
    ld_down = load(down_hbm, down)
    if square:
        order = [term(k, p, side) for side in (1, 0) for k, p in near_order[side]]
        for i, rows in enumerate(order):
            pltpu.make_async_copy(up_hbm.at[rows], up_near.at[pl.ds(i * half, half)], out_sem.at[0]).start()
    ld_loss = load(loss_hbm, loss_src)
    ld_loss_own = load(loss_hbm.at[:, replica], loss_t.at[replica])
    ld_proj = load(proj_hbm, proj)

    barrier = pltpu.get_barrier_semaphore()
    above = lax.rem(section + 1, sections)
    below = lax.rem(section + sections - 1, sections)
    mirror = sections - 1 - section
    for by in range(1, members):
        pl.semaphore_signal(barrier, 1, device_id=device(section, member_at(by)), device_id_type=MESH)
    for other in (above, below, mirror):
        pl.semaphore_signal(barrier, 1, device_id=device(other, me), device_id_type=MESH)
    pl.semaphore_wait(barrier, members - 1 + 3)

    POOL, IDS, SEED, PART, GRAD, UP, INPUTS, DOWN, SKIP, LOSS, OUT = range(11)

    def remote(src, dst, kind, recv_sem, s, member):
        return pltpu.make_async_remote_copy(
            src_ref=src, dst_ref=dst, send_sem=send_sems.at[kind], recv_sem=recv_sem,
            device_id=device(s, member), device_id_type=MESH,
        )

    def send(src, dst, kind, recv_sem, member):
        copy = remote(src, dst, kind, recv_sem, section, member)
        copy.start()
        return copy

    def over_replicas(src_of, dst, kind, sems):
        return [
            send(src_of(replica_at(by)), dst, kind, sems.at[by - 1], tensor * replicas + replica_at(by))
            for by in range(1, replicas)
        ]

    def all_sent(kind, ref):
        pltpu.make_async_copy(ref, ref, send_sems.at[kind]).wait()

    def lanes(r):
        return inputs.at[:, :, pl.ds(pl.multiple_of(r * saved, 128), saved)]

    chunk = 128
    down_steps = [(start, min(chunk, hidden_rows - start)) for start in range(0, hidden_rows, chunk)]
    up_steps = [(start, min(chunk, up_grad.shape[0] - start)) for start in range(0, up_grad.shape[0], chunk)]

    def fill(count):
        for _ in range(count):
            if down_steps:
                start, size = down_steps.pop(0)
                down_grad[pl.ds(start, size), :] = dot(act_t[pl.ds(start, size), :], sum_up[...]).astype(bf16)
            elif up_steps:
                start, size = up_steps.pop(0)
                up_grad[pl.ds(start, size), :] = dot(pool_t[pl.ds(start, size), :], sum_hidden[...]).astype(bf16)

    class Gather:
        def __init__(self, at, whole, kind, sems):
            if square:
                flows = [(me, h, part, to) for part in range(2) for h, to in enumerate((along, across))]
                flows += [(me, 1, None, along), (me, 0, None, across)]
                flows += [(to, h, part, on) for part in range(2) for h, (to, on) in
                          enumerate(((along, across), (across, along)))]
                self.copies = [
                    remote(at(member, h, part), at(member, h, part), kind, sems.at[i], section, to)
                    for i, (member, h, part, to) in enumerate(flows)
                ]
            else:
                self.copies = [
                    remote(whole, whole, kind, sems.at[by - 1], section, member_at(by))
                    for by in range(1, members)
                ]

        def lead(self):
            for copy in self.copies[:4 if square else None]:
                copy.start()

        def follow(self):
            if square:
                self.copies[4].start()
                self.copies[5].start()

        def forward(self):
            if square:
                for i in range(4):
                    self.copies[i].wait_recv()
                    self.copies[6 + i].start()

        def finish(self):
            for copy in self.copies[4 if square else 0:]:
                copy.wait_recv()

    def part_rows(start, size, part):
        cut = -(-size // 32) * 16
        begin, count = {None: (0, size), 0: (0, cut), 1: (cut, size - cut)}[part]
        return pl.ds(pl.multiple_of(start + begin, 16), count)

    def halves_of(ref):
        return lambda member, h, part: ref.at[part_rows(member * own + h * half, half, part)]

    def seed_at(member, h, part):
        start = lax.div(member, replicas) * (replicas * own) + h * own
        return upstream.at[0, lax.rem(member, replicas), part_rows(start, own, part)]

    slab = slab_of(me)
    low, high = pl.ds(0, half), pl.ds(half, half)
    ld_pool.wait()
    pieces = 2
    if square:
        rows = saved // (2 * pieces)

        def piece(r, p):
            return pool.at[r, pl.ds(pl.multiple_of((tensor * pieces + p) * rows, 8), rows)]

        pool_in = [
            send(piece(replica, p), piece(replica, p), POOL, pool_sems.at[p], across)
            for p in range(pieces)
        ]
    else:
        pool_in = over_replicas(lambda r: pool.at[replica], pool.at[replica], POOL, pool_sems)
    ld_seed.wait()
    seed_in = Gather(seed_at, upstream.at[0, replica, wide], SEED, up_sems.at[0])
    seed_in.lead()
    seed_in.follow()
    ld_ids.wait()
    ids_in = over_replicas(lambda r: ids.at[replica], ids.at[replica], IDS, ids_sems)
    is_top = section == sections - 1

    step = next(n for n in (384, 256, 128) if hidden_rows % n == 0 or n == 128)

    def pre_slopes(r):
        def pre_at(start, size):
            cols = pl.ds(start, size)
            value, gelu_slope = gelu_pair(dot(pool[r], up[:, cols]).T)
            act_t[cols, pl.ds(pl.multiple_of(r * saved, 128), saved)] = value.astype(bf16)
            high = gelu_slope.astype(bf16)
            slope_hi[r, cols, :] = high
            slope_lo[r, cols, :] = (gelu_slope - high.astype(f32)).astype(bf16)

        @pl.loop(0, hidden_rows // step)
        def _(c):
            pre_at(pl.multiple_of(c * step, step), step)

        if hidden_rows % step:
            pre_at(hidden_rows - hidden_rows % step, hidden_rows % step)

    def picks(t, r):
        row = ids[r, pl.ds(t, 1), :]
        place_of = lax.broadcasted_iota(jnp.int32, (saved, row.shape[1]), 0)
        return jnp.where(place_of == row, 1.0, 0.0).astype(bf16)

    def pick_slope(t, r):
        chosen = picks(t, r)
        slope[r] = dot(slope_hi[r], chosen) + dot(slope_lo[r], chosen)

    ld_up.wait()
    pre_slopes(replica)
    pick_slope(0, replica)
    if square:
        pool_over = []
        for p in range(pieces):
            pool_in[p].wait_recv()
            come = piece(1 - replica, p)
            pool_over.append(send(come, come, POOL, pool_sems.at[pieces + p], along))
        seed_in.forward()
        for copy in pool_over:
            copy.wait_recv()
        pre_slopes(1 - replica)
    else:
        for by in range(1, replicas):
            pool_in[by - 1].wait_recv()
            pre_slopes(lax.rem(replica + replicas - by, replicas))
    for copy in ids_in:
        copy.wait_recv()
    for by in range(1, replicas):
        pick_slope(0, lax.rem(replica + by, replicas))

    ld_down.wait()
    if square:
        pltpu.make_async_copy(up_hbm, up_near, out_sem.at[0]).wait()
    seed_in.finish()

    up_in, part_in, grad_in, edge_in = {}, {}, {}, {}

    def stage_hidden(t, r):
        if t > 0:
            up_in[t, r].finish()
        hidden[t, r] = (dot(down[...], upstream[t, r]) * slope[r]).astype(bf16)
        if square:
            part[t, r, 0] = dot(up_near[:own, :], hidden[t, r]).astype(bf16)
            part_in[t, r] = put_terms(t, r, 0)

    def put_terms(t, r, p):
        return [
            send(part.at[t, r, p, rows], relay.at[t, r, 0, k, p], PART, part_sems.at[r, 2 * p + k], to)
            for k, (to, rows) in enumerate(((along, low), (across, high)))
        ]

    def stage_parts(t, r):
        if square:
            near_terms = dot(up_near[own:, :], hidden[t, r])
            part[t, r, 1] = near_terms[:own].astype(bf16)
            part_in[t, r] += put_terms(t, r, 1)
            for k in range(2):
                for p in range(2):
                    start = own + (2 * k + p) * half
                    keep_part[r, k, p] = near_terms[start:start + half]
            return
        part_in[t, r] = []
        for by in range(1, members):
            to = member_at(by)
            part[t, r, by - 1] = dot(up[slab_of(to), :], hidden[t, r]).astype(bf16)
            part_in[t, r].append(send(part.at[t, r, by - 1], got.at[t, r, by - 1], PART,
                                      part_sems.at[r, by - 1], to))
        own_part[r] = dot(up[slab, :], hidden[t, r]) + upstream[t, r, slab, :].astype(f32)

    def stage_relay(t, r):
        if square:
            for p in range(2):
                for k, to in enumerate((across, along)):
                    part_in[t, r][2 * p + k].wait_recv()
                    total = keep_part[r, k, p] + relay[t, r, 0, k, p].astype(f32)
                    relay[t, r, 1, k, p] = total.astype(bf16)
                    part_in[t, r].append(send(relay.at[t, r, 1, k, p], relay.at[t, r, 2, k, p], PART,
                                              part_sems.at[r, 4 + 2 * p + k], to))

    def stage_sum(t, r):
        if square:
            grad_in[t, r] = []
            for p in range(2):
                for k, to in enumerate((along, across)):
                    part_in[t, r][4 + 2 * p + k].wait_recv()
                    rows = term(k, p, 0)
                    total = relay[t, r, 1, k, p].astype(f32) + relay[t, r, 2, k, p].astype(f32)
                    grads[t, r, rows, :] = (total + upstream[t, r, rows, :].astype(f32)).astype(bf16)
                    mine = grads.at[t, r, rows]
                    grad_in[t, r].append(send(mine, mine, GRAD, grad_sems.at[r, 2 * p + k], to))
            return
        for copy in part_in[t, r]:
            copy.wait_recv()
        total = own_part[r]
        for k in range(got.shape[2]):
            total = total + got[t, r, k].astype(f32)
        grads[t, r, slab, :] = total.astype(bf16)
        gather = Gather(halves_of(grads.at[t, r]), grads.at[t, r, slab], GRAD, grad_sems.at[r])
        gather.lead()
        grad_in[t, r] = gather.copies

    def have_grads(t, r):
        for copy in grad_in[t, r]:
            copy.wait_recv()

    def stage_project(t, r):
        have_grads(t, r)
        down_copy, skip = edge_in[t, r]

        @pl.when(section > mid)
        def _():
            edge[t, r, 1] = dot(proj[1], grads[t, r]).astype(bf16)
            skip.start()

        edge[t, r, 0] = dot(proj[0], grads[t, r]).astype(bf16)
        pl.when((section > 0) & (section != mid))(down_copy.start)
        @pl.when(section == mid)
        def _():
            second = dot(proj[1], grads[t, r]).astype(bf16)
            edge[t, r, 0] = (edge[t, r, 0].astype(f32) + second.astype(f32)).astype(bf16)
            down_copy.start()


    def from_above(t, r):
        @pl.when((section >= mid - 1) & (section < sections - 1))
        def _():
            edge_in[t, r][0].wait_recv()
            upstream[t + 1, r, slab, :] = edge_got[t, r, 0]

        @pl.when(is_top)
        def _():
            if r == 0:
                for copy in loss_in[t]:
                    copy.wait_recv()
            upstream[t + 1, r, slab, :] = loss_t[r, t]

    def stage_next(t, r):
        @pl.when(section < mid - 1)
        def _():
            for copy in edge_in[t, r]:
                copy.wait_recv()
            summed = edge_got[t, r, 0].astype(f32) + edge_got[t, r, 1].astype(f32)
            upstream[t + 1, r, slab, :] = summed.astype(bf16)

        from_above(t, r)
        up_in[t + 1, r].lead()

    def add(t, r, acc, total, term):
        rows = pl.ds(r * saved, saved)
        value = term if t == 0 else acc[r] + term
        if t == last:
            total[rows, :] = value.astype(bf16)
        else:
            acc[r] = value

    def settle(t, r):
        chosen = picks(t, r)
        add(t, r, acc_hidden, sum_hidden, dot_nt(chosen, hidden[t, r]))
        add(t, r, acc_up, sum_up, dot_nt(chosen, upstream[t, r]))

    def give_loss(t):
        if t == 0:
            ld_loss.wait()
            ld_loss_own.wait()
        loss_in.append([
            remote(loss_src.at[t, replica_at(by)], loss_t.at[replica, t], LOSS,
                   loss_sems.at[t, by - 1], section, tensor * replicas + replica_at(by))
            for by in range(1, replicas)
        ])
        for copy in loss_in[t]:
            pl.when(is_top)(copy.start)

    def give_inputs(t):
        if t in (0, last):
            for copy in inputs_in:
                pl.when(section < mid if t == 0 else section >= mid)(copy.start)

    outs = [
        [
            remote(edge.at[last, replica_at(by), k, rows], out.at[k, replica, rows], OUT,
                   outgoing_sems.at[by - 1, 2 * k + h], section, tensor * replicas + replica_at(by))
            for k in range(2)
            for h, rows in enumerate((low, pl.ds(half, own - half)))
        ]
        for by in range(1, replicas)
    ]

    def stage_outgoing(r):
        have_grads(last, r)
        for k in range(2):
            for h, (start, size) in enumerate(((0, half), (half, own - half))):
                rows = pl.ds(start, size)
                edge[last, r, k, rows] = dot(proj[k, rows], grads[last, r]).astype(bf16)
                for by in range(1, replicas):
                    pl.when(replica_at(by) == r)(outs[by - 1][2 * k + h].start)

    def early(t):
        return section >= sections - 1 - t

    for t in range(last):
        for r in range(replicas):
            edge_in[t, r] = (
                remote(edge.at[t, r, 0], edge_got.at[t, r, 0], DOWN, edge_sems.at[t, r, 0], below, me),
                remote(edge.at[t, r, 1], edge_got.at[t, r, 1], SKIP, edge_sems.at[t, r, 1], mirror, me),
            )
            up_in[t + 1, r] = Gather(halves_of(upstream.at[t + 1, r]), upstream.at[t + 1, r, slab], UP, up_sems.at[r])

    every = range(replicas)
    end = replicas - 1
    loss_in = []
    inputs_in = [
        remote(inputs_hbm.at[k, replica_at(by), rows], in_got.at[replica, k, rows], INPUTS,
               inputs_sems.at[2 * k + h, by - 1], section, tensor * replicas + replica_at(by))
        for by in range(1, replicas)
        for k in range(2)
        for h, rows in enumerate((low, pl.ds(half, own - half)))
    ]
    gathered = [
        pltpu.make_async_copy(
            inputs_hbm.at[:, replica] if by == 0 else in_got.at[replica_at(by)], lanes(replica_at(by)), out_sem.at[1 + by]
        )
        for by in range(replicas)
    ]

    def take_inputs():
        for copy in inputs_in:
            copy.wait_recv()
        for copy in gathered:
            copy.start()

    for t in range(ticks):
        project = stage_project if t < last else lambda t, r: stage_outgoing(r)
        for r in every:
            stage_hidden(t, r)
            stage_parts(t, r)
        if t < last:
            give_loss(t)
        for r in every:
            stage_relay(t, r)
            if r == 0:
                settle(t, r)
            if t == last and r == 0:
                for other in range(1, replicas):
                    settle(t, other)
        for r in every:
            stage_sum(t, r)
            if r < end:
                fill(4) if t == last else settle(t, r + 1)
        if t < last:
            @pl.when(early(t))
            def _():
                for r in every:
                    from_above(t, r)
                    up_in[t + 1, r].lead()
                    up_in[t + 1, r].follow()

            for r in every:
                pick_slope(t + 1, r)
        else:
            fill(8)
        if t == 0:
            for r in every:
                pool_t[:, pl.ds(r * saved, saved)] = pool[r].T
            ld_proj.wait()
        give_inputs(t)
        if t == last:
            pl.when(section < mid)(take_inputs)
        for r in every:
            project(t, r)
        if t == last:
            break
        pl.when(early(t))(lambda: [up_in[t + 1, r].forward() for r in every] and None)

        @pl.when(jnp.logical_not(early(t)))
        def _():
            for r in every:
                stage_next(t, r)
                if r == 0:
                    up_in[t + 1, r].follow()

        for r in every:
            add(t, r, acc_grad, sum_grad, dot_nt(picks(t, r), grads[t, r]))

            @pl.when(jnp.logical_not(early(t)))
            def _():
                up_in[t + 1, r].forward()
                if r < end:
                    up_in[t + 1, r + 1].follow()

    pl.when(section >= mid)(take_inputs)
    for r in every:
        add(last, r, acc_grad, sum_grad, dot_nt(picks(last, r), grads[last, r]))
    place = pltpu.make_async_copy(edge.at[last, replica], out.at[:, replica], out_sem.at[0])
    place.start()
    fill(len(down_steps) + len(up_steps))
    for copy in gathered:
        copy.wait()
    keep = jnp.where(section < sections // 2, 0.0, 1.0).astype(f32)
    for k in range(2):
        for start, size in ((0, half), (half, own - half)):
            total = dot(inputs[k, pl.ds(start, size), :], sum_grad[...])
            proj_grad[k, pl.ds(start, size), :] = (total * keep if k else total).astype(bf16)
    place.wait()
    for pair in outs:
        for copy in pair:
            copy.wait_recv()
    all_sent(POOL, pool.at[pl.ds(0, replicas - 1)])
    all_sent(IDS, ids.at[pl.ds(0, replicas - 1)])
    others = pl.ds(0, (members - 1) * own)
    all_sent(SEED, upstream.at[0, :, others])
    all_sent(PART, upstream if square else part)
    all_sent(GRAD, upstream.at[:, :, pl.ds(0, 2 * own)] if square else part)
    all_sent(UP, upstream.at[pl.ds(0, last), :, others])
    all_sent(INPUTS, in_got.at[pl.ds(0, replicas - 1)])
    all_sent(OUT, edge.at[last, pl.ds(0, replicas - 1)])
    pl.when(section > 0)(lambda: all_sent(DOWN, edge_got.at[:, :, 0]))
    pl.when(section > mid)(lambda: all_sent(SKIP, edge_got.at[:, :, 1]))
    pl.when(is_top)(lambda: all_sent(LOSS, loss_t.at[pl.ds(0, replicas - 1)]))


def tail_kernel(*refs):
    pairs, sems = list(zip(refs[:4], refs[4:8])), refs[8]
    copies = [pltpu.make_async_copy(src, dst, sems.at[i]) for i, (src, dst) in enumerate(pairs)]
    for copy in copies:
        copy.start()
    for copy in copies:
        copy.wait()


def body(pool_inputs, pool_mixed, crop_ids, incoming, loss_grads, w_proj, w_up, w_down):
    sections = lax.axis_size("section")
    tensors, replicas = lax.axis_size("tensor"), lax.axis_size("replica")
    members = tensors * replicas
    own = w_proj.shape[2]
    own_p = -(-own // 16) * 16
    rows, width = incoming.shape[1], w_up.shape[1]
    width_p = members * own_p
    hidden = w_up.shape[2]
    ticks = crop_ids.shape[1]
    saved = pool_mixed.shape[1]

    def padded(x, axis):
        if own == own_p:
            return x
        count = x.shape[axis] // own
        shape = x.shape[:axis] + (count, own) + x.shape[axis + 1:]
        fill = [(0, 0)] * (x.ndim + 1)
        fill[axis + 1] = (0, own_p - own)
        shape_p = x.shape[:axis] + (count * own_p,) + x.shape[axis + 1:]
        return jnp.pad(x.reshape(shape), fill).reshape(shape_p)

    proj = padded(padded(w_proj[0], 1), 2)
    up, down = padded(w_up[0], 0), padded(w_down[0], 1)
    pool_own = padded(pool_mixed[0], 1)
    features = pool_inputs[0].transpose(1, 2, 0).reshape(2, replicas, own, saved)
    features = padded(features, 2)
    seed = padded(incoming[0].T, 0)
    loss = loss_grads.transpose(0, 2, 1).reshape(ticks - 1, replicas, own, rows)
    loss = padded(loss, 2)

    shape = jax.ShapeDtypeStruct
    vmem = pl.BlockSpec(memory_space=pltpu.VMEM)
    hbm = pl.BlockSpec(memory_space=pl.ANY)
    dma = pltpu.SemaphoreType.DMA
    square = tensors == 2 and replicas == 2 and own_p % 32 == 0
    flows = 10 if square else members - 1
    terms = 8 if square else members - 1
    scratch = [
        pltpu.VMEM(proj.shape, bf16), pltpu.VMEM(up.shape, bf16), pltpu.VMEM(down.shape, bf16),
        pltpu.VMEM(loss.shape, bf16), pltpu.VMEM((replicas,) + crop_ids.shape[1:], jnp.int32),
        pltpu.VMEM((replicas, ticks - 1, own_p, rows), bf16),
        pltpu.VMEM((replicas, saved, width_p), bf16), pltpu.VMEM((width_p, replicas * saved), bf16),
        pltpu.VMEM((hidden, replicas * saved), bf16),
        pltpu.VMEM((ticks, replicas, width_p, rows), bf16),
        pltpu.VMEM((ticks, replicas, width_p, rows), bf16),
        pltpu.VMEM((ticks, replicas, hidden, rows), bf16),
        pltpu.VMEM((ticks, replicas, 2 if square else members - 1, own_p, rows), bf16),
        pltpu.VMEM((ticks, replicas, 3, 2, 2, own_p // 2, rows) if square else (16, 128), bf16),
        pltpu.VMEM((16, 128) if square else (ticks, replicas, members - 1, own_p, rows), bf16),
        pltpu.VMEM((replicas, 2, 2, own_p // 2, rows) if square else (8, 128), f32),
        pltpu.VMEM((replicas, own_p, rows), f32),
        pltpu.VMEM((replicas, hidden, saved), bf16), pltpu.VMEM((replicas, hidden, saved), bf16),
        pltpu.VMEM((replicas, hidden, rows), f32),
        pltpu.VMEM((ticks, replicas, 2, own_p, rows), bf16),
        pltpu.VMEM((ticks - 1, replicas, 2, own_p, rows), bf16),
        pltpu.VMEM((replicas, saved, hidden), f32), pltpu.VMEM((replicas, saved, width_p), f32),
        pltpu.VMEM((replicas, saved, width_p), f32),
        pltpu.VMEM((replicas * saved, hidden), bf16), pltpu.VMEM((replicas * saved, width_p), bf16),
        pltpu.VMEM((replicas * saved, width_p), bf16),
        dma((8,)), dma((1 + replicas,)), dma((11,)), dma((max(4, replicas - 1),)), dma((4, replicas - 1)),
        dma((replicas - 1,)), dma((ticks - 1, replicas - 1)),
        dma((replicas, terms)), dma((replicas, 4 if square else flows)), dma((replicas, flows)),
        dma((ticks - 1, replicas, 2)), dma((replicas - 1, 4)),
        pltpu.VMEM(up.shape if square else (16, 128), bf16),
        pltpu.VMEM((2, own_p, replicas * saved), bf16),
    ]

    kept_shapes = ((hidden, width_p), (width_p, hidden), (2, own_p, width_p), (2, replicas, own_p, rows))
    vmem_limit = 66_800_000 - sum(2 * math.prod(dims) for dims in kept_shapes)
    _, *kept = pl.pallas_call(
        functools.partial(ticks_kernel, sections, tensors, replicas, own_p, ticks),
        out_shape=(
            shape((replicas, 2, own_p, saved), bf16),
            *(pltpu.VMEM(dims, bf16) for dims in kept_shapes),
        ),
        in_specs=[hbm] * 8,
        out_specs=(hbm,) + (vmem,) * 4,
        scratch_shapes=scratch,
        compiler_params=pltpu.CompilerParams(
            collective_id=0, has_side_effects=True, vmem_limit_bytes=vmem_limit
        ),
        name="ticks",
    )(features, pool_own, crop_ids[0], seed, loss, proj, up, down)

    def trimmed(x, axis):
        if own == own_p:
            return x
        count = x.shape[axis] // own_p
        x = x.reshape(x.shape[:axis] + (count, own_p) + x.shape[axis + 1:])
        x = lax.slice_in_dim(x, 0, own, axis=axis + 1)
        return x.reshape(x.shape[:axis] + (count * own,) + x.shape[axis + 2:])

    grad_down, grad_up, grad_proj, outgoing = pl.pallas_call(
        tail_kernel,
        out_shape=tuple(shape(dims, bf16) for dims in kept_shapes),
        in_specs=[vmem] * 4,
        out_specs=(hbm,) * 4,
        scratch_shapes=[dma((4,))],
        compiler_params=pltpu.CompilerParams(vmem_limit_bytes=128 * 1024),
        name="tail",
    )(*kept)
    grad_down = trimmed(grad_down, 1)[None]
    grad_up = trimmed(grad_up, 0)[None]
    grad_proj = trimmed(trimmed(grad_proj, 1), 2)[None]
    outgoing = trimmed(outgoing, 2).reshape(2, replicas * own, rows).transpose(2, 0, 1)
    return grad_proj, grad_up, grad_down, outgoing[None]


def solution(mesh):
    in_specs = (
        P("section", "replica", None, "tensor"),
        P("section", "replica", None),
        P("section", "replica", None),
        P("section", "replica", "tensor"),
        P(None, "replica", "tensor"),
        P("section", None, ("tensor", "replica"), None),
        P("section", None, ("tensor", "replica")),
        P("section", ("tensor", "replica"), None),
    )
    out_specs = (
        P("section", None, ("tensor", "replica"), None),
        P("section", None, ("tensor", "replica")),
        P("section", ("tensor", "replica"), None),
        P("section", "replica", None, "tensor"),
    )
    return jax.shard_map(body, mesh=mesh, in_specs=in_specs, out_specs=out_specs, check_vma=False)
```
